128 devices in a mesh: expert: 32 (over z, x, core), tensor: 4 (over y).
Axes of the slice: x: 4, y: 4, z: 4, core: 2. Of those that a mesh axis runs over, the one named last changes fastest.
Arguments:
- tokens: bfloat16 [16384, 2560], P(('expert', 'tensor')), may hold values from -6 to 6
- expert_ids: int32 [16384, 1], P(('expert', 'tensor')), may hold values from 0 to 31; in each aligned block of 128 rows (0 to 127, 128 to 255, ...) at most 6 rows name the same one
- live_counts: int32 [128], P(('expert', 'tensor')), may hold values from 1 to 128, 10240 in all
- router: bfloat16 [2560, 32], replicated, may hold values from -0.125 to 0.125
- up_weight: bfloat16 [32, 2560, 4096], P('expert', None, 'tensor'), may hold values from -0.125 to 0.125
- down_weight: bfloat16 [32, 4096, 2560], P('expert', 'tensor'), may hold values from -0.09375 to 0.09375
- out_grad: bfloat16 [16384, 2560], P(('expert', 'tensor')), may hold values from -6 to 6
Outputs:
- mixed: bfloat16 [16384, 2560], P(('expert', 'tensor'))
- token_grad: bfloat16 [16384, 2560], P(('expert', 'tensor'))
- up_grad: bfloat16 [32, 2560, 4096], P('expert', None, 'tensor')
- down_grad: bfloat16 [32, 4096, 2560], P('expert', 'tensor')
- router_grad: float32 [2560, 32], replicated
The draws below stay inside these ranges and needn't reach their ends.
Inputs may be any that keep to these rules, and one draw needn't show every extreme that they name: `expert_ids`: within the rows of one device (aligned blocks of 128 rows) no expert is named by more than 6 rows; in every draw some expert is named by exactly 6 rows of some device. live_counts[k] real token rows lead device k's 128 rows, the rest are padding; some device holds exactly 128 real rows in every draw.
All inputs are finite; a program needn't handle non-finite values.
Results may differ from the reference program's by a relative error of at most 0.0063.
Values may be sent and summed in bfloat16 or wider, within the bound.
A program may use at most 128 MiB of HBM per device.

```python
import math
import jax
import jax.numpy as jnp
import numpy as np
from jax import lax

D = 2560
FFW = 4096
TOK_DEV = 128
EXPERTS = 32
MOST = 6
TOKENS = 16384
N_EXPERT = 32
N_TENSOR = 4


def levels(own_key, shape, split, least, largest):
    gain, own = 1.0, jax.random.fold_in(own_key, 6)
    for dim, shards_of in split:
        heights = jnp.exp(jax.random.uniform(jax.random.fold_in(own, dim), (shards_of,), jnp.float32, least / len(split), largest / len(split)))
        gain = gain * jnp.repeat(heights, shape[dim] // shards_of).reshape([-1 if axis == dim else 1 for axis in range(len(shape))])
    return gain


def length_profile(amount, total, limit, lean):
    weights = [(1 << 20) // math.isqrt(grade ** lean) + 1 for grade in range(2, amount + 1)]
    spare, given = total - limit - (amount - 1), [1] * (amount - 1)
    while spare > 0:
        candidates = [i for i in range(amount - 1) if given[i] < limit]
        whole, budget = sum([weights[i] for i in candidates]), spare
        for i in candidates:
            addition = min(limit - given[i], max(1, budget * weights[i] // whole), spare)
            given[i] = given[i] + addition
            spare = spare - addition
    return np.array([limit] + given)


def uneven(key, count, total, reach, lean):
    if count == 2:
        one = jax.random.randint(key, (), max(1, total - reach), min(reach, total - 1) + 1)
        return jnp.stack([one, total - one])
    sizes = jnp.asarray(length_profile(count, total, reach, lean), jnp.int32)
    pairs = (count - 1) // 2
    source_of, receiver = sizes[1:1 + 2 * pairs:2], sizes[2:2 + 2 * pairs:2]
    slack = jnp.minimum(source_of - 1, reach - receiver)
    moved = jax.random.randint(jax.random.fold_in(key, 1), (pairs,), 0, 1 << 20) % (slack + 1)
    sizes = sizes.at[1:1 + 2 * pairs:2].set(source_of - moved).at[2:2 + 2 * pairs:2].set(receiver + moved)
    return sizes[jax.random.permutation(jax.random.fold_in(key, 2), count)]


def routed_block(stream_key, own, number, rows, number_of, top, limit, lean):
    order = jax.random.permutation(stream_key, number_of)
    packed, ordinary = load_shares(number_of, rows * top, limit, lean, True), load_shares(number_of, rows * top, limit, lean, False)
    places = jnp.arange(number_of)

    def named(sizes, rotation):
        used = int((sizes > 0).sum())
        fixed = max(1, used // 4)
        passed = fixed + (places - fixed + rotation * (used - fixed)) % max(1, number_of - fixed)
        return jnp.zeros((number_of,), jnp.int32).at[order[jnp.where(places < fixed, places, passed)]].set(jnp.asarray(sizes, jnp.int32))

    sizes = jnp.where(number % 4 == 0, named(packed, number // 4), named(ordinary, number - number // 4 - 1))
    mixed = jax.random.permutation(jax.random.fold_in(own, 3), number_of)
    giver, receiver = mixed[0:number_of // 2 * 2:2], mixed[1:number_of // 2 * 2:2]
    room = jnp.minimum(sizes[giver] - 1, limit - sizes[receiver]) // 2
    room = jnp.where((giver == order[0]) | (receiver == order[0]) | (sizes[receiver] == 0), 0, jnp.maximum(room, 0))
    passed = jax.random.randint(jax.random.fold_in(own, 4), (number_of // 2,), 0, 1 << 20) % (room + 1)
    sizes = sizes.at[giver].add(-passed).at[receiver].add(passed)
    members = jnp.searchsorted(jnp.cumsum(sizes), jnp.arange(rows * top), side="right").astype(jnp.int32)
    table = members.reshape(top, rows).T
    table = table[jax.random.permutation(jax.random.fold_in(own, 1), rows)]
    rotation = jax.random.randint(jax.random.fold_in(own, 2), (rows, 1), 0, top)
    return jnp.take_along_axis(table, (jnp.arange(top)[None, :] + rotation) % top, axis=1)


def load_shares(count, total, bound, lean, full):
    loads = [(1 << 20) // math.isqrt(rank ** lean) + 1 for rank in range(1, count + 1)]
    largest = bound if full else min(bound, max(-(-total // count), total * loads[0] // sum(loads)))
    least = 1 if total - largest >= count - 1 else 0
    counts, rest = [largest] + [least] * (count - 1), total - largest - least * (count - 1)
    while rest > 0:
        movable = [i for i in range(1, count) if counts[i] < largest] or [i for i in range(1, count) if counts[i] < bound]
        pool, left = sum([loads[i] for i in movable]), rest
        for i in movable:
            addition = min(bound - counts[i], max(1, left * loads[i] // pool), rest)
            counts[i] = counts[i] + addition
            rest = rest - addition
    return np.array(counts)


def scatter_about(own_key, dims, deviation, reach, shards=(), kind=jnp.bfloat16):
    array = deviation * jax.random.normal(own_key, dims, jnp.float32)
    if shards:
        array = array * levels(own_key, dims, shards, -0.22, 0.18)
    return jnp.clip(array, -reach, reach).astype(kind)


def setup_inputs(seed: int = 0) -> dict:
    splits = jax.random.split(jax.random.key(seed), 8)
    tokens = scatter_about(splits[0], (TOKENS, D), 1.0, 6.0, ((0, 128),))
    expert_ids_keys = jax.random.split(jax.random.fold_in(splits[1], 1), TOKENS // TOK_DEV)
    expert_ids_turns = jax.random.permutation(jax.random.fold_in(splits[1], 3), TOKENS // TOK_DEV)
    expert_ids = jax.vmap(lambda own, number: routed_block(jax.random.fold_in(splits[1], 2), own, number, TOK_DEV, EXPERTS, 1, MOST, 2))(expert_ids_keys, expert_ids_turns).reshape((TOKENS, 1))
    live_counts = uneven(splits[2], N_EXPERT * N_TENSOR, N_EXPERT * N_TENSOR * TOK_DEV * 5 // 8, TOK_DEV, 2).astype(jnp.int32)
    router = scatter_about(splits[3], (D, EXPERTS), D ** -0.5, 0.125)
    up_weight = scatter_about(splits[4], (EXPERTS, D, FFW), D ** -0.5, 0.125, ((0, 32), (2, 4)))
    down_weight = scatter_about(splits[5], (EXPERTS, FFW, D), FFW ** -0.5, 0.09375, ((0, 32), (1, 4)))
    out_grad = scatter_about(splits[6], (TOKENS, D), 1.0, 6.0, ((0, 128),))
    return {"tokens": tokens, "expert_ids": expert_ids, "live_counts": live_counts, "router": router, "up_weight": up_weight, "down_weight": down_weight, "out_grad": out_grad}


def silu_slope(hidden):
    sig = jax.nn.sigmoid(hidden)
    return sig * (1.0 + hidden * (1.0 - sig))


def reference(tokens, expert_ids, live_counts, router, up_weight, down_weight, out_grad):
    total = tokens.shape[0]
    width = tokens.shape[1]
    per_dev = total // live_counts.shape[0]
    row_ids = jnp.arange(total, dtype=jnp.int32)
    owner = row_ids // per_dev
    live = (row_ids - owner * per_dev) < live_counts[owner]
    live_rows = jnp.where(live[:, None], tokens, jnp.zeros_like(tokens))
    ids = expert_ids[:, 0]
    logits = jnp.dot(tokens, router, preferred_element_type=jnp.float32)
    onehot = (ids[:, None] == jnp.arange(EXPERTS, dtype=jnp.int32)[None, :]).astype(jnp.float32)
    gate = jax.nn.sigmoid(jnp.sum(logits * onehot, axis=1))
    out_cot = jnp.where(live[:, None], gate[:, None] * out_grad.astype(jnp.float32), 0.0).astype(jnp.bfloat16)
    pad_b = jnp.zeros((1, width), jnp.bfloat16)
    x_pad = jnp.concatenate([live_rows, pad_b], axis=0)
    cot_pad = jnp.concatenate([out_cot, pad_b], axis=0)
    dy_pad = jnp.concatenate([out_grad, pad_b], axis=0)
    gate_pad = jnp.concatenate([gate, jnp.zeros((1,), jnp.float32)], axis=0)
    capacity = N_EXPERT * N_TENSOR * MOST

    def one_expert(index):
        picks = jnp.nonzero(ids == index, size=capacity, fill_value=total)[0].astype(jnp.int32)
        x_e = x_pad[picks]
        cot_e = cot_pad[picks]
        dy_e = dy_pad[picks]
        gate_e = gate_pad[picks]
        w_up = up_weight[index]
        w_down = down_weight[index]
        hidden = jnp.dot(x_e, w_up, preferred_element_type=jnp.float32)
        active = jax.nn.silu(hidden).astype(jnp.bfloat16)
        expert_out = jnp.dot(active, w_down, preferred_element_type=jnp.float32).astype(jnp.bfloat16)
        mixed_e = (gate_e[:, None] * expert_out.astype(jnp.float32)).astype(jnp.bfloat16)
        slope = jnp.sum(dy_e.astype(jnp.float32) * expert_out.astype(jnp.float32), axis=1) * gate_e * (1.0 - gate_e)
        hidden_cot = (jnp.dot(cot_e, w_down.T, preferred_element_type=jnp.float32) * silu_slope(hidden)).astype(jnp.bfloat16)
        down_g = jnp.dot(active.T, cot_e, preferred_element_type=jnp.float32).astype(jnp.bfloat16)
        up_g = jnp.dot(x_e.T, hidden_cot, preferred_element_type=jnp.float32).astype(jnp.bfloat16)
        expert_cot = jnp.dot(hidden_cot, w_up.T, preferred_element_type=jnp.float32).astype(jnp.bfloat16)
        column = router[:, index].astype(jnp.float32)
        grad_e = (expert_cot.astype(jnp.float32) + slope[:, None] * column[None, :]).astype(jnp.bfloat16)
        router_e = jnp.dot(x_e.astype(jnp.float32).T, slope, precision=lax.Precision.HIGHEST)
        return picks, mixed_e, grad_e, up_g, down_g, router_e

    picks, mixed_all, grad_all, up_grad, down_grad, router_cols = lax.map(one_expert, jnp.arange(EXPERTS, dtype=jnp.int32))
    flat = picks.reshape(-1)
    mixed = jnp.zeros((total + 1, width), jnp.bfloat16).at[flat].set(mixed_all.reshape(-1, width))[:total]
    token_grad = jnp.zeros((total + 1, width), jnp.bfloat16).at[flat].set(grad_all.reshape(-1, width))[:total]
    return mixed, token_grad, up_grad, down_grad, router_cols.T
```

```python
import jax
import jax.numpy as jnp
from jax import lax
from jax.sharding import PartitionSpec as P

F32, BF16 = jnp.float32, jnp.bfloat16


def per_device(tokens, expert_ids, live_counts, router, up_weight, down_weight, out_grad):
    tok_rows, width = tokens.shape
    experts = router.shape[1]
    most = 3 * tok_rows // (2 * experts)
    slots = experts * most
    ids = expert_ids[:, 0]
    live = lax.iota(jnp.int32, tok_rows) < live_counts[0]
    chosen = ids[:, None] == lax.iota(jnp.int32, experts)[None, :]
    logits = jnp.dot(tokens, router, preferred_element_type=F32)
    gate = jax.nn.sigmoid(jnp.sum(jnp.where(chosen, logits, 0.0), axis=1))
    before = (lax.iota(jnp.int32, tok_rows)[:, None] > lax.iota(jnp.int32, tok_rows)[None, :])
    same = ids[:, None] == ids[None, :]
    rank = jnp.sum(jnp.where(before & same, 1, 0), axis=1)
    target = jnp.where(live, ids * most + rank, -1)
    placing = (lax.iota(jnp.int32, slots)[:, None] == target[None, :]).astype(BF16)
    w_up = up_weight[0]
    w_down = down_weight[0]
    out_cot = (gate[:, None] * out_grad.astype(F32)).astype(BF16)
    both = jnp.concatenate([tokens, out_cot], axis=1)
    box = jnp.dot(placing, both, preferred_element_type=F32).astype(BF16)
    inbox = lax.all_to_all(
        box.reshape(experts, most, 2 * width), "expert", split_axis=0, concat_axis=0, tiled=True
    ).reshape(slots, 2 * width)
    rows_all = lax.all_gather(inbox, "tensor", axis=0, tiled=True)
    rows, cot = rows_all[:, :width], rows_all[:, width:]
    me = lax.axis_index("expert")
    column = lax.dynamic_index_in_dim(router, me, axis=1, keepdims=False)
    slot_logit = jnp.dot(rows, router, preferred_element_type=F32)
    slot_gate = jax.nn.sigmoid(lax.dynamic_index_in_dim(slot_logit, me, axis=1, keepdims=False))
    hidden = jnp.dot(rows, w_up, preferred_element_type=F32)
    sig = jax.nn.sigmoid(hidden)
    active = (hidden * sig).astype(BF16)
    back = lax.dot_general(cot, w_down, (((1,), (1,)), ((), ())), preferred_element_type=F32)
    hidden_cot = (back * (sig * (1.0 + hidden * (1.0 - sig)))).astype(BF16)
    slope = jnp.sum(active.astype(F32) * back, axis=1) * (1.0 - slot_gate)
    tn = (((0,), (0,)), ((), ()))
    down_grad = lax.dot_general(active, cot, tn, preferred_element_type=F32).astype(BF16)[None]
    up_grad = lax.dot_general(rows, hidden_cot, tn, preferred_element_type=F32).astype(BF16)[None]
    value = jnp.dot(active, w_down, preferred_element_type=F32).astype(BF16)
    grad = (
        lax.dot_general(hidden_cot, w_up, (((1,), (1,)), ((), ())), preferred_element_type=F32)
        + slope[:, None] * column.astype(F32)[None, :]
    ).astype(BF16)
    router_col = jnp.sum(rows.astype(F32) * slope[:, None], axis=0)
    router_col = lax.psum(router_col, "tensor")
    router_grad = lax.all_gather(router_col, "expert", axis=0).T
    summed = lax.psum_scatter(
        jnp.concatenate([value, grad], axis=1), "tensor", scatter_dimension=0, tiled=True
    )
    back_box = lax.all_to_all(
        summed.reshape(experts, most, 2 * width), "expert", split_axis=0, concat_axis=0, tiled=True
    ).reshape(slots, 2 * width)
    out = lax.dot_general(placing, back_box, tn, preferred_element_type=F32)
    mixed = (gate[:, None] * out[:, :width]).astype(BF16)
    token_grad = out[:, width:].astype(BF16)
    return (mixed, token_grad, up_grad, down_grad, router_grad)


def solution(mesh):
    rows = P(("expert", "tensor"), None)
    in_specs = (
        rows,
        rows,
        P(("expert", "tensor")),
        P(),
        P("expert", None, "tensor"),
        P("expert", "tensor", None),
        rows,
    )
    out_specs = (rows, rows, P("expert", None, "tensor"), P("expert", "tensor", None), P())
    return jax.shard_map(
        per_device, mesh=mesh, in_specs=in_specs, out_specs=out_specs, check_vma=False
    )
```

```python
import jax
import jax.numpy as jnp
from jax import lax
from jax.experimental import pallas as pl
from jax.experimental.pallas import tpu as pltpu
from jax.sharding import PartitionSpec as P

F32, BF16, I32 = jnp.float32, jnp.bfloat16, jnp.int32
MESH = pl.DeviceIdType.MESH

NZ, NQ, NT = 4, 8, 4
EXPERTS = NZ * NQ
ROWS, MOST = 128, 6
SLOTS = EXPERTS * MOST
BOTH = 2 * SLOTS
C, NC = 512, 5
H = 1024
N = 256


def dot(a, b, dims=((1,), (0,))):
    return lax.dot_general(a, b, (dims, ((), ())), preferred_element_type=F32)


NTD = ((1,), (1,))
TND = ((0,), (0,))


def iota(shape, axis):
    return lax.broadcasted_iota(I32, shape, axis).astype(F32)


def onehot(mask):
    return jnp.where(mask, 1.0, 0.0).astype(BF16)


def div(a, b):
    return jnp.floor((a + 0.5) * (1.0 / b))


def source_1(o):
    q = div(o, 2 * NZ * MOST)
    r = o - q * (2 * NZ * MOST)
    a = div(r, NZ * MOST)
    r = r - a * (NZ * MOST)
    z = div(r, MOST)
    k = r - z * MOST
    return z * (NQ * 2 * MOST) + q * (2 * MOST) + a * MOST + k


def source_2(o):
    a = div(o, SLOTS)
    r = o - a * SLOTS
    q = div(r, NZ * MOST)
    m = r - q * (NZ * MOST)
    return q * (2 * NZ * MOST) + a * (NZ * MOST) + m


def kernel(
    ids_ref, live_ref, router_ref, tok_ref, og_ref, up_hbm, down_hbm,
    mixed_ref, tgrad_ref, upg_hbm, downg_hbm, rgrad_ref,
    box, inz, outx, inx, yb, wu, wd, hid, dh, act, hc, lg, gate_s, slope_s, slope3,
    sa, ra, sb, rb, rx, rz, gsu, gsd, p1, p1t, p2, p2t, plc, pltx, pltc, rrow,
    vy, vx, vz,
    wsem, zs, zr, xs, xr, ys, yr, as_, ar, bs, br, xs2, xr2, zs2, zr2, gsem,
    vys, vyr, vxs, vxr, vzs, vzr,
):
    me = lax.axis_index("expert")
    t = lax.axis_index("tensor")
    z, q = me // NQ, me % NQ

    def zpeer(d):
        return (((z + d) % NZ) * NQ + q, t)

    def xpeer(d):
        return (z * NQ + (q + d) % NQ, t)

    def ypeer(d):
        return (me, (t + d) % NT)

    def remote(src, dst, ssem, rsem, peer):
        return pltpu.make_async_remote_copy(
            src_ref=src, dst_ref=dst, send_sem=ssem, recv_sem=rsem,
            device_id=peer, device_id_type=MESH,
        )

    def weights(s):
        cols = pl.ds(pl.multiple_of(s * C, C), C)
        return (
            pltpu.make_async_copy(up_hbm.at[0, cols, :], wu.at[s], wsem.at[0, s]),
            pltpu.make_async_copy(down_hbm.at[0, :, cols], wd.at[s], wsem.at[1, s]),
        )

    def zcopy(s, d):
        return remote(box.at[s, (z + d) % NZ], inz.at[s, z], zs.at[s, d], zr.at[s, d], zpeer(d))

    def zland(s, d):
        return remote(box.at[s, z], inz.at[s, (z + NZ - d) % NZ], zs.at[s, d], zr.at[s, d], zpeer(d))

    def xcopy(s, d):
        return remote(outx.at[s, (q + d) % NQ], inx.at[s, q], xs.at[s, d], xr.at[s, d], xpeer(d))

    def xland(s, d):
        return remote(outx.at[s, q], inx.at[s, (q + NQ - d) % NQ], xs.at[s, d], xr.at[s, d], xpeer(d))

    left, right = (t + NT - 1) % NT, (t + 1) % NT
    far = (t + 2) % NT
    lo, hi = pl.ds(0, SLOTS), pl.ds(SLOTS, SLOTS)

    def ycopy(s, i):
        if i == 0:
            src, peer = yb.at[s, t], ypeer(1)
        elif i == 1:
            src, peer = yb.at[s, t], ypeer(NT - 1)
        elif i == 2:
            src, peer = yb.at[s, left, lo], ypeer(1)
        else:
            src, peer = yb.at[s, right, hi], ypeer(NT - 1)
        return remote(src, src, ys.at[s, i], yr.at[s, i], peer)

    def yland(s, i):
        dst = (yb.at[s, left], yb.at[s, right], yb.at[s, far, lo], yb.at[s, far, hi])[i]
        return remote(dst, dst, ys.at[s, i], yr.at[s, i], ypeer(1))

    def acopy(s, i):
        return remote(sa.at[s, i], ra.at[s, i], as_.at[s, i], ar.at[s, i], ypeer((1, NT - 1)[i]))

    def bcopy(s, i):
        return remote(sb.at[s, i], rb.at[s, i], bs.at[s, i], br.at[s, i], ypeer((1, NT - 1)[i]))

    def x2copy(s, d):
        return remote(outx.at[s, (q + d) % NQ], rx.at[s, q], xs2.at[s, d], xr2.at[s, d], xpeer(d))

    def x2land(s, d):
        return remote(outx.at[s, q], rx.at[s, (q + NQ - d) % NQ], xs2.at[s, d], xr2.at[s, d], xpeer(d))

    def z2copy(s, d):
        return remote(box.at[s, (z + d) % NZ], rz.at[s, z], zs2.at[s, d], zr2.at[s, d], zpeer(d))

    def z2land(s, d):
        return remote(box.at[s, z], rz.at[s, (z + NZ - d) % NZ], zs2.at[s, d], zr2.at[s, d], zpeer(d))

    def vycopy(d):
        return remote(vy.at[t], vy.at[t], vys.at[d], vyr.at[d], ypeer(d))

    def vyland(d):
        dst = vy.at[(t + NT - d) % NT]
        return remote(dst, dst, vys.at[d], vyr.at[d], ypeer(d))

    def vxcopy(d):
        return remote(vx.at[q], vx.at[q], vxs.at[d], vxr.at[d], xpeer(d))

    def vxland(d):
        dst = vx.at[(q + NQ - d) % NQ]
        return remote(dst, dst, vxs.at[d], vxr.at[d], xpeer(d))

    def vzcopy(d):
        return remote(vx, vz.at[z], vzs.at[d], vzr.at[d], zpeer(d))

    def vzland(d):
        return remote(vx, vz.at[(z + NZ - d) % NZ], vzs.at[d], vzr.at[d], zpeer(d))

    for s in range(NC):
        for copy in weights(s):
            copy.start()

    barrier = pltpu.get_barrier_semaphore()
    for d in range(1, NZ):
        pl.semaphore_signal(barrier, inc=1, device_id=zpeer(d), device_id_type=MESH)
    for d in range(1, NQ):
        pl.semaphore_signal(barrier, inc=1, device_id=xpeer(d), device_id_type=MESH)
    for d in range(1, NT):
        pl.semaphore_signal(barrier, inc=1, device_id=ypeer(d), device_id_type=MESH)

    ids = ids_ref[...].astype(F32)
    chosen = ids == iota((ROWS, EXPERTS), 1)
    tri = onehot(iota((ROWS, ROWS), 0) > iota((ROWS, ROWS), 1))
    counts = dot(tri, onehot(chosen))
    rank = jnp.sum(jnp.where(chosen, counts, 0.0), axis=1, keepdims=True)
    logits = dot(tok_ref[...], router_ref[...])
    gate = jax.nn.sigmoid(jnp.sum(jnp.where(chosen, logits, 0.0), axis=1, keepdims=True))
    gate_s[...] = jnp.broadcast_to(gate, (ROWS, 128))
    live = lax.broadcasted_iota(I32, (ROWS, 1), 0) < live_ref[0]
    target = jnp.where(live, ids * (2.0 * MOST) + rank, -1000.0)
    diag = iota((ROWS, ROWS), 0) == iota((ROWS, ROWS), 1)
    target_row = jnp.sum(jnp.where(diag, target, 0.0), axis=0, keepdims=True)
    slot = iota((BOTH, ROWS), 0)
    plc[:, :ROWS] = onehot(slot == target_row)
    plc[:, ROWS:] = onehot(slot == target_row + MOST)
    lane = iota((ROWS, BOTH), 1)
    pltx[...] = onehot(lane == target)
    pltc[...] = onehot(lane == target + MOST)
    column, line = iota((BOTH, 1), 0), iota((1, BOTH), 1)
    across, down = iota((BOTH, BOTH), 1), iota((BOTH, BOTH), 0)
    p1[...] = onehot(source_1(column) == across)
    p1t[...] = onehot(source_1(line) == down)
    p2[...] = onehot(source_2(column) == across)
    p2t[...] = onehot(source_2(line) == down)

    pl.semaphore_wait(barrier, NZ + NQ + NT - 3)

    def piece(s):
        return pl.ds(pl.multiple_of(s * C, C), C)

    @pl.loop(0, NC)
    def _(s):
        cot = (gate_s[:, :1] * og_ref[:, piece(s)].astype(F32)).astype(BF16)
        both = jnp.concatenate([tok_ref[:, piece(s)], cot], axis=0)
        box[s] = dot(plc[...], both).astype(BF16).reshape(NZ, NQ * 2 * MOST, C)
        for d in range(1, NZ):
            zcopy(s, d).start()
        inz[s, z] = box[s, z]

    hid[...] = jnp.zeros_like(hid)
    dh[...] = jnp.zeros_like(dh)
    lg[...] = jnp.zeros_like(lg)
    own = onehot(iota((8, EXPERTS), 1) == me.astype(F32))

    @pl.loop(0, NC)
    def _(s):
        rrow[s] = dot(own, router_ref[piece(s), :], NTD)

    def rows_of(s):
        return yb[s, :, :SLOTS, :].reshape(NT * SLOTS, C)

    def cots_of(s):
        return yb[s, :, SLOTS:, :].reshape(NT * SLOTS, C)

    def dispatch_1(s):
        for d in range(1, NZ):
            zland(s, d).wait_recv()
        outx[s] = dot(p1[...], inz[s].reshape(BOTH, C)).astype(BF16).reshape(NQ, 2 * NZ * MOST, C)
        for d in range(1, NQ):
            xcopy(s, d).start()
        inx[s, q] = outx[s, q]

    def dispatch_2(s):
        for d in range(1, NQ):
            xland(s, d).wait_recv()
        yb[s, t] = dot(p2[...], inx[s].reshape(BOTH, C)).astype(BF16)
        ycopy(s, 0).start()
        ycopy(s, 1).start()

    def dispatch_3(s):
        yland(s, 0).wait_recv()
        ycopy(s, 2).start()
        yland(s, 1).wait_recv()
        ycopy(s, 3).start()

    def dispatch_4(s):
        yland(s, 2).wait_recv()
        yland(s, 3).wait_recv()
        for copy in weights(s):
            copy.wait()
        lg[...] += dot(rows_of(s), router_ref[piece(s), :])

        @pl.loop(0, H // N)
        def _(n):
            part = pl.ds(pl.multiple_of(n * N, N), N)
            hid[:, part] += dot(rows_of(s), wu[s, :, part])
            dh[:, part] += dot(cots_of(s), wd[s, part, :], NTD)

    @pl.loop(0, NC + 4)
    def _(i):
        @pl.when(i < NC)
        def _():
            dispatch_1(i)

        @pl.when((i >= 1) & (i < NC + 1))
        def _():
            dispatch_2(i - 1)

        @pl.when((i >= 3) & (i < NC + 3))
        def _():
            dispatch_3(i - 3)

        @pl.when(i >= 4)
        def _():
            dispatch_4(i - 4)

    @pl.loop(0, NC)
    def _(s):
        for d in range(1, NZ):
            zcopy(s, d).wait_send()
        for d in range(1, NQ):
            xcopy(s, d).wait_send()
        for i in range(4):
            ycopy(s, i).wait_send()

    BR = 32

    @pl.loop(0, NT * SLOTS // BR)
    def _(b):
        r = pl.ds(pl.multiple_of(b * BR, BR), BR)
        v, back = hid[r, :], dh[r, :]
        sig = 1.0 / (1.0 + jnp.exp(-v))
        a = (v * sig).astype(BF16)
        act[r, :] = a
        hc[r, :] = (back * (sig * (1.0 + v * (1.0 - sig)))).astype(BF16)
        part = jnp.sum(a.astype(F32) * back, axis=1, keepdims=True)
        mine = iota((BR, EXPERTS), 1) == me.astype(F32)
        logit = jnp.sum(jnp.where(mine, lg[r, :], 0.0), axis=1, keepdims=True)
        slope = part * (1.0 - 1.0 / (1.0 + jnp.exp(-logit)))
        slope_s[r, :] = jnp.broadcast_to(slope, (BR, 128))
        s1 = slope.astype(BF16).astype(F32)
        s2 = (slope - s1).astype(BF16).astype(F32)
        s3 = slope - s1 - s2
        k = iota((BR, 128), 1)
        slope3[r, :] = jnp.where(
            k == 0.0, s1, jnp.where(k == 1.0, s2, jnp.where(k == 2.0, s3, 0.0))
        ).astype(BF16)

    def partial(s, b):
        r = pl.ds(pl.multiple_of(b * SLOTS, SLOTS), SLOTS)
        value = dot(act[r, :], wd[s])
        grad = dot(hc[r, :], wu[s], NTD) + slope_s[r, :1] * rrow[s, :1, :]
        return value, grad

    def return_0(s):
        value, grad = partial(s, far)
        sa[s, 0] = value.astype(BF16)
        sa[s, 1] = grad.astype(BF16)
        acopy(s, 0).start()
        acopy(s, 1).start()

    def return_1(s):
        value, grad = partial(s, right)
        acopy(s, 0).wait_recv()
        sb[s, 0, lo] = (value + ra[s, 0].astype(F32)).astype(BF16)
        sb[s, 0, hi] = grad.astype(BF16)
        bcopy(s, 0).start()
        value, grad = partial(s, left)
        acopy(s, 1).wait_recv()
        sb[s, 1, lo] = value.astype(BF16)
        sb[s, 1, hi] = (grad + ra[s, 1].astype(F32)).astype(BF16)
        bcopy(s, 1).start()

    def return_2(s):
        value, grad = partial(s, t)
        bcopy(s, 0).wait_recv()
        bcopy(s, 1).wait_recv()
        value = value + rb[s, 0, :SLOTS, :].astype(F32) + rb[s, 1, :SLOTS, :].astype(F32)
        grad = grad + rb[s, 0, SLOTS:, :].astype(F32) + rb[s, 1, SLOTS:, :].astype(F32)
        both = jnp.concatenate([value, grad], axis=0).astype(BF16)
        outx[s] = dot(p2t[...], both).astype(BF16).reshape(NQ, 2 * NZ * MOST, C)
        for d in range(1, NQ):
            x2copy(s, d).start()
        rx[s, q] = outx[s, q]

    def return_3(s):
        for d in range(1, NQ):
            x2land(s, d).wait_recv()
        box[s] = dot(p1t[...], rx[s].reshape(BOTH, C)).astype(BF16).reshape(NZ, NQ * 2 * MOST, C)
        for d in range(1, NZ):
            z2copy(s, d).start()
        rz[s, z] = box[s, z]

    def return_4(s):
        for d in range(1, NZ):
            z2land(s, d).wait_recv()
        got = rz[s].reshape(BOTH, C)
        mixed_ref[:, piece(s)] = (gate_s[:, :1] * dot(pltx[...], got)).astype(BF16)
        tgrad_ref[:, piece(s)] = dot(pltc[...], got).astype(BF16)

    def grads_out(s):
        return (
            pltpu.make_async_copy(gsu.at[s % 2], upg_hbm.at[0, piece(s), :], gsem.at[0, s]),
            pltpu.make_async_copy(gsd.at[s % 2], downg_hbm.at[0, :, piece(s)], gsem.at[1, s]),
        )

    def grads(s):
        @pl.when(s >= 2)
        def _():
            for copy in grads_out(s - 2):
                copy.wait()

        @pl.loop(0, H // N)
        def _(n):
            part = pl.ds(pl.multiple_of(n * N, N), N)
            gsd[s % 2, part, :] = dot(act[:, part], cots_of(s), TND).astype(BF16)
            gsu[s % 2, :, part] = dot(rows_of(s), hc[:, part], TND).astype(BF16)

        for copy in grads_out(s):
            copy.start()

    def vector_0():
        @pl.loop(0, NC)
        def _(s):
            three = dot(slope3[...], rows_of(s), TND)
            vy[t, :, piece(s)] = jnp.sum(three, axis=0, keepdims=True)

        for d in range(1, NT):
            vycopy(d).start()

    def vector_1():
        for d in range(1, NT):
            vyland(d).wait_recv()
        vx[q] = (vy[0] + vy[1]) + (vy[2] + vy[3])
        for d in range(1, NQ):
            vxcopy(d).start()

    def vector_2():
        for d in range(1, NQ):
            vxland(d).wait_recv()
        for d in range(1, NZ):
            vzcopy(d).start()
        vz[z] = vx[...]

    @pl.loop(0, NC + 4)
    def _(j):
        @pl.when(j < NC)
        def _():
            return_0(j)

        @pl.when((j >= 1) & (j < NC + 1))
        def _():
            return_1(j - 1)

        @pl.when(j == 1)
        def _():
            vector_0()

        @pl.when(j == 3)
        def _():
            vector_1()

        @pl.when(j == 5)
        def _():
            vector_2()

        @pl.when((j >= 1) & (j < NC + 1))
        def _():
            grads(j - 1)

        @pl.when((j >= 2) & (j < NC + 2))
        def _():
            return_2(j - 2)

        @pl.when((j >= 3) & (j < NC + 3))
        def _():
            return_3(j - 3)

        @pl.when(j >= 4)
        def _():
            return_4(j - 4)

    for d in range(1, NZ):
        vzland(d).wait_recv()
    rgrad_ref[...] = vz[...].reshape(EXPERTS, 1, C * NC)
    for d in range(1, NT):
        vycopy(d).wait_send()
    for d in range(1, NQ):
        vxcopy(d).wait_send()
    for d in range(1, NZ):
        vzcopy(d).wait_send()

    @pl.loop(0, NC)
    def _(s):
        for i in range(2):
            acopy(s, i).wait_send()
            bcopy(s, i).wait_send()
        for d in range(1, NQ):
            x2copy(s, d).wait_send()
        for d in range(1, NZ):
            z2copy(s, d).wait_send()

    for s in (NC - 2, NC - 1):
        for copy in grads_out(s):
            copy.wait()


def per_device(tokens, expert_ids, live_counts, router, up_weight, down_weight, out_grad):
    width = tokens.shape[1]
    assert tokens.shape == (ROWS, C * NC) and router.shape[1] == EXPERTS
    assert up_weight.shape == (1, C * NC, H)
    vmem = pl.BlockSpec(memory_space=pltpu.VMEM)
    smem = pl.BlockSpec(memory_space=pltpu.SMEM)
    hbm = pl.BlockSpec(memory_space=pl.ANY)
    all_rows = NT * SLOTS
    V, DMA = pltpu.VMEM, pltpu.SemaphoreType.DMA
    scratch = [
        V((NC, NZ, NQ * 2 * MOST, C), BF16),
        V((NC, NZ, NQ * 2 * MOST, C), BF16),
        V((NC, NQ, 2 * NZ * MOST, C), BF16),
        V((NC, NQ, 2 * NZ * MOST, C), BF16),
        V((NC, NT, BOTH, C), BF16),
        V((NC, C, H), BF16),
        V((NC, H, C), BF16),
        V((all_rows, H), F32),
        V((all_rows, H), F32),
        V((all_rows, H), BF16),
        V((all_rows, H), BF16),
        V((all_rows, EXPERTS), F32),
        V((ROWS, 128), F32),
        V((all_rows, 128), F32),
        V((all_rows, 128), BF16),
        V((NC, 2, SLOTS, C), BF16),
        V((NC, 2, SLOTS, C), BF16),
        V((NC, 2, BOTH, C), BF16),
        V((NC, 2, BOTH, C), BF16),
        V((NC, NQ, 2 * NZ * MOST, C), BF16),
        V((NC, NZ, NQ * 2 * MOST, C), BF16),
        V((2, C, H), BF16),
        V((2, H, C), BF16),
        V((BOTH, BOTH), BF16),
        V((BOTH, BOTH), BF16),
        V((BOTH, BOTH), BF16),
        V((BOTH, BOTH), BF16),
        V((BOTH, 2 * ROWS), BF16),
        V((ROWS, BOTH), BF16),
        V((ROWS, BOTH), BF16),
        V((NC, 8, C), F32),
        V((NT, 1, width), F32),
        V((NQ, 1, width), F32),
        V((NZ, NQ, 1, width), F32),
        DMA((2, NC)),
        DMA((NC, NZ)), DMA((NC, NZ)), DMA((NC, NQ)), DMA((NC, NQ)), DMA((NC, 4)), DMA((NC, 4)),
        DMA((NC, 2)), DMA((NC, 2)), DMA((NC, 2)), DMA((NC, 2)),
        DMA((NC, NQ)), DMA((NC, NQ)), DMA((NC, NZ)), DMA((NC, NZ)),
        DMA((2, NC)),
        DMA((NT,)), DMA((NT,)), DMA((NQ,)), DMA((NQ,)), DMA((NZ,)), DMA((NZ,)),
    ]
    S = jax.ShapeDtypeStruct
    mixed, tgrad, upg, downg, rgrad = pl.pallas_call(
        kernel,
        out_shape=(
            S((ROWS, width), BF16),
            S((ROWS, width), BF16),
            S((1, width, H), BF16),
            S((1, H, width), BF16),
            S((EXPERTS, 1, width), F32),
        ),
        in_specs=[vmem, smem, vmem, vmem, vmem, hbm, hbm],
        out_specs=(vmem, vmem, hbm, hbm, vmem),
        scratch_shapes=scratch,
        compiler_params=pltpu.CompilerParams(
            collective_id=0, has_side_effects=True, vmem_limit_bytes=67043328
        ),
    )(expert_ids, live_counts, router, tokens, out_grad, up_weight, down_weight)
    return (mixed, tgrad, upg, downg, rgrad.reshape(EXPERTS, width).T)


def solution(mesh):
    rows = P(("expert", "tensor"), None)
    in_specs = (
        rows,
        rows,
        P(("expert", "tensor")),
        P(),
        P("expert", None, "tensor"),
        P("expert", "tensor", None),
        rows,
    )
    out_specs = (rows, rows, P("expert", None, "tensor"), P("expert", "tensor", None), P())
    return jax.shard_map(
        per_device, mesh=mesh, in_specs=in_specs, out_specs=out_specs, check_vma=False
    )
```

```python
import jax
import jax.numpy as jnp
from jax import lax
from jax.experimental import pallas as pl
from jax.experimental.pallas import tpu as pltpu
from jax.sharding import PartitionSpec as P

F32, BF16, I32 = jnp.float32, jnp.bfloat16, jnp.int32
MESH = pl.DeviceIdType.MESH

NZ, NQ, NT = 4, 8, 4
EXPERTS = NZ * NQ
ROWS, MOST = 128, 6
SLOTS = EXPERTS * MOST
BOTH = 2 * SLOTS
C, NC = 512, 5
NN, NS = 3, 2
NU = 2 * NS
ZR, XR = NQ * 2 * MOST, 2 * NZ * MOST
H = 1024
N = 256


def dot(a, b, dims=((1,), (0,))):
    return lax.dot_general(a, b, (dims, ((), ())), preferred_element_type=F32)


NTD = ((1,), (1,))
TND = ((0,), (0,))


def iota(shape, axis):
    return lax.broadcasted_iota(I32, shape, axis).astype(F32)


def onehot(mask):
    return jnp.where(mask, 1.0, 0.0).astype(BF16)


def div(a, b):
    return jnp.floor((a + 0.5) * (1.0 / b))


def source_1(o):
    q = div(o, 2 * NZ * MOST)
    r = o - q * (2 * NZ * MOST)
    a = div(r, NZ * MOST)
    r = r - a * (NZ * MOST)
    z = div(r, MOST)
    k = r - z * MOST
    return z * (NQ * 2 * MOST) + q * (2 * MOST) + a * MOST + k


def source_2(o):
    a = div(o, SLOTS)
    r = o - a * SLOTS
    q = div(r, NZ * MOST)
    m = r - q * (NZ * MOST)
    return q * (2 * NZ * MOST) + a * (NZ * MOST) + m


def kernel(
    ids_ref, live_ref, router_ref, tok_ref, og_ref, up_hbm, down_hbm,
    mixed_ref, tgrad_ref, upg_hbm, downg_hbm, rgrad_ref,
    box, inz, outx, inx, ubox, uinz, uoutx, uinx, raw, yb, wu, wd, hid, dh, act, hc,
    lg, gate_s, slope_s, slope3, sa, ra, sb, rb, ua, ub, gsu, gsd,
    p1, p1t, p2, p2t, plc, pltx, pltc, rrow, vt, vy, vx, vz,
    wsem, zs, zr, xs, xr, ys, yr, as_, ar, bs, br, uzs, uzr, uxs, uxr, rs, rr,
    uas, uar, ubs, ubr, gsem, vts, vtr, vys, vyr, vxs, vxr, vzs, vzr, free,
):
    me = lax.axis_index("expert")
    t = lax.axis_index("tensor")
    z, q = me // NQ, me % NQ
    left, right, far = (t + NT - 1) % NT, (t + 1) % NT, (t + 2) % NT
    lo, hi = pl.ds(0, SLOTS), pl.ds(SLOTS, SLOTS)
    rlo, rhi = pl.ds(0, ROWS), pl.ds(ROWS, ROWS)
    ZD, XD, YD = range(1, NZ), range(1, NQ), range(1, NT)

    def zpeer(d):
        return (((z + d) % NZ) * NQ + q, t)

    def xpeer(d):
        return (z * NQ + (q + d) % NQ, t)

    def ypeer(d):
        return (me, (t + d) % NT)

    def remote(src, dst, ssem, rsem, peer):
        return pltpu.make_async_remote_copy(
            src_ref=src, dst_ref=dst, send_sem=ssem, recv_sem=rsem,
            device_id=peer, device_id_type=MESH,
        )

    def piece(s):
        return pl.ds(pl.multiple_of(s * C, C), C)

    def normal(n):
        return n + (n + 1) // 2

    def special(v):
        return 1 + 3 * v

    def weights(s):
        return (
            pltpu.make_async_copy(up_hbm.at[0, piece(s), :], wu.at[s], wsem.at[0, s]),
            pltpu.make_async_copy(down_hbm.at[0, :, piece(s)], wd.at[s], wsem.at[1, s]),
        )

    def zcopy(n, d):
        return remote(box.at[n, (z + d) % NZ], inz.at[n, z], zs.at[n, d], zr.at[n, d], zpeer(d))

    def zland(n, d):
        return remote(box.at[n, z], inz.at[n, (z + NZ - d) % NZ], zs.at[n, d], zr.at[n, d], zpeer(d))

    def xcopy(n, d):
        return remote(outx.at[n, (q + d) % NQ], inx.at[n, q], xs.at[n, d], xr.at[n, d], xpeer(d))

    def xland(n, d):
        return remote(outx.at[n, q], inx.at[n, (q + NQ - d) % NQ], xs.at[n, d], xr.at[n, d], xpeer(d))

    def uzcopy(u, d):
        return remote(ubox.at[u, (z + d) % NZ], uinz.at[u, z], uzs.at[u, d], uzr.at[u, d], zpeer(d))

    def uzland(u, d):
        return remote(ubox.at[u, z], uinz.at[u, (z + NZ - d) % NZ], uzs.at[u, d], uzr.at[u, d], zpeer(d))

    def uxcopy(u, d):
        return remote(uoutx.at[u, (q + d) % NQ], uinx.at[u, q], uxs.at[u, d], uxr.at[u, d], xpeer(d))

    def uxland(u, d):
        return remote(uoutx.at[u, q], uinx.at[u, (q + NQ - d) % NQ], uxs.at[u, d], uxr.at[u, d], xpeer(d))

    SIDE = (1, NT - 1, 1, NT - 1)

    def ycopy(n, i):
        s = normal(n)
        src = (yb.at[s, t], yb.at[s, t], yb.at[s, left, lo], yb.at[s, right, hi])[i]
        return remote(src, src, ys.at[n, i], yr.at[n, i], ypeer(SIDE[i]))

    def yland(n, i):
        s = normal(n)
        dst = (yb.at[s, left], yb.at[s, right], yb.at[s, far, lo], yb.at[s, far, hi])[i]
        return remote(dst, dst, ys.at[n, i], yr.at[n, i], ypeer(SIDE[i]))

    def rcopy(v, i):
        src = (raw.at[v, t], raw.at[v, t], raw.at[v, left, rlo], raw.at[v, right, rhi])[i]
        return remote(src, src, rs.at[v, i], rr.at[v, i], ypeer(SIDE[i]))

    def rland(v, i):
        dst = (raw.at[v, left], raw.at[v, right], raw.at[v, far, rlo], raw.at[v, far, rhi])[i]
        return remote(dst, dst, rs.at[v, i], rr.at[v, i], ypeer(SIDE[i]))

    def acopy(n, i):
        return remote(sa.at[n, i], ra.at[n, i], as_.at[n, i], ar.at[n, i], ypeer(SIDE[i]))

    def bcopy(n, i):
        return remote(sb.at[n, i], rb.at[n, i], bs.at[n, i], br.at[n, i], ypeer(SIDE[i]))

    def uacopy(v, i):
        src = raw.at[v, 2, (rlo, rhi)[i]]
        return remote(src, ua.at[v, i], uas.at[v, i], uar.at[v, i], ypeer(SIDE[i]))

    def ubcopy(v, i):
        return remote(raw.at[v, SIDE[i]], ub.at[v, i], ubs.at[v, i], ubr.at[v, i], ypeer(SIDE[i]))

    def vtcopy(d):
        return remote(vt.at[t], vt.at[t], vts.at[d], vtr.at[d], ypeer(d))

    def vtland(d):
        dst = vt.at[(t + NT - d) % NT]
        return remote(dst, dst, vts.at[d], vtr.at[d], ypeer(d))

    def vycopy(d):
        return remote(vy.at[t], vy.at[t], vys.at[d], vyr.at[d], ypeer(d))

    def vyland(d):
        dst = vy.at[(t + NT - d) % NT]
        return remote(dst, dst, vys.at[d], vyr.at[d], ypeer(d))

    def vxcopy(d):
        return remote(vx.at[q], vx.at[q], vxs.at[d], vxr.at[d], xpeer(d))

    def vxland(d):
        dst = vx.at[(q + NQ - d) % NQ]
        return remote(dst, dst, vxs.at[d], vxr.at[d], xpeer(d))

    def vzcopy(d):
        return remote(vx, vz.at[z], vzs.at[d], vzr.at[d], zpeer(d))

    def vzland(d):
        return remote(vx, vz.at[(z + NZ - d) % NZ], vzs.at[d], vzr.at[d], zpeer(d))

    for s in range(NC):
        for copy in weights(s):
            copy.start()

    barrier = pltpu.get_barrier_semaphore()
    for peers, ds in ((zpeer, ZD), (xpeer, XD), (ypeer, YD)):
        for d in ds:
            pl.semaphore_signal(barrier, inc=1, device_id=peers(d), device_id_type=MESH)

    diag = iota((ROWS, ROWS), 0) == iota((ROWS, ROWS), 1)

    def turned(line):
        return jnp.sum(jnp.where(diag, line, 0.0), axis=1, keepdims=True)

    ids = turned(ids_ref[...].astype(F32))
    chosen = ids == iota((ROWS, EXPERTS), 1)
    tri = onehot(iota((ROWS, ROWS), 0) > iota((ROWS, ROWS), 1))
    counts = dot(tri, onehot(chosen))
    rank = jnp.sum(jnp.where(chosen, counts, 0.0), axis=1, keepdims=True)
    logits = dot(tok_ref[...], router_ref[...], NTD)
    gate = jax.nn.sigmoid(jnp.sum(jnp.where(chosen, logits, 0.0), axis=1, keepdims=True))
    gate_s[...] = jnp.broadcast_to(gate, (ROWS, 128))
    live = lax.broadcasted_iota(I32, (ROWS, 1), 0) < live_ref[0]
    target = jnp.where(live, ids * (2.0 * MOST) + rank, -1000.0)
    vt[t] = jnp.sum(jnp.where(diag, target, 0.0), axis=0, keepdims=True)

    def both_of(s):
        cot = (gate_s[:, :1] * og_ref[:, piece(s)].astype(F32)).astype(BF16)
        return jnp.concatenate([tok_ref[:, piece(s)], cot], axis=0)

    def place(b):
        line = vt[b]
        slot = iota((BOTH, ROWS), 0)
        plc[b, :, :ROWS] = onehot(slot == line)
        plc[b, :, ROWS:] = onehot(slot == line + MOST)
        column = turned(line)
        lane = iota((ROWS, BOTH), 1)
        pltx[b] = onehot(lane == column)
        pltc[b] = onehot(lane == column + MOST)

    @pl.loop(0, NS)
    def _(v):
        raw[v, t] = both_of(special(v))

    pl.semaphore_wait(barrier, NZ + NQ + NT - 3)

    @pl.loop(0, NS)
    def _(v):
        rcopy(v, 0).start()
        rcopy(v, 1).start()

    for d in YD:
        vtcopy(d).start()
    place(t)

    @pl.loop(0, NN)
    def _(n):
        box[n] = dot(plc[t], both_of(normal(n))).astype(BF16).reshape(NZ, ZR, C)
        for d in ZD:
            zcopy(n, d).start()
        inz[n, z] = box[n, z]

    column, line = iota((BOTH, 1), 0), iota((1, BOTH), 1)
    across, down = iota((BOTH, BOTH), 1), iota((BOTH, BOTH), 0)
    p1[...] = onehot(source_1(column) == across)
    p1t[...] = onehot(source_1(line) == down)
    p2[...] = onehot(source_2(column) == across)
    p2t[...] = onehot(source_2(line) == down)
    for d in YD:
        vtland(d).wait_recv()
        place((t + NT - d) % NT)

    hid[...] = jnp.zeros_like(hid)
    dh[...] = jnp.zeros_like(dh)
    lg[...] = jnp.zeros_like(lg)
    own = onehot(iota((8, EXPERTS), 1) == me.astype(F32))

    @pl.loop(0, NC)
    def _(s):
        rrow[s] = dot(own, router_ref[:, piece(s)])

    def rows_of(s):
        return yb[s, :, :SLOTS, :].reshape(NT * SLOTS, C)

    def cots_of(s):
        return yb[s, :, SLOTS:, :].reshape(NT * SLOTS, C)

    def order(perm, rows, shape):
        return dot(perm[...], rows.reshape(BOTH, C)).astype(BF16).reshape(shape)

    def out_z(n):
        for d in ZD:
            zland(n, d).wait_recv()
        outx[n] = order(p1, inz[n], (NQ, XR, C))
        for d in XD:
            xcopy(n, d).start()
        inx[n, q] = outx[n, q]

    def out_x(n):
        for d in XD:
            xland(n, d).wait_recv()
        yb[normal(n), t] = order(p2, inx[n], (BOTH, C))
        ycopy(n, 0).start()
        ycopy(n, 1).start()

    def out_y(n):
        yland(n, 0).wait_recv()
        ycopy(n, 2).start()
        yland(n, 1).wait_recv()
        ycopy(n, 3).start()

    def raw_on(v):
        rland(v, 0).wait_recv()
        rcopy(v, 2).start()
        rland(v, 1).wait_recv()
        rcopy(v, 3).start()

    def unit_box(u):
        v, h = u // 2, u % 2

        @pl.when(h == 1)
        def _():
            rland(v, 2).wait_recv()
            rland(v, 3).wait_recv()

        for j in range(2):
            b = (t + 2 * h + j) % NT
            ubox[u, :, j] = dot(plc[b], raw[v, b]).astype(BF16).reshape(NZ, ZR, C)
        for d in ZD:
            uzcopy(u, d).start()
        uinz[u, z] = ubox[u, z]

    def unit_z(u):
        for d in ZD:
            uzland(u, d).wait_recv()
        for j in range(2):
            uoutx[u, :, j] = order(p1, uinz[u, :, j], (NQ, XR, C))
        for d in XD:
            uxcopy(u, d).start()
        uinx[u, q] = uoutx[u, q]

    def unit_x(u):
        for d in XD:
            uxland(u, d).wait_recv()
        v, h = u // 2, u % 2
        for j in range(2):
            yb[special(v), (t + 2 * h + j) % NT] = order(p2, uinx[u, :, j], (BOTH, C))

    def work(s):
        for copy in weights(s):
            copy.wait()
        lg[...] += dot(rows_of(s), router_ref[:, piece(s)], NTD)

        @pl.loop(0, H // N)
        def _(n):
            part = pl.ds(pl.multiple_of(n * N, N), N)
            hid[:, part] += dot(rows_of(s), wu[s, :, part])
            dh[:, part] += dot(cots_of(s), wd[s, part, :], NTD)

    def whole(n):
        yland(n, 2).wait_recv()
        yland(n, 3).wait_recv()

    @pl.loop(0, 12)
    def _(i):
        @pl.when(i < NN)
        def _():
            out_z(i)

        @pl.when(i < NS)
        def _():
            raw_on(i)

        @pl.when((i >= 1) & (i < NN + 1))
        def _():
            out_x(i - 1)

        @pl.when((i >= 1) & (i < NU + 1))
        def _():
            unit_box(i - 1)

        @pl.when((i >= 4) & (i < NU + 4))
        def _():
            unit_z(i - 4)

        @pl.when(((i >= 5) & (i < 8)) | (i == 11))
        def _():
            unit_x(i - 5 - 3 * (i // 11))

        @pl.when((i >= 4) & (i < NN + 4))
        def _():
            out_y(i - 4)

        @pl.when(i == 7)
        def _():
            whole(0)

        @pl.when(i >= 9)
        def _():
            @pl.when(i < 11)
            def _():
                whole(i - 8)

        @pl.when(i >= 7)
        def _():
            work(i - 7)

    for peers, ds in ((zpeer, ZD), (xpeer, XD)):
        for d in ds:
            pl.semaphore_signal(free, inc=1, device_id=peers(d), device_id_type=MESH)

    @pl.loop(0, NN)
    def _(n):
        for d in ZD:
            zcopy(n, d).wait_send()
        for d in XD:
            xcopy(n, d).wait_send()
        for i in range(4):
            ycopy(n, i).wait_send()

    @pl.loop(0, NU)
    def _(u):
        for d in ZD:
            uzcopy(u, d).wait_send()
        for d in XD:
            uxcopy(u, d).wait_send()

    @pl.loop(0, NS)
    def _(v):
        for i in range(4):
            rcopy(v, i).wait_send()

    BR = 32

    @pl.loop(0, NT * SLOTS // BR)
    def _(b):
        r = pl.ds(pl.multiple_of(b * BR, BR), BR)
        v, back = hid[r, :], dh[r, :]
        sig = 1.0 / (1.0 + jnp.exp(-v))
        a = (v * sig).astype(BF16)
        act[r, :] = a
        hc[r, :] = (back * (sig * (1.0 + v * (1.0 - sig)))).astype(BF16)
        part = jnp.sum(a.astype(F32) * back, axis=1, keepdims=True)
        mine = iota((BR, EXPERTS), 1) == me.astype(F32)
        logit = jnp.sum(jnp.where(mine, lg[r, :], 0.0), axis=1, keepdims=True)
        slope = part * (1.0 - 1.0 / (1.0 + jnp.exp(-logit)))
        slope_s[r, :] = jnp.broadcast_to(slope, (BR, 128))
        s1 = slope.astype(BF16).astype(F32)
        s2 = (slope - s1).astype(BF16).astype(F32)
        s3 = slope - s1 - s2
        k = iota((BR, 128), 1)
        slope3[r, :] = jnp.where(
            k == 0.0, s1, jnp.where(k == 1.0, s2, jnp.where(k == 2.0, s3, 0.0))
        ).astype(BF16)

    pl.semaphore_wait(free, NZ + NQ - 2)

    def partial(s, b):
        r = pl.ds(pl.multiple_of(b * SLOTS, SLOTS), SLOTS)
        value = dot(act[r, :], wd[s])
        grad = dot(hc[r, :], wu[s], NTD) + slope_s[r, :1] * rrow[s, :1, :]
        return value, grad

    def back_far(n):
        value, grad = partial(normal(n), far)
        sa[n, 0] = value.astype(BF16)
        sa[n, 1] = grad.astype(BF16)
        acopy(n, 0).start()
        acopy(n, 1).start()

    def back_near(n):
        value, grad = partial(normal(n), right)
        acopy(n, 0).wait_recv()
        sb[n, 0, lo] = (value + ra[n, 0].astype(F32)).astype(BF16)
        sb[n, 0, hi] = grad.astype(BF16)
        bcopy(n, 0).start()
        value, grad = partial(normal(n), left)
        acopy(n, 1).wait_recv()
        sb[n, 1, lo] = value.astype(BF16)
        sb[n, 1, hi] = (grad + ra[n, 1].astype(F32)).astype(BF16)
        bcopy(n, 1).start()

    def back_own(n):
        value, grad = partial(normal(n), t)
        bcopy(n, 0).wait_recv()
        bcopy(n, 1).wait_recv()
        value = value + rb[n, 0, :SLOTS, :].astype(F32) + rb[n, 1, :SLOTS, :].astype(F32)
        grad = grad + rb[n, 0, SLOTS:, :].astype(F32) + rb[n, 1, SLOTS:, :].astype(F32)
        both = jnp.concatenate([value, grad], axis=0).astype(BF16)
        outx[n] = order(p2t, both, (NQ, XR, C))
        for d in XD:
            xcopy(n, d).start()
        inx[n, q] = outx[n, q]

    def back_x(n):
        for d in XD:
            xland(n, d).wait_recv()
        box[n] = order(p1t, inx[n], (NZ, ZR, C))
        for d in ZD:
            zcopy(n, d).start()
        inz[n, z] = box[n, z]

    def back_z(n):
        for d in ZD:
            zland(n, d).wait_recv()
        got = inz[n].reshape(BOTH, C)
        cols = piece(normal(n))
        mixed_ref[:, cols] = (gate_s[:, :1] * dot(pltx[t], got)).astype(BF16)
        tgrad_ref[:, cols] = dot(pltc[t], got).astype(BF16)

    def unit_back(u):
        v, h = u // 2, 1 - u % 2
        for j in range(2):
            value, grad = partial(special(v), (t + 2 * h + j) % NT)
            both = jnp.concatenate([value, grad], axis=0).astype(BF16)
            uoutx[u, :, j] = order(p2t, both, (NQ, XR, C))
        for d in XD:
            uxcopy(u, d).start()
        uinx[u, q] = uoutx[u, q]

    def unit_back_x(u):
        for d in XD:
            uxland(u, d).wait_recv()
        for j in range(2):
            ubox[u, :, j] = order(p1t, uinx[u, :, j], (NZ, ZR, C))
        for d in ZD:
            uzcopy(u, d).start()
        uinz[u, z] = ubox[u, z]

    def unit_back_z(u):
        for d in ZD:
            uzland(u, d).wait_recv()
        v, h = u // 2, 1 - u % 2
        for j in range(2):
            o = 2 * h + j
            b = (t + o) % NT
            got = uinz[u, :, j].reshape(BOTH, C)
            raw[v, o, rlo] = dot(pltx[b], got).astype(BF16)
            raw[v, o, rhi] = dot(pltc[b], got).astype(BF16)

        @pl.when(h == 1)
        def _():
            uacopy(v, 0).start()
            uacopy(v, 1).start()

        @pl.when(h == 0)
        def _():
            uacopy(v, 0).wait_recv()
            raw[v, 1, rlo] = (raw[v, 1, rlo].astype(F32) + ua[v, 0].astype(F32)).astype(BF16)
            ubcopy(v, 0).start()
            uacopy(v, 1).wait_recv()
            raw[v, 3, rhi] = (raw[v, 3, rhi].astype(F32) + ua[v, 1].astype(F32)).astype(BF16)
            ubcopy(v, 1).start()

    def unit_sum(v):
        ubcopy(v, 0).wait_recv()
        ubcopy(v, 1).wait_recv()
        got = raw[v, 0].astype(F32) + ub[v, 0].astype(F32) + ub[v, 1].astype(F32)
        cols = piece(special(v))
        value = got[:ROWS].astype(BF16).astype(F32)
        mixed_ref[:, cols] = (gate_s[:, :1] * value).astype(BF16)
        tgrad_ref[:, cols] = got[ROWS:].astype(BF16)

    def grads_out(s, n):
        part = pl.ds(pl.multiple_of(n * N, N), N)
        k = n % 2
        return (
            pltpu.make_async_copy(gsu.at[k], upg_hbm.at[0, piece(s), part], gsem.at[0, k]),
            pltpu.make_async_copy(gsd.at[k], downg_hbm.at[0, part, piece(s)], gsem.at[1, k]),
        )

    def grads(s):
        @pl.loop(0, H // N)
        def _(n):
            @pl.when((s > 0) | (n >= 2))
            def _():
                for copy in grads_out(s, n):
                    copy.wait()

            part = pl.ds(pl.multiple_of(n * N, N), N)
            gsd[n % 2] = dot(act[:, part], cots_of(s), TND).astype(BF16)
            gsu[n % 2] = dot(rows_of(s), hc[:, part], TND).astype(BF16)
            for copy in grads_out(s, n):
                copy.start()

    def vector_0():
        @pl.loop(0, NC)
        def _(s):
            three = dot(slope3[...], rows_of(s), TND)
            vy[t, :, piece(s)] = jnp.sum(three, axis=0, keepdims=True)

        for d in YD:
            vycopy(d).start()

    def vector_1():
        for d in YD:
            vyland(d).wait_recv()
        vx[q] = (vy[0] + vy[1]) + (vy[2] + vy[3])
        for d in XD:
            vxcopy(d).start()

    def vector_2():
        for d in XD:
            vxland(d).wait_recv()
        for d in ZD:
            vzcopy(d).start()
        vz[z] = vx[...]

    @pl.loop(0, 10)
    def _(j):
        @pl.when(j < NN)
        def _():
            back_far(j)

        @pl.when((j >= 1) & (j < NN + 1))
        def _():
            back_near(j - 1)

        @pl.when(j < NU)
        def _():
            unit_back(j)

        @pl.when(j == 3)
        def _():
            vector_0()

        @pl.when(j == 5)
        def _():
            vector_1()

        @pl.when(j == 7)
        def _():
            vector_2()

        @pl.when((j >= 3) & (j < NU + 3))
        def _():
            unit_back_x(j - 3)

        @pl.when((j >= 4) & (j < NU + 4))
        def _():
            unit_back_z(j - 4)

        @pl.when((j >= 4) & (j < NC + 4))
        def _():
            grads(j - 4)

        @pl.when((j >= 3) & (j < NN + 3))
        def _():
            back_own(j - 3)

        @pl.when((j >= 4) & (j < NN + 4))
        def _():
            back_x(j - 4)

        @pl.when((j >= 5) & (j < NN + 5))
        def _():
            back_z(j - 5)

        @pl.when(j >= 8)
        def _():
            unit_sum(j - 8)

    for d in ZD:
        vzland(d).wait_recv()
    rgrad_ref[...] = vz[...].reshape(EXPERTS, 1, C * NC)
    for d in YD:
        vtcopy(d).wait_send()
        vycopy(d).wait_send()
    for d in XD:
        vxcopy(d).wait_send()
    for d in ZD:
        vzcopy(d).wait_send()

    @pl.loop(0, NN)
    def _(n):
        for i in range(2):
            acopy(n, i).wait_send()
            bcopy(n, i).wait_send()
        for d in XD:
            xcopy(n, d).wait_send()
        for d in ZD:
            zcopy(n, d).wait_send()

    @pl.loop(0, NU)
    def _(u):
        for d in XD:
            uxcopy(u, d).wait_send()
        for d in ZD:
            uzcopy(u, d).wait_send()

    @pl.loop(0, NS)
    def _(v):
        for i in range(2):
            uacopy(v, i).wait_send()
            ubcopy(v, i).wait_send()

    for n in range(2):
        for copy in grads_out(NC - 1, n):
            copy.wait()


def per_device(tokens, expert_ids, live_counts, router, up_weight, down_weight, out_grad):
    width = tokens.shape[1]
    assert tokens.shape == (ROWS, C * NC) and router.shape[1] == EXPERTS
    assert up_weight.shape == (1, C * NC, H)
    vmem = pl.BlockSpec(memory_space=pltpu.VMEM)
    smem = pl.BlockSpec(memory_space=pltpu.SMEM)
    hbm = pl.BlockSpec(memory_space=pl.ANY)
    every = NT * SLOTS
    V, DMA = pltpu.VMEM, pltpu.SemaphoreType.DMA
    scratch = [
        V((NN, NZ, ZR, C), BF16),
        V((NN, NZ, ZR, C), BF16),
        V((NN, NQ, XR, C), BF16),
        V((NN, NQ, XR, C), BF16),
        V((NU, NZ, 2, ZR, C), BF16),
        V((NU, NZ, 2, ZR, C), BF16),
        V((NU, NQ, 2, XR, C), BF16),
        V((NU, NQ, 2, XR, C), BF16),
        V((NS, NT, 2 * ROWS, C), BF16),
        V((NC, NT, BOTH, C), BF16),
        V((NC, C, H), BF16),
        V((NC, H, C), BF16),
        V((every, H), F32),
        V((every, H), F32),
        V((every, H), BF16),
        V((every, H), BF16),
        V((every, EXPERTS), F32),
        V((ROWS, 128), F32),
        V((every, 128), F32),
        V((every, 128), BF16),
        V((NN, 2, SLOTS, C), BF16),
        V((NN, 2, SLOTS, C), BF16),
        V((NN, 2, BOTH, C), BF16),
        V((NN, 2, BOTH, C), BF16),
        V((NS, 2, ROWS, C), BF16),
        V((NS, 2, 2 * ROWS, C), BF16),
        V((2, C, N), BF16),
        V((2, N, C), BF16),
        V((BOTH, BOTH), BF16),
        V((BOTH, BOTH), BF16),
        V((BOTH, BOTH), BF16),
        V((BOTH, BOTH), BF16),
        V((NT, BOTH, 2 * ROWS), BF16),
        V((NT, ROWS, BOTH), BF16),
        V((NT, ROWS, BOTH), BF16),
        V((NC, 8, C), F32),
        V((NT, 1, ROWS), F32),
        V((NT, 1, width), F32),
        V((NQ, 1, width), F32),
        V((NZ, NQ, 1, width), F32),
        DMA((2, NC)),
        DMA((NN, NZ)), DMA((NN, NZ)), DMA((NN, NQ)), DMA((NN, NQ)), DMA((NN, 4)), DMA((NN, 4)),
        DMA((NN, 2)), DMA((NN, 2)), DMA((NN, 2)), DMA((NN, 2)),
        DMA((NU, NZ)), DMA((NU, NZ)), DMA((NU, NQ)), DMA((NU, NQ)), DMA((NS, 4)), DMA((NS, 4)),
        DMA((NS, 2)), DMA((NS, 2)), DMA((NS, 2)), DMA((NS, 2)),
        DMA((2, 2)),
        DMA((NT,)), DMA((NT,)), DMA((NT,)), DMA((NT,)),
        DMA((NQ,)), DMA((NQ,)), DMA((NZ,)), DMA((NZ,)),
        pltpu.SemaphoreType.REGULAR,
    ]
    S = jax.ShapeDtypeStruct
    mixed, tgrad, upg, downg, rgrad = pl.pallas_call(
        kernel,
        out_shape=(
            S((ROWS, width), BF16),
            S((ROWS, width), BF16),
            S((1, width, H), BF16),
            S((1, H, width), BF16),
            S((EXPERTS, 1, width), F32),
        ),
        in_specs=[vmem, smem, vmem, vmem, vmem, hbm, hbm],
        out_specs=(vmem, vmem, hbm, hbm, vmem),
        scratch_shapes=scratch,
        compiler_params=pltpu.CompilerParams(
            collective_id=0, has_side_effects=True, vmem_limit_bytes=67043328
        ),
    )(
        expert_ids.reshape(1, ROWS), live_counts, router.T, tokens, out_grad, up_weight, down_weight
    )
    return (mixed, tgrad, upg, downg, rgrad.reshape(EXPERTS, width).T)


def solution(mesh):
    rows = P(("expert", "tensor"), None)
    in_specs = (
        rows,
        rows,
        P(("expert", "tensor")),
        P(),
        P("expert", None, "tensor"),
        P("expert", "tensor", None),
        rows,
    )
    out_specs = (rows, rows, P("expert", None, "tensor"), P("expert", "tensor", None), P())
    return jax.shard_map(
        per_device, mesh=mesh, in_specs=in_specs, out_specs=out_specs, check_vma=False
    )
```

```python
import jax
import jax.numpy as jnp
from jax import lax
from jax.experimental import pallas as pl
from jax.experimental.pallas import tpu as pltpu
from jax.sharding import PartitionSpec as P

F32, BF16, I32 = jnp.float32, jnp.bfloat16, jnp.int32
MESH = pl.DeviceIdType.MESH

NZ, NQ, NT = 4, 8, 4
EXPERTS = NZ * NQ
ROWS, MOST = 128, 6
SLOTS = EXPERTS * MOST
BOTH = 2 * SLOTS
C, NC = 512, 5
NN, NS = 3, 2
NU = NT * NS
ZR, XR = NQ * 2 * MOST, 2 * NZ * MOST
H = 1024
N = 256


OUT_STEPS = 22
OUT = dict(
    out_z=(1, 3, 4,),
    raw_on=(1, 3,),
    unit_box=(0, 1, 2, 4, 5, 6, 7, 8,),
    out_x=(3, 7, 9,),
    unit_z=(8, 9, 10, 11, 12, 13, 14, 15,),
    unit_x=(9, 10, 11, 12, 13, 14, 16, 19,),
    release=(19,),
    out_y=(9, 11, 13,),
    near=(9, 10, 11, 13, 14,),
    away=(16, 17, 18, 19, 20,),
    middle=(14, 15, 20, 21,),
)
BACK_STEPS = 28
BACK = dict(
    back_far=(0, 1, 2,),
    unit_back=(2, 3, 4, 5, 6, 7, 8, 9,),
    vector_0=(9,),
    back_near=(9, 10, 11,),
    unit_back_x=(8, 9, 11, 12, 13, 15, 16, 20,),
    unit_back_z=(10, 16, 17, 18, 19, 23, 24, 25,),
    grads=(11, 12, 13, 14, 15,),
    back_own=(12, 15, 21,),
    vector_1=(12,),
    vector_2=(15,),
    back_x=(20, 21, 22,),
    unit_sum=(21, 27,),
    back_z=(21, 25, 26,),
)


def dot(a, b, dims=((1,), (0,))):
    return lax.dot_general(a, b, (dims, ((), ())), preferred_element_type=F32)


NTD = ((1,), (1,))
TND = ((0,), (0,))


def iota(shape, axis):
    return lax.broadcasted_iota(I32, shape, axis).astype(F32)


def gray(r):
    return r + r // 2 - 2 * (r // 3)


def at(i, steps, task):
    here, k = i == steps[0], 0
    for step in steps[1:]:
        here = here | (i == step)
        k = k + (i + 64 - step) // 64

    @pl.when(here)
    def _():
        task(k)


def onehot(mask):
    return jnp.where(mask, 1.0, 0.0).astype(BF16)


def div(a, b):
    return jnp.floor((a + 0.5) * (1.0 / b))


def source_1(o):
    q = div(o, 2 * NZ * MOST)
    r = o - q * (2 * NZ * MOST)
    a = div(r, NZ * MOST)
    r = r - a * (NZ * MOST)
    z = div(r, MOST)
    k = r - z * MOST
    return z * (NQ * 2 * MOST) + q * (2 * MOST) + a * MOST + k


def source_2(o):
    a = div(o, SLOTS)
    r = o - a * SLOTS
    q = div(r, NZ * MOST)
    m = r - q * (NZ * MOST)
    return q * (2 * NZ * MOST) + a * (NZ * MOST) + m


def kernel(
    ids_ref, live_ref, router_ref, tok_ref, og_ref, up_hbm, down_hbm,
    mixed_ref, tgrad_ref, upg_hbm, downg_hbm, rgrad_ref,
    box, inz, outx, inx, ubox, uinz, uoutx, uinx, raw, yb, wu, wd, hid, dh, act, hc,
    lg, gate_s, slope_s, slope3, sa, ra, sb, rb, ua, ub, gsu, gsd,
    p1, p1t, p2, p2t, plc, pltx, pltc, rrow, vt, vy, vx, vz,
    wsem, zs, zr, xs, xr, ys, yr, as_, ar, bs, br, uzs, uzr, uxs, uxr, rs, rr,
    uas, uar, ubs, ubr, gsem, vts, vtr, vys, vyr, vxs, vxr, vzs, vzr, free,
):
    me = lax.axis_index("expert")
    t = lax.axis_index("tensor")
    z, q = me // NQ, me % NQ
    lo, hi = pl.ds(0, SLOTS), pl.ds(SLOTS, SLOTS)
    rlo, rhi = pl.ds(0, ROWS), pl.ds(ROWS, ROWS)
    ZD, XD, YD = range(1, NZ), range(1, NQ), range(1, NT)

    def zpeer(d):
        return (((z + d) % NZ) * NQ + q, t)

    def xpeer(d):
        return (z * NQ + (q + d) % NQ, t)

    def ypeer(d):
        return (me, (t + d) % NT)

    def remote(src, dst, ssem, rsem, peer):
        return pltpu.make_async_remote_copy(
            src_ref=src, dst_ref=dst, send_sem=ssem, recv_sem=rsem,
            device_id=peer, device_id_type=MESH,
        )

    def piece(s):
        return pl.ds(pl.multiple_of(s * C, C), C)

    def normal(n):
        return n + (n + 1) // 2

    def special(v):
        return 1 + 3 * v

    def weights(s):
        return (
            pltpu.make_async_copy(up_hbm.at[0, piece(s), :], wu.at[s], wsem.at[0, s]),
            pltpu.make_async_copy(down_hbm.at[0, :, piece(s)], wd.at[s], wsem.at[1, s]),
        )

    def zcopy(n, d):
        return remote(box.at[n, (z + d) % NZ], inz.at[n, z], zs.at[n, d], zr.at[n, d], zpeer(d))

    def zland(n, d):
        return remote(box.at[n, z], inz.at[n, (z + NZ - d) % NZ], zs.at[n, d], zr.at[n, d], zpeer(d))

    def xcopy(n, d):
        return remote(outx.at[n, (q + d) % NQ], inx.at[n, q], xs.at[n, d], xr.at[n, d], xpeer(d))

    def xland(n, d):
        return remote(outx.at[n, q], inx.at[n, (q + NQ - d) % NQ], xs.at[n, d], xr.at[n, d], xpeer(d))

    def uzcopy(u, d):
        return remote(ubox.at[u, (z + d) % NZ], uinz.at[u, z], uzs.at[u, d], uzr.at[u, d], zpeer(d))

    def uzland(u, d):
        return remote(ubox.at[u, z], uinz.at[u, (z + NZ - d) % NZ], uzs.at[u, d], uzr.at[u, d], zpeer(d))

    def uxcopy(u, d):
        return remote(uoutx.at[u, (q + d) % NQ], uinx.at[u, q], uxs.at[u, d], uxr.at[u, d], xpeer(d))

    def uxland(u, d):
        return remote(uoutx.at[u, q], uinx.at[u, (q + NQ - d) % NQ], uxs.at[u, d], uxr.at[u, d], xpeer(d))

    SIDE = (1, NT - 1, 1, NT - 1)

    def ycopy(n, i):
        b = yb.at[normal(n)]
        src = (b.at[0], b.at[0], b.at[3, lo], b.at[1, hi])[i]
        dst = (b.at[3], b.at[1], b.at[2, lo], b.at[2, hi])[i]
        return remote(src, dst, ys.at[n, i], yr.at[n, i], ypeer(SIDE[i]))

    def rcopy(v, i):
        b = raw.at[v]
        src = (b.at[0], b.at[0], b.at[3, rlo], b.at[1, rhi])[i]
        dst = (b.at[3], b.at[1], b.at[2, rlo], b.at[2, rhi])[i]
        return remote(src, dst, rs.at[v, i], rr.at[v, i], ypeer(SIDE[i]))

    def acopy(n, i):
        return remote(sa.at[n, i], ra.at[n, i], as_.at[n, i], ar.at[n, i], ypeer(SIDE[i]))

    def bcopy(n, i):
        return remote(sb.at[n, i], rb.at[n, i], bs.at[n, i], br.at[n, i], ypeer(SIDE[i]))

    def uacopy(v, i):
        src = raw.at[v, 2, (rlo, rhi)[i]]
        return remote(src, ua.at[v, i], uas.at[v, i], uar.at[v, i], ypeer(SIDE[i]))

    def ubcopy(v, i):
        return remote(raw.at[v, SIDE[i]], ub.at[v, i], ubs.at[v, i], ubr.at[v, i], ypeer(SIDE[i]))

    def vtcopy(d):
        return remote(vt.at[0], vt.at[NT - d], vts.at[d], vtr.at[d], ypeer(d))

    def vycopy(d):
        return remote(vy.at[t], vy.at[t], vys.at[d], vyr.at[d], ypeer(d))

    def vyland(d):
        dst = vy.at[(t + NT - d) % NT]
        return remote(dst, dst, vys.at[d], vyr.at[d], ypeer(d))

    def vxcopy(d):
        return remote(vx.at[q], vx.at[q], vxs.at[d], vxr.at[d], xpeer(d))

    def vxland(d):
        dst = vx.at[(q + NQ - d) % NQ]
        return remote(dst, dst, vxs.at[d], vxr.at[d], xpeer(d))

    def vzcopy(d):
        return remote(vx, vz.at[z], vzs.at[d], vzr.at[d], zpeer(d))

    def vzland(d):
        return remote(vx, vz.at[(z + NZ - d) % NZ], vzs.at[d], vzr.at[d], zpeer(d))

    for s in range(NC):
        for copy in weights(s):
            copy.start()

    barrier = pltpu.get_barrier_semaphore()
    for peers, ds in ((zpeer, ZD), (xpeer, XD), (ypeer, YD)):
        for d in ds:
            pl.semaphore_signal(barrier, inc=1, device_id=peers(d), device_id_type=MESH)

    diag = iota((ROWS, ROWS), 0) == iota((ROWS, ROWS), 1)

    def turned(line):
        return jnp.sum(jnp.where(diag, line, 0.0), axis=1, keepdims=True)

    def both_of(s):
        cot = (gate_s[:, :1] * og_ref[:, piece(s)].astype(F32)).astype(BF16)
        return jnp.concatenate([tok_ref[:, piece(s)], cot], axis=0)

    def place(o):
        line = vt[o]
        slot = iota((BOTH, ROWS), 0)
        plc[o, :, :ROWS] = onehot(slot == line)
        plc[o, :, ROWS:] = onehot(slot == line + MOST)
        column = turned(line)
        lane = iota((ROWS, BOTH), 1)
        pltx[o] = onehot(lane == column)
        pltc[o] = onehot(lane == column + MOST)

    ids = turned(ids_ref[...].astype(F32))
    chosen = ids == iota((ROWS, EXPERTS), 1)
    logits = dot(tok_ref[...], router_ref[...], NTD)
    gate = jax.nn.sigmoid(jnp.sum(jnp.where(chosen, logits, 0.0), axis=1, keepdims=True))
    gate_s[...] = jnp.broadcast_to(gate, (ROWS, 128))
    raw[0, 0] = both_of(special(0))
    pl.semaphore_wait(barrier, NZ + NQ + NT - 3)
    rcopy(0, 0).start()
    rcopy(0, 1).start()

    tri = onehot(iota((ROWS, ROWS), 0) > iota((ROWS, ROWS), 1))
    counts = dot(tri, onehot(chosen))
    rank = jnp.sum(jnp.where(chosen, counts, 0.0), axis=1, keepdims=True)
    live = lax.broadcasted_iota(I32, (ROWS, 1), 0) < live_ref[0]
    target = jnp.where(live, ids * (2.0 * MOST) + rank, -1000.0)
    vt[0] = jnp.sum(jnp.where(diag, target, 0.0), axis=0, keepdims=True)
    raw[1, 0] = both_of(special(1))
    for d in YD:
        vtcopy(d).start()
    rcopy(1, 0).start()
    rcopy(1, 1).start()
    place(0)

    @pl.loop(0, NN)
    def _(n):
        box[n] = dot(plc[0], both_of(normal(n))).astype(BF16).reshape(NZ, ZR, C)
        for d in ZD:
            zcopy(n, d).start()
        inz[n, z] = box[n, z]

    column, line = iota((BOTH, 1), 0), iota((1, BOTH), 1)
    across, down = iota((BOTH, BOTH), 1), iota((BOTH, BOTH), 0)
    p1[...] = onehot(source_1(column) == across)
    p1t[...] = onehot(source_1(line) == down)
    p2[...] = onehot(source_2(column) == across)
    p2t[...] = onehot(source_2(line) == down)
    for d in YD:
        vtcopy(d).wait_recv()
        place(NT - d)

    hid[...] = jnp.zeros_like(hid)
    dh[...] = jnp.zeros_like(dh)
    lg[...] = jnp.zeros_like(lg)
    own = onehot(iota((8, EXPERTS), 1) == me.astype(F32))

    @pl.loop(0, NC)
    def _(s):
        rrow[s] = dot(own, router_ref[:, piece(s)])

    def rows_of(s):
        return yb[s, :, :SLOTS, :].reshape(NT * SLOTS, C)

    def cots_of(s):
        return yb[s, :, SLOTS:, :].reshape(NT * SLOTS, C)

    def order(perm, rows, shape):
        return dot(perm[...], rows.reshape(BOTH, C)).astype(BF16).reshape(shape)

    def out_z(n):
        for d in ZD:
            zland(n, d).wait_recv()
        outx[n] = order(p1, inz[n], (NQ, XR, C))
        for d in XD:
            xcopy(n, d).start()
        inx[n, q] = outx[n, q]

    def out_x(n):
        for d in XD:
            xland(n, d).wait_recv()
        yb[normal(n), 0] = order(p2, inx[n], (BOTH, C))
        ycopy(n, 0).start()
        ycopy(n, 1).start()

    def out_y(n):
        ycopy(n, 0).wait_recv()
        ycopy(n, 2).start()
        ycopy(n, 1).wait_recv()
        ycopy(n, 3).start()

    def raw_on(v):
        rcopy(v, 0).wait_recv()
        rcopy(v, 2).start()
        rcopy(v, 1).wait_recv()
        rcopy(v, 3).start()

    def unit_box(u):
        v, r = u // NT, u % NT

        @pl.when(r == 3)
        def _():
            rcopy(v, 2).wait_recv()
            rcopy(v, 3).wait_recv()

        o = gray(r)
        ubox[u] = dot(plc[o], raw[v, o]).astype(BF16).reshape(NZ, ZR, C)
        for d in ZD:
            uzcopy(u, d).start()
        uinz[u, z] = ubox[u, z]

    def unit_z(u):
        for d in ZD:
            uzland(u, d).wait_recv()
        uoutx[u] = order(p1, uinz[u], (NQ, XR, C))
        for d in XD:
            uxcopy(u, d).start()
        uinx[u, q] = uoutx[u, q]

    def unit_x(u):
        for d in XD:
            uxland(u, d).wait_recv()
        yb[special(u // NT), gray(u % NT)] = order(p2, uinx[u], (BOTH, C))

    def release(_):
        for peers, ds in ((zpeer, ZD), (xpeer, XD)):
            for d in ds:
                pl.semaphore_signal(free, inc=1, device_id=peers(d), device_id_type=MESH)

    HALF = 2 * SLOTS

    def work(s, h):
        r = pl.ds(h * HALF, HALF)
        rows = yb[s, 2 * h : 2 * h + 2, :SLOTS, :].reshape(HALF, C)
        cots = yb[s, 2 * h : 2 * h + 2, SLOTS:, :].reshape(HALF, C)
        lg[r, :] += dot(rows, router_ref[:, piece(s)], NTD)

        @pl.loop(0, H // N)
        def _(n):
            part = pl.ds(pl.multiple_of(n * N, N), N)
            hid[r, part] += dot(rows, wu[s, :, part])
            dh[r, part] += dot(cots, wd[s, part, :], NTD)

    def near(s):
        for copy in weights(s):
            copy.wait()
        work(s, 0)

    def away(s):
        for n in range(NN):

            @pl.when(s == normal(n))
            def _():
                ycopy(n, 2).wait_recv()
                ycopy(n, 3).wait_recv()

        work(s, 1)

    BR = 32

    def middle(o):
        @pl.loop(0, SLOTS // BR)
        def _(b):
            silu_rows(pl.ds(pl.multiple_of(o * SLOTS + b * BR, BR), BR))

    def silu_rows(r):
        v, back = hid[r, :], dh[r, :]
        sig = 1.0 / (1.0 + jnp.exp(-v))
        a = (v * sig).astype(BF16)
        act[r, :] = a
        hc[r, :] = (back * (sig * (1.0 + v * (1.0 - sig)))).astype(BF16)
        part = jnp.sum(a.astype(F32) * back, axis=1, keepdims=True)
        mine = iota((BR, EXPERTS), 1) == me.astype(F32)
        logit = jnp.sum(jnp.where(mine, lg[r, :], 0.0), axis=1, keepdims=True)
        slope = part * (1.0 - 1.0 / (1.0 + jnp.exp(-logit)))
        slope_s[r, :] = jnp.broadcast_to(slope, (BR, 128))
        s1 = slope.astype(BF16).astype(F32)
        s2 = (slope - s1).astype(BF16).astype(F32)
        s3 = slope - s1 - s2
        k = iota((BR, 128), 1)
        slope3[r, :] = jnp.where(
            k == 0.0, s1, jnp.where(k == 1.0, s2, jnp.where(k == 2.0, s3, 0.0))
        ).astype(BF16)

    @pl.loop(0, OUT_STEPS)
    def _(i):
        for task in (out_z, raw_on, unit_box, out_x, unit_z, unit_x, release, out_y, near, away, middle):
            at(i, OUT[task.__name__], task)

    def partial(s, b):
        r = pl.ds(pl.multiple_of(b * SLOTS, SLOTS), SLOTS)
        value = dot(act[r, :], wd[s])
        grad = dot(hc[r, :], wu[s], NTD) + slope_s[r, :1] * rrow[s, :1, :]
        return value, grad

    def back_far(n):
        value, grad = partial(normal(n), 2)
        sa[n, 0] = value.astype(BF16)
        sa[n, 1] = grad.astype(BF16)
        acopy(n, 0).start()
        acopy(n, 1).start()

    def back_near(n):
        value, grad = partial(normal(n), 1)
        acopy(n, 0).wait_recv()
        sb[n, 0, lo] = (value + ra[n, 0].astype(F32)).astype(BF16)
        sb[n, 0, hi] = grad.astype(BF16)
        bcopy(n, 0).start()
        value, grad = partial(normal(n), 3)
        acopy(n, 1).wait_recv()
        sb[n, 1, lo] = value.astype(BF16)
        sb[n, 1, hi] = (grad + ra[n, 1].astype(F32)).astype(BF16)
        bcopy(n, 1).start()

    def back_own(n):
        value, grad = partial(normal(n), 0)
        bcopy(n, 0).wait_recv()
        bcopy(n, 1).wait_recv()
        value = value + rb[n, 0, :SLOTS, :].astype(F32) + rb[n, 1, :SLOTS, :].astype(F32)
        grad = grad + rb[n, 0, SLOTS:, :].astype(F32) + rb[n, 1, SLOTS:, :].astype(F32)
        both = jnp.concatenate([value, grad], axis=0).astype(BF16)
        for d in XD:
            xcopy(n, d).wait_send()
        outx[n] = order(p2t, both, (NQ, XR, C))
        for d in XD:
            xcopy(n, d).start()
        inx[n, q] = outx[n, q]

    def back_x(n):
        for d in XD:
            xland(n, d).wait_recv()
        for d in ZD:
            zcopy(n, d).wait_send()
        box[n] = order(p1t, inx[n], (NZ, ZR, C))
        for d in ZD:
            zcopy(n, d).start()
        inz[n, z] = box[n, z]

    def back_z(n):
        for d in ZD:
            zland(n, d).wait_recv()
        got = inz[n].reshape(BOTH, C)
        cols = piece(normal(n))
        mixed_ref[:, cols] = (gate_s[:, :1] * dot(pltx[0], got)).astype(BF16)
        tgrad_ref[:, cols] = dot(pltc[0], got).astype(BF16)

    def unit_back(u):
        value, grad = partial(special(u // NT), gray(3 - u % NT))
        both = jnp.concatenate([value, grad], axis=0).astype(BF16)
        for d in XD:
            uxcopy(u, d).wait_send()
        uoutx[u] = order(p2t, both, (NQ, XR, C))

        @pl.when(u == 0)
        def _():
            pl.semaphore_wait(free, NZ + NQ - 2)

        for d in XD:
            uxcopy(u, d).start()
        uinx[u, q] = uoutx[u, q]

    def unit_back_x(u):
        for d in XD:
            uxland(u, d).wait_recv()
        for d in ZD:
            uzcopy(u, d).wait_send()
        ubox[u] = order(p1t, uinx[u], (NZ, ZR, C))
        for d in ZD:
            uzcopy(u, d).start()
        uinz[u, z] = ubox[u, z]

    def unit_back_z(u):
        for d in ZD:
            uzland(u, d).wait_recv()
        v, r = u // NT, u % NT

        @pl.when(r == 0)
        def _():
            for i in range(4):
                rcopy(v, i).wait_send()

        o = gray(3 - r)
        got = uinz[u].reshape(BOTH, C)
        raw[v, o, rlo] = dot(pltx[o], got).astype(BF16)
        raw[v, o, rhi] = dot(pltc[o], got).astype(BF16)

        @pl.when(r == 0)
        def _():
            uacopy(v, 0).start()
            uacopy(v, 1).start()

        @pl.when(r == 1)
        def _():
            uacopy(v, 1).wait_recv()
            raw[v, 3, rhi] = (raw[v, 3, rhi].astype(F32) + ua[v, 1].astype(F32)).astype(BF16)
            ubcopy(v, 1).start()

        @pl.when(r == 2)
        def _():
            uacopy(v, 0).wait_recv()
            raw[v, 1, rlo] = (raw[v, 1, rlo].astype(F32) + ua[v, 0].astype(F32)).astype(BF16)
            ubcopy(v, 0).start()

    def unit_sum(v):
        ubcopy(v, 0).wait_recv()
        ubcopy(v, 1).wait_recv()
        got = raw[v, 0].astype(F32) + ub[v, 0].astype(F32) + ub[v, 1].astype(F32)
        cols = piece(special(v))
        value = got[:ROWS].astype(BF16).astype(F32)
        mixed_ref[:, cols] = (gate_s[:, :1] * value).astype(BF16)
        tgrad_ref[:, cols] = got[ROWS:].astype(BF16)

    def grads_out(s, n):
        part = pl.ds(pl.multiple_of(n * N, N), N)
        k = n % 2
        return (
            pltpu.make_async_copy(gsu.at[k], upg_hbm.at[0, piece(s), part], gsem.at[0, k]),
            pltpu.make_async_copy(gsd.at[k], downg_hbm.at[0, part, piece(s)], gsem.at[1, k]),
        )

    def grads(s):
        @pl.loop(0, H // N)
        def _(n):
            @pl.when((s > 0) | (n >= 2))
            def _():
                for copy in grads_out(s, n):
                    copy.wait()

            part = pl.ds(pl.multiple_of(n * N, N), N)
            gsd[n % 2] = dot(act[:, part], cots_of(s), TND).astype(BF16)
            gsu[n % 2] = dot(rows_of(s), hc[:, part], TND).astype(BF16)
            for copy in grads_out(s, n):
                copy.start()

    def vector_0(_):
        @pl.loop(0, NC)
        def _(s):
            three = dot(slope3[...], rows_of(s), TND)
            vy[t, :, piece(s)] = jnp.sum(three, axis=0, keepdims=True)

        for d in YD:
            vycopy(d).start()

    def vector_1(_):
        for d in YD:
            vyland(d).wait_recv()
        vx[q] = (vy[0] + vy[1]) + (vy[2] + vy[3])
        for d in XD:
            vxcopy(d).start()

    def vector_2(_):
        for d in XD:
            vxland(d).wait_recv()
        for d in ZD:
            vzcopy(d).start()
        vz[z] = vx[...]

    @pl.loop(0, BACK_STEPS)
    def _(i):
        for task in (
            back_far, unit_back, vector_0, back_near, unit_back_x, unit_back_z, grads, back_own,
            vector_1, vector_2, back_x, unit_sum, back_z,
        ):
            at(i, BACK[task.__name__], task)

    for d in ZD:
        vzland(d).wait_recv()
    rgrad_ref[...] = vz[...].reshape(EXPERTS, 1, C * NC)
    for d in YD:
        vtcopy(d).wait_send()
        vycopy(d).wait_send()
    for d in XD:
        vxcopy(d).wait_send()
    for d in ZD:
        vzcopy(d).wait_send()

    @pl.loop(0, NN)
    def _(n):
        for i in range(4):
            ycopy(n, i).wait_send()
        for i in range(2):
            acopy(n, i).wait_send()
            bcopy(n, i).wait_send()
        for d in XD:
            xcopy(n, d).wait_send()
        for d in ZD:
            zcopy(n, d).wait_send()

    @pl.loop(0, NU)
    def _(u):
        for d in XD:
            uxcopy(u, d).wait_send()
        for d in ZD:
            uzcopy(u, d).wait_send()

    @pl.loop(0, NS)
    def _(v):
        for i in range(2):
            uacopy(v, i).wait_send()
            ubcopy(v, i).wait_send()

    for n in range(2):
        for copy in grads_out(NC - 1, n):
            copy.wait()


def per_device(tokens, expert_ids, live_counts, router, up_weight, down_weight, out_grad):
    width = tokens.shape[1]
    assert tokens.shape == (ROWS, C * NC) and router.shape[1] == EXPERTS
    assert up_weight.shape == (1, C * NC, H)
    vmem = pl.BlockSpec(memory_space=pltpu.VMEM)
    smem = pl.BlockSpec(memory_space=pltpu.SMEM)
    hbm = pl.BlockSpec(memory_space=pl.ANY)
    every = NT * SLOTS
    V, DMA = pltpu.VMEM, pltpu.SemaphoreType.DMA
    scratch = [
        V((NN, NZ, ZR, C), BF16),
        V((NN, NZ, ZR, C), BF16),
        V((NN, NQ, XR, C), BF16),
        V((NN, NQ, XR, C), BF16),
        V((NU, NZ, ZR, C), BF16),
        V((NU, NZ, ZR, C), BF16),
        V((NU, NQ, XR, C), BF16),
        V((NU, NQ, XR, C), BF16),
        V((NS, NT, 2 * ROWS, C), BF16),
        V((NC, NT, BOTH, C), BF16),
        V((NC, C, H), BF16),
        V((NC, H, C), BF16),
        V((every, H), F32),
        V((every, H), F32),
        V((every, H), BF16),
        V((every, H), BF16),
        V((every, EXPERTS), F32),
        V((ROWS, 128), F32),
        V((every, 128), F32),
        V((every, 128), BF16),
        V((NN, 2, SLOTS, C), BF16),
        V((NN, 2, SLOTS, C), BF16),
        V((NN, 2, BOTH, C), BF16),
        V((NN, 2, BOTH, C), BF16),
        V((NS, 2, ROWS, C), BF16),
        V((NS, 2, 2 * ROWS, C), BF16),
        V((2, C, N), BF16),
        V((2, N, C), BF16),
        V((BOTH, BOTH), BF16),
        V((BOTH, BOTH), BF16),
        V((BOTH, BOTH), BF16),
        V((BOTH, BOTH), BF16),
        V((NT, BOTH, 2 * ROWS), BF16),
        V((NT, ROWS, BOTH), BF16),
        V((NT, ROWS, BOTH), BF16),
        V((NC, 8, C), F32),
        V((NT, 1, ROWS), F32),
        V((NT, 1, width), F32),
        V((NQ, 1, width), F32),
        V((NZ, NQ, 1, width), F32),
        DMA((2, NC)),
        DMA((NN, NZ)), DMA((NN, NZ)), DMA((NN, NQ)), DMA((NN, NQ)), DMA((NN, 4)), DMA((NN, 4)),
        DMA((NN, 2)), DMA((NN, 2)), DMA((NN, 2)), DMA((NN, 2)),
        DMA((NU, NZ)), DMA((NU, NZ)), DMA((NU, NQ)), DMA((NU, NQ)), DMA((NS, 4)), DMA((NS, 4)),
        DMA((NS, 2)), DMA((NS, 2)), DMA((NS, 2)), DMA((NS, 2)),
        DMA((2, 2)),
        DMA((NT,)), DMA((NT,)), DMA((NT,)), DMA((NT,)),
        DMA((NQ,)), DMA((NQ,)), DMA((NZ,)), DMA((NZ,)),
        pltpu.SemaphoreType.REGULAR,
    ]
    S = jax.ShapeDtypeStruct
    mixed, tgrad, upg, downg, rgrad = pl.pallas_call(
        kernel,
        out_shape=(
            S((ROWS, width), BF16),
            S((ROWS, width), BF16),
            S((1, width, H), BF16),
            S((1, H, width), BF16),
            S((EXPERTS, 1, width), F32),
        ),
        in_specs=[vmem, smem, vmem, vmem, vmem, hbm, hbm],
        out_specs=(vmem, vmem, hbm, hbm, vmem),
        scratch_shapes=scratch,
        compiler_params=pltpu.CompilerParams(
            collective_id=0, has_side_effects=True, vmem_limit_bytes=67043328
        ),
    )(
        expert_ids.reshape(1, ROWS), live_counts, router.T, tokens, out_grad, up_weight, down_weight
    )
    return (mixed, tgrad, upg, downg, rgrad.reshape(EXPERTS, width).T)


def solution(mesh):
    rows = P(("expert", "tensor"), None)
    in_specs = (
        rows,
        rows,
        P(("expert", "tensor")),
        P(),
        P("expert", None, "tensor"),
        P("expert", "tensor", None),
        rows,
    )
    out_specs = (rows, rows, P("expert", None, "tensor"), P("expert", "tensor", None), P())
    return jax.shard_map(
        per_device, mesh=mesh, in_specs=in_specs, out_specs=out_specs, check_vma=False
    )
```

```python
import jax
import jax.numpy as jnp
from jax import lax
from jax.experimental import pallas as pl
from jax.experimental.pallas import tpu as pltpu
from jax.sharding import PartitionSpec as P

F32, BF16, I32 = jnp.float32, jnp.bfloat16, jnp.int32
MESH = pl.DeviceIdType.MESH

NZ, NQ, NT = 4, 8, 4
EXPERTS = NZ * NQ
ROWS, MOST = 128, 6
SLOTS = EXPERTS * MOST
BOTH = 2 * SLOTS
C, NC = 512, 5
NN, NS = 3, 2
NU = NT * NS
ZR, XR = NQ * 2 * MOST, 2 * NZ * MOST
H = 1024
N = 256


OUT_STEPS = 28
OUT = dict(
    out_z=(2, 4, 5,),
    raw_on=(1, 4,),
    unit_box=(0, 2, 3, 5, 6, 7, 8, 9,),
    out_x=(4, 8, 10,),
    unit_z=(9, 10, 11, 13, 15, 17, 18, 20,),
    unit_x=(11, 12, 14, 16, 18, 19, 21, 25,),
    release=(25,),
    out_y=(10, 13, 17,),
    near=(10, 14, 15, 17, 21,),
    away=(18, 19, 20, 26, 27,),
    middle=(21, 22, 25, 27,),
    early=(22, 23, 24,),
)
BACK_STEPS = 25
BACK = dict(
    unit_back=(0, 1, 2, 3, 4, 5, 6, 7,),
    back_far=(7, 8, 9,),
    vector_0=(10,),
    grads=(10, 11, 12, 13, 16,),
    vector_1=(12,),
    unit_back_x=(6, 9, 10, 11, 12, 13, 16, 18,),
    unit_back_z=(10, 13, 14, 15, 16, 20, 21, 22,),
    back_near=(10, 11, 12,),
    back_own=(16, 17, 18,),
    vector_2=(16,),
    back_x=(18, 19, 22,),
    unit_sum=(19, 24,),
    back_z=(19, 22, 23,),
)


def dot(a, b, dims=((1,), (0,))):
    return lax.dot_general(a, b, (dims, ((), ())), preferred_element_type=F32)


NTD = ((1,), (1,))
TND = ((0,), (0,))


def iota(shape, axis):
    return lax.broadcasted_iota(I32, shape, axis).astype(F32)


def turn(r):
    return r + 1 - 3 * (r // 2) + 2 * (r // 3)


def at(i, steps, task):
    here, k = i == steps[0], 0
    for step in steps[1:]:
        here = here | (i == step)
        k = k + (i + 64 - step) // 64

    @pl.when(here)
    def _():
        task(k)


def onehot(mask):
    return jnp.where(mask, 1.0, 0.0).astype(BF16)


def div(a, b):
    return jnp.floor((a + 0.5) * (1.0 / b))


def source_1(o):
    q = div(o, 2 * NZ * MOST)
    r = o - q * (2 * NZ * MOST)
    a = div(r, NZ * MOST)
    r = r - a * (NZ * MOST)
    z = div(r, MOST)
    k = r - z * MOST
    return z * (NQ * 2 * MOST) + q * (2 * MOST) + a * MOST + k


def source_2(o):
    a = div(o, SLOTS)
    r = o - a * SLOTS
    q = div(r, NZ * MOST)
    m = r - q * (NZ * MOST)
    return q * (2 * NZ * MOST) + a * (NZ * MOST) + m


def kernel(
    ids_ref, live_ref, router_ref, tok_ref, og_ref, up_hbm, down_hbm,
    mixed_ref, tgrad_ref, upg_hbm, downg_hbm, rgrad_ref,
    box, inz, outx, inx, ubox, uinz, uoutx, uinx, raw, yb, wu, wd, hid, dh, act, hc,
    lg, gate_s, slope_s, slope3, sa, ra, sb, rb, ua, ub, gsu, gsd,
    p1, p1t, p2, p2t, plc, pltx, pltc, rrow, vt, vy, vx, vz,
    wsem, zs, zr, xs, xr, ys, yr, as_, ar, bs, br, uzs, uzr, uxs, uxr, rs, rr,
    uas, uar, ubs, ubr, gsem, vts, vtr, vys, vyr, vxs, vxr, vzs, vzr, free,
):
    me = lax.axis_index("expert")
    t = lax.axis_index("tensor")
    z, q = me // NQ, me % NQ
    lo, hi = pl.ds(0, SLOTS), pl.ds(SLOTS, SLOTS)
    rlo, rhi = pl.ds(0, ROWS), pl.ds(ROWS, ROWS)
    ZD, XD, YD = range(1, NZ), range(1, NQ), range(1, NT)

    def zpeer(d):
        return (((z + d) % NZ) * NQ + q, t)

    def xpeer(d):
        return (z * NQ + (q + d) % NQ, t)

    def ypeer(d):
        return (me, (t + d) % NT)

    def remote(src, dst, ssem, rsem, peer):
        return pltpu.make_async_remote_copy(
            src_ref=src, dst_ref=dst, send_sem=ssem, recv_sem=rsem,
            device_id=peer, device_id_type=MESH,
        )

    def piece(s):
        return pl.ds(pl.multiple_of(s * C, C), C)

    def normal(n):
        return n + (n + 1) // 2

    def special(v):
        return 1 + 3 * v

    def weights(s):
        return (
            pltpu.make_async_copy(up_hbm.at[0, piece(s), :], wu.at[s], wsem.at[0, s]),
            pltpu.make_async_copy(down_hbm.at[0, :, piece(s)], wd.at[s], wsem.at[1, s]),
        )

    def zcopy(n, d):
        return remote(box.at[n, (z + d) % NZ], inz.at[n, z], zs.at[n, d], zr.at[n, d], zpeer(d))

    def zland(n, d):
        return remote(box.at[n, z], inz.at[n, (z + NZ - d) % NZ], zs.at[n, d], zr.at[n, d], zpeer(d))

    def xcopy(n, d):
        return remote(outx.at[n, (q + d) % NQ], inx.at[n, q], xs.at[n, d], xr.at[n, d], xpeer(d))

    def xland(n, d):
        return remote(outx.at[n, q], inx.at[n, (q + NQ - d) % NQ], xs.at[n, d], xr.at[n, d], xpeer(d))

    def uzcopy(u, d):
        return remote(ubox.at[u, (z + d) % NZ], uinz.at[u, z], uzs.at[u, d], uzr.at[u, d], zpeer(d))

    def uzland(u, d):
        return remote(ubox.at[u, z], uinz.at[u, (z + NZ - d) % NZ], uzs.at[u, d], uzr.at[u, d], zpeer(d))

    def uxcopy(u, d):
        return remote(uoutx.at[u, (q + d) % NQ], uinx.at[u, q], uxs.at[u, d], uxr.at[u, d], xpeer(d))

    def uxland(u, d):
        return remote(uoutx.at[u, q], uinx.at[u, (q + NQ - d) % NQ], uxs.at[u, d], uxr.at[u, d], xpeer(d))

    SIDE = (1, NT - 1, 1, NT - 1)

    def ycopy(n, i):
        b = yb.at[normal(n)]
        src = (b.at[1], b.at[1], b.at[0, lo], b.at[2, hi])[i]
        dst = (b.at[0], b.at[2], b.at[3, lo], b.at[3, hi])[i]
        return remote(src, dst, ys.at[n, i], yr.at[n, i], ypeer(SIDE[i]))

    def rcopy(v, i):
        b = raw.at[v]
        src = (b.at[1], b.at[1], b.at[0, rlo], b.at[2, rhi])[i]
        dst = (b.at[0], b.at[2], b.at[3, rlo], b.at[3, rhi])[i]
        return remote(src, dst, rs.at[v, i], rr.at[v, i], ypeer(SIDE[i]))

    def acopy(n, i):
        return remote(sa.at[n, i], ra.at[n, i], as_.at[n, i], ar.at[n, i], ypeer(SIDE[i]))

    def bcopy(n, i):
        k, half = i % 2, (lo, hi, hi, lo)[i]
        return remote(sb.at[n, k, half], rb.at[n, k, half], bs.at[n, i], br.at[n, i], ypeer(SIDE[i]))

    def uacopy(v, i):
        src = raw.at[v, 3, (rlo, rhi)[i]]
        return remote(src, ua.at[v, i], uas.at[v, i], uar.at[v, i], ypeer(SIDE[i]))

    def ubcopy(v, i):
        return remote(raw.at[v, (2, 0)[i]], ub.at[v, i], ubs.at[v, i], ubr.at[v, i], ypeer(SIDE[i]))

    def vtcopy(d):
        return remote(vt.at[1], vt.at[(1, 0, 3, 2)[d]], vts.at[d], vtr.at[d], ypeer(d))

    def vycopy(d):
        return remote(vy.at[t], vy.at[t], vys.at[d], vyr.at[d], ypeer(d))

    def vyland(d):
        dst = vy.at[(t + NT - d) % NT]
        return remote(dst, dst, vys.at[d], vyr.at[d], ypeer(d))

    def vxcopy(d):
        return remote(vx.at[q], vx.at[q], vxs.at[d], vxr.at[d], xpeer(d))

    def vxland(d):
        dst = vx.at[(q + NQ - d) % NQ]
        return remote(dst, dst, vxs.at[d], vxr.at[d], xpeer(d))

    def vzcopy(d):
        return remote(vx, vz.at[z], vzs.at[d], vzr.at[d], zpeer(d))

    def vzland(d):
        return remote(vx, vz.at[(z + NZ - d) % NZ], vzs.at[d], vzr.at[d], zpeer(d))

    for s in range(NC):
        for copy in weights(s):
            copy.start()

    barrier = pltpu.get_barrier_semaphore()
    for peers, ds in ((zpeer, ZD), (xpeer, XD), (ypeer, YD)):
        for d in ds:
            pl.semaphore_signal(barrier, inc=1, device_id=peers(d), device_id_type=MESH)

    diag = iota((ROWS, ROWS), 0) == iota((ROWS, ROWS), 1)

    def turned(line):
        return jnp.sum(jnp.where(diag, line, 0.0), axis=1, keepdims=True)

    def both_of(s):
        cot = (gate_s[:, :1] * og_ref[:, piece(s)].astype(F32)).astype(BF16)
        return jnp.concatenate([tok_ref[:, piece(s)], cot], axis=0)

    def place(o):
        line = vt[o]
        slot = iota((BOTH, ROWS), 0)
        plc[o, :, :ROWS] = onehot(slot == line)
        plc[o, :, ROWS:] = onehot(slot == line + MOST)
        column = turned(line)
        lane = iota((ROWS, BOTH), 1)
        pltx[o] = onehot(lane == column)
        pltc[o] = onehot(lane == column + MOST)

    ids = turned(ids_ref[...].astype(F32))
    chosen = ids == iota((ROWS, EXPERTS), 1)
    logits = dot(tok_ref[...], router_ref[...], NTD)
    gate = jax.nn.sigmoid(jnp.sum(jnp.where(chosen, logits, 0.0), axis=1, keepdims=True))
    gate_s[...] = jnp.broadcast_to(gate, (ROWS, 128))
    raw[0, 1] = both_of(special(0))
    pl.semaphore_wait(barrier, NZ + NQ + NT - 3)
    rcopy(0, 0).start()
    rcopy(0, 1).start()

    tri = onehot(iota((ROWS, ROWS), 0) > iota((ROWS, ROWS), 1))
    counts = dot(tri, onehot(chosen))
    rank = jnp.sum(jnp.where(chosen, counts, 0.0), axis=1, keepdims=True)
    live = lax.broadcasted_iota(I32, (ROWS, 1), 0) < live_ref[0]
    target = jnp.where(live, ids * (2.0 * MOST) + rank, -1000.0)
    vt[1] = jnp.sum(jnp.where(diag, target, 0.0), axis=0, keepdims=True)
    raw[1, 1] = both_of(special(1))
    for d in YD:
        vtcopy(d).start()
    rcopy(1, 0).start()
    rcopy(1, 1).start()
    place(1)

    @pl.loop(0, NN)
    def _(n):
        box[n] = dot(plc[1], both_of(normal(n))).astype(BF16).reshape(NZ, ZR, C)
        for d in ZD:
            zcopy(n, d).start()
        inz[n, z] = box[n, z]

    column, line = iota((BOTH, 1), 0), iota((1, BOTH), 1)
    across, down = iota((BOTH, BOTH), 1), iota((BOTH, BOTH), 0)
    p1[...] = onehot(source_1(column) == across)
    p1t[...] = onehot(source_1(line) == down)
    p2[...] = onehot(source_2(column) == across)
    p2t[...] = onehot(source_2(line) == down)
    for d in YD:
        vtcopy(d).wait_recv()
        place((1, 0, 3, 2)[d])

    hid[...] = jnp.zeros_like(hid)
    dh[...] = jnp.zeros_like(dh)
    lg[...] = jnp.zeros_like(lg)
    own = onehot(iota((8, EXPERTS), 1) == me.astype(F32))

    @pl.loop(0, NC)
    def _(s):
        rrow[s] = dot(own, router_ref[:, piece(s)])

    def rows_of(s):
        return yb[s, :, :SLOTS, :].reshape(NT * SLOTS, C)

    def cots_of(s):
        return yb[s, :, SLOTS:, :].reshape(NT * SLOTS, C)

    def order(perm, rows, shape):
        return dot(perm[...], rows.reshape(BOTH, C)).astype(BF16).reshape(shape)

    def out_z(n):
        for d in ZD:
            zland(n, d).wait_recv()
        outx[n] = order(p1, inz[n], (NQ, XR, C))
        for d in XD:
            xcopy(n, d).start()
        inx[n, q] = outx[n, q]

    def out_x(n):
        for d in XD:
            xland(n, d).wait_recv()
        yb[normal(n), 1] = order(p2, inx[n], (BOTH, C))
        ycopy(n, 0).start()
        ycopy(n, 1).start()

    def out_y(n):
        ycopy(n, 0).wait_recv()
        ycopy(n, 2).start()
        ycopy(n, 1).wait_recv()
        ycopy(n, 3).start()

    def raw_on(v):
        rcopy(v, 0).wait_recv()
        rcopy(v, 2).start()
        rcopy(v, 1).wait_recv()
        rcopy(v, 3).start()

    def unit_box(u):
        v, r = u // NT, u % NT

        @pl.when(r == 3)
        def _():
            rcopy(v, 2).wait_recv()
            rcopy(v, 3).wait_recv()

        o = turn(r)
        ubox[u] = dot(plc[o], raw[v, o]).astype(BF16).reshape(NZ, ZR, C)
        for d in ZD:
            uzcopy(u, d).start()
        uinz[u, z] = ubox[u, z]

    def unit_z(u):
        for d in ZD:
            uzland(u, d).wait_recv()
        uoutx[u] = order(p1, uinz[u], (NQ, XR, C))
        for d in XD:
            uxcopy(u, d).start()
        uinx[u, q] = uoutx[u, q]

    def unit_x(u):
        for d in XD:
            uxland(u, d).wait_recv()
        yb[special(u // NT), turn(u % NT)] = order(p2, uinx[u], (BOTH, C))

    def release(_):
        for peers, ds in ((zpeer, ZD), (xpeer, XD)):
            for d in ds:
                pl.semaphore_signal(free, inc=1, device_id=peers(d), device_id_type=MESH)

    def work(s, first, last):
        size = (last - first) * SLOTS
        r = pl.ds(first * SLOTS, size)
        rows = yb[s, first:last, :SLOTS, :].reshape(size, C)
        cots = yb[s, first:last, SLOTS:, :].reshape(size, C)
        lg[r, :] += dot(rows, router_ref[:, piece(s)], NTD)

        @pl.loop(0, H // N)
        def _(n):
            part = pl.ds(pl.multiple_of(n * N, N), N)
            hid[r, part] += dot(rows, wu[s, :, part])
            dh[r, part] += dot(cots, wd[s, part, :], NTD)

    def near(s):
        for copy in weights(s):
            copy.wait()
        work(s, 0, 3)

    def away(s):
        for n in range(NN):

            @pl.when(s == normal(n))
            def _():
                ycopy(n, 2).wait_recv()
                ycopy(n, 3).wait_recv()

        work(s, 3, 4)

    BR = 32

    def middle(k):
        o = 2 * k - 3 * (k // 2)

        @pl.loop(0, SLOTS // BR)
        def _(b):
            silu_rows(pl.ds(pl.multiple_of(o * SLOTS + b * BR, BR), BR))

    def silu_rows(r):
        v, back = hid[r, :], dh[r, :]
        sig = 1.0 / (1.0 + jnp.exp(-v))
        a = (v * sig).astype(BF16)
        act[r, :] = a
        hc[r, :] = (back * (sig * (1.0 + v * (1.0 - sig)))).astype(BF16)
        part = jnp.sum(a.astype(F32) * back, axis=1, keepdims=True)
        mine = iota((BR, EXPERTS), 1) == me.astype(F32)
        logit = jnp.sum(jnp.where(mine, lg[r, :], 0.0), axis=1, keepdims=True)
        slope = part * (1.0 - 1.0 / (1.0 + jnp.exp(-logit)))
        slope_s[r, :] = jnp.broadcast_to(slope, (BR, 128))
        s1 = slope.astype(BF16).astype(F32)
        s2 = (slope - s1).astype(BF16).astype(F32)
        s3 = slope - s1 - s2
        k = iota((BR, 128), 1)
        slope3[r, :] = jnp.where(
            k == 0.0, s1, jnp.where(k == 1.0, s2, jnp.where(k == 2.0, s3, 0.0))
        ).astype(BF16)

    def value_of(s, o):
        r = pl.ds(pl.multiple_of(o * SLOTS, SLOTS), SLOTS)
        return dot(act[r, :], wd[s])

    def grad_of(s, o):
        r = pl.ds(pl.multiple_of(o * SLOTS, SLOTS), SLOTS)
        return dot(hc[r, :], wu[s], NTD) + slope_s[r, :1] * rrow[s, :1, :]

    def early(n):
        s = normal(n)
        sb[n, 0, hi] = grad_of(s, 2).astype(BF16)
        bcopy(n, 2).start()
        sb[n, 1, lo] = value_of(s, 0).astype(BF16)
        bcopy(n, 3).start()

    @pl.loop(0, OUT_STEPS)
    def _(i):
        for task in (out_z, raw_on, unit_box, out_x, unit_z, unit_x, release, out_y, near, away, middle, early):
            at(i, OUT[task.__name__], task)

    def back_far(n):
        s = normal(n)
        sa[n, 0] = value_of(s, 3).astype(BF16)
        acopy(n, 0).start()
        sa[n, 1] = grad_of(s, 3).astype(BF16)
        acopy(n, 1).start()

    def back_near(n):
        s = normal(n)
        value = value_of(s, 2)
        acopy(n, 0).wait_recv()
        sb[n, 0, lo] = (value + ra[n, 0].astype(F32)).astype(BF16)
        bcopy(n, 0).start()
        grad = grad_of(s, 0)
        acopy(n, 1).wait_recv()
        sb[n, 1, hi] = (grad + ra[n, 1].astype(F32)).astype(BF16)
        bcopy(n, 1).start()

    def back_own(n):
        value, grad = value_of(normal(n), 1), grad_of(normal(n), 1)
        for i in range(4):
            bcopy(n, i).wait_recv()
        value = value + rb[n, 0, :SLOTS, :].astype(F32) + rb[n, 1, :SLOTS, :].astype(F32)
        grad = grad + rb[n, 0, SLOTS:, :].astype(F32) + rb[n, 1, SLOTS:, :].astype(F32)
        both = jnp.concatenate([value, grad], axis=0).astype(BF16)
        for d in XD:
            xcopy(n, d).wait_send()
        outx[n] = order(p2t, both, (NQ, XR, C))
        for d in XD:
            xcopy(n, d).start()
        inx[n, q] = outx[n, q]

    def back_x(n):
        for d in XD:
            xland(n, d).wait_recv()
        for d in ZD:
            zcopy(n, d).wait_send()
        box[n] = order(p1t, inx[n], (NZ, ZR, C))
        for d in ZD:
            zcopy(n, d).start()
        inz[n, z] = box[n, z]

    def back_z(n):
        for d in ZD:
            zland(n, d).wait_recv()
        got = inz[n].reshape(BOTH, C)
        cols = piece(normal(n))
        mixed_ref[:, cols] = (gate_s[:, :1] * dot(pltx[1], got)).astype(BF16)
        tgrad_ref[:, cols] = dot(pltc[1], got).astype(BF16)

    def unit_back(u):
        s, o = special(u // NT), turn(3 - u % NT)
        value, grad = value_of(s, o), grad_of(s, o)
        both = jnp.concatenate([value, grad], axis=0).astype(BF16)
        for d in XD:
            uxcopy(u, d).wait_send()
        uoutx[u] = order(p2t, both, (NQ, XR, C))

        @pl.when(u == 0)
        def _():
            pl.semaphore_wait(free, NZ + NQ - 2)

        for d in XD:
            uxcopy(u, d).start()
        uinx[u, q] = uoutx[u, q]

    def unit_back_x(u):
        for d in XD:
            uxland(u, d).wait_recv()
        for d in ZD:
            uzcopy(u, d).wait_send()
        ubox[u] = order(p1t, uinx[u], (NZ, ZR, C))
        for d in ZD:
            uzcopy(u, d).start()
        uinz[u, z] = ubox[u, z]

    def unit_back_z(u):
        for d in ZD:
            uzland(u, d).wait_recv()
        v, r = u // NT, u % NT

        @pl.when(r == 0)
        def _():
            for i in range(4):
                rcopy(v, i).wait_send()

        o = turn(3 - r)
        got = uinz[u].reshape(BOTH, C)
        raw[v, o, rlo] = dot(pltx[o], got).astype(BF16)
        raw[v, o, rhi] = dot(pltc[o], got).astype(BF16)

        @pl.when(r == 0)
        def _():
            uacopy(v, 0).start()
            uacopy(v, 1).start()

        @pl.when(r == 1)
        def _():
            uacopy(v, 1).wait_recv()
            raw[v, 0, rhi] = (raw[v, 0, rhi].astype(F32) + ua[v, 1].astype(F32)).astype(BF16)
            ubcopy(v, 1).start()

        @pl.when(r == 2)
        def _():
            uacopy(v, 0).wait_recv()
            raw[v, 2, rlo] = (raw[v, 2, rlo].astype(F32) + ua[v, 0].astype(F32)).astype(BF16)
            ubcopy(v, 0).start()

    def unit_sum(v):
        ubcopy(v, 0).wait_recv()
        ubcopy(v, 1).wait_recv()
        got = raw[v, 1].astype(F32) + ub[v, 0].astype(F32) + ub[v, 1].astype(F32)
        cols = piece(special(v))
        value = got[:ROWS].astype(BF16).astype(F32)
        mixed_ref[:, cols] = (gate_s[:, :1] * value).astype(BF16)
        tgrad_ref[:, cols] = got[ROWS:].astype(BF16)

    def grads_out(s, n):
        part = pl.ds(pl.multiple_of(n * N, N), N)
        k = n % 2
        return (
            pltpu.make_async_copy(gsu.at[k], upg_hbm.at[0, piece(s), part], gsem.at[0, k]),
            pltpu.make_async_copy(gsd.at[k], downg_hbm.at[0, part, piece(s)], gsem.at[1, k]),
        )

    def grads(s):
        @pl.loop(0, H // N)
        def _(n):
            @pl.when((s > 0) | (n >= 2))
            def _():
                for copy in grads_out(s, n):
                    copy.wait()

            part = pl.ds(pl.multiple_of(n * N, N), N)
            gsd[n % 2] = dot(act[:, part], cots_of(s), TND).astype(BF16)
            gsu[n % 2] = dot(rows_of(s), hc[:, part], TND).astype(BF16)
            for copy in grads_out(s, n):
                copy.start()

    def vector_0(_):
        @pl.loop(0, NC)
        def _(s):
            three = dot(slope3[...], rows_of(s), TND)
            vy[t, :, piece(s)] = jnp.sum(three, axis=0, keepdims=True)

        for d in YD:
            vycopy(d).start()

    def vector_1(_):
        for d in YD:
            vyland(d).wait_recv()
        vx[q] = (vy[0] + vy[1]) + (vy[2] + vy[3])
        for d in XD:
            vxcopy(d).start()

    def vector_2(_):
        for d in XD:
            vxland(d).wait_recv()
        for d in ZD:
            vzcopy(d).start()
        vz[z] = vx[...]

    @pl.loop(0, BACK_STEPS)
    def _(i):
        for task in (
            unit_back, back_far, vector_0, grads, vector_1, unit_back_x, unit_back_z, back_near, back_own,
            vector_2, back_x, unit_sum, back_z,
        ):
            at(i, BACK[task.__name__], task)

    for d in ZD:
        vzland(d).wait_recv()
    rgrad_ref[...] = vz[...].reshape(EXPERTS, C * NC)
    for d in YD:
        vtcopy(d).wait_send()
        vycopy(d).wait_send()
    for d in XD:
        vxcopy(d).wait_send()
    for d in ZD:
        vzcopy(d).wait_send()

    @pl.loop(0, NN)
    def _(n):
        for i in range(4):
            ycopy(n, i).wait_send()
            bcopy(n, i).wait_send()
        for i in range(2):
            acopy(n, i).wait_send()
        for d in XD:
            xcopy(n, d).wait_send()
        for d in ZD:
            zcopy(n, d).wait_send()

    @pl.loop(0, NU)
    def _(u):
        for d in XD:
            uxcopy(u, d).wait_send()
        for d in ZD:
            uzcopy(u, d).wait_send()

    @pl.loop(0, NS)
    def _(v):
        for i in range(2):
            uacopy(v, i).wait_send()
            ubcopy(v, i).wait_send()

    for n in range(2):
        for copy in grads_out(NC - 1, n):
            copy.wait()


def hand_over(arrays):
    cuts = []
    for k, a in enumerate(arrays):
        axis = len(a.shape) - 2
        parts = 4 if a.size > 1 << 20 else 1
        size = a.shape[axis] // parts
        cuts += [(k, (slice(None),) * axis + (pl.ds(p * size, size),)) for p in range(parts)]

    def body(*refs):
        n = len(arrays)
        ins, outs, bufs, sems = refs[:n], refs[n : 2 * n], refs[2 * n : 3 * n], refs[3 * n]
        reads = [
            pltpu.make_async_copy(ins[k].at[c], bufs[k].at[c], sems.at[0, i])
            for i, (k, c) in enumerate(cuts)
        ]
        writes = [
            pltpu.make_async_copy(bufs[k].at[c], outs[k].at[c], sems.at[1, i])
            for i, (k, c) in enumerate(cuts)
        ]
        for copy in reads:
            copy.start()
        for read, write in zip(reads, writes):
            read.wait()
            write.start()
        for copy in writes:
            copy.wait()

    hbm = pl.BlockSpec(memory_space=pl.ANY)
    return pl.pallas_call(
        body,
        out_shape=tuple(jax.ShapeDtypeStruct(a.shape, a.dtype) for a in arrays),
        in_specs=[hbm] * len(arrays),
        out_specs=(hbm,) * len(arrays),
        scratch_shapes=[pltpu.VMEM(a.shape, a.dtype) for a in arrays]
        + [pltpu.SemaphoreType.DMA((2, len(cuts)))],
        compiler_params=pltpu.CompilerParams(vmem_limit_bytes=60 << 20),
    )(*arrays)


def per_device(tokens, expert_ids, live_counts, router, up_weight, down_weight, out_grad):
    width = tokens.shape[1]
    assert tokens.shape == (ROWS, C * NC) and router.shape[1] == EXPERTS
    assert up_weight.shape == (1, C * NC, H)
    vmem = pl.BlockSpec(memory_space=pltpu.VMEM)
    smem = pl.BlockSpec(memory_space=pltpu.SMEM)
    hbm = pl.BlockSpec(memory_space=pl.ANY)
    every = NT * SLOTS
    V, DMA = pltpu.VMEM, pltpu.SemaphoreType.DMA
    scratch = [
        V((NN, NZ, ZR, C), BF16),
        V((NN, NZ, ZR, C), BF16),
        V((NN, NQ, XR, C), BF16),
        V((NN, NQ, XR, C), BF16),
        V((NU, NZ, ZR, C), BF16),
        V((NU, NZ, ZR, C), BF16),
        V((NU, NQ, XR, C), BF16),
        V((NU, NQ, XR, C), BF16),
        V((NS, NT, 2 * ROWS, C), BF16),
        V((NC, NT, BOTH, C), BF16),
        V((NC, C, H), BF16),
        V((NC, H, C), BF16),
        V((every, H), F32),
        V((every, H), F32),
        V((every, H), BF16),
        V((every, H), BF16),
        V((every, EXPERTS), F32),
        V((ROWS, 128), F32),
        V((every, 128), F32),
        V((every, 128), BF16),
        V((NN, 2, SLOTS, C), BF16),
        V((NN, 2, SLOTS, C), BF16),
        V((NN, 2, BOTH, C), BF16),
        V((NN, 2, BOTH, C), BF16),
        V((NS, 2, ROWS, C), BF16),
        V((NS, 2, 2 * ROWS, C), BF16),
        V((2, C, N), BF16),
        V((2, N, C), BF16),
        V((BOTH, BOTH), BF16),
        V((BOTH, BOTH), BF16),
        V((BOTH, BOTH), BF16),
        V((BOTH, BOTH), BF16),
        V((NT, BOTH, 2 * ROWS), BF16),
        V((NT, ROWS, BOTH), BF16),
        V((NT, ROWS, BOTH), BF16),
        V((NC, 8, C), F32),
        V((NT, 1, ROWS), F32),
        V((NT, 1, width), F32),
        V((NQ, 1, width), F32),
        V((NZ, NQ, 1, width), F32),
        DMA((2, NC)),
        DMA((NN, NZ)), DMA((NN, NZ)), DMA((NN, NQ)), DMA((NN, NQ)), DMA((NN, 4)), DMA((NN, 4)),
        DMA((NN, 2)), DMA((NN, 2)), DMA((NN, 4)), DMA((NN, 4)),
        DMA((NU, NZ)), DMA((NU, NZ)), DMA((NU, NQ)), DMA((NU, NQ)), DMA((NS, 4)), DMA((NS, 4)),
        DMA((NS, 2)), DMA((NS, 2)), DMA((NS, 2)), DMA((NS, 2)),
        DMA((2, 2)),
        DMA((NT,)), DMA((NT,)), DMA((NT,)), DMA((NT,)),
        DMA((NQ,)), DMA((NQ,)), DMA((NZ,)), DMA((NZ,)),
        pltpu.SemaphoreType.REGULAR,
    ]
    S = jax.ShapeDtypeStruct
    results = pl.pallas_call(
        kernel,
        out_shape=(
            S((ROWS, width), BF16),
            S((ROWS, width), BF16),
            S((1, width, H), BF16),
            S((1, H, width), BF16),
            S((EXPERTS, width), F32),
        ),
        in_specs=[vmem, smem, vmem, vmem, vmem, hbm, hbm],
        out_specs=(vmem, vmem, hbm, hbm, vmem),
        scratch_shapes=scratch,
        compiler_params=pltpu.CompilerParams(
            collective_id=0, has_side_effects=True, vmem_limit_bytes=67043328
        ),
    )(
        expert_ids.reshape(1, ROWS), live_counts, router.T, tokens, out_grad, up_weight, down_weight
    )
    mixed, tgrad, upg, downg, rgrad = hand_over(results)
    return (mixed, tgrad, upg, downg, rgrad.T)


def solution(mesh):
    rows = P(("expert", "tensor"), None)
    in_specs = (
        rows,
        rows,
        P(("expert", "tensor")),
        P(),
        P("expert", None, "tensor"),
        P("expert", "tensor", None),
        rows,
    )
    out_specs = (rows, rows, P("expert", None, "tensor"), P("expert", "tensor", None), P())
    return jax.shard_map(
        per_device, mesh=mesh, in_specs=in_specs, out_specs=out_specs, check_vma=False
    )
```

```python
import jax
import jax.numpy as jnp
from jax import lax
from jax.experimental import pallas as pl
from jax.experimental.pallas import tpu as pltpu
from jax.sharding import PartitionSpec as P

F32, BF16, I32 = jnp.float32, jnp.bfloat16, jnp.int32
MESH = pl.DeviceIdType.MESH

NZ, NQ, NT = 4, 8, 4
EXPERTS = NZ * NQ
ROWS, MOST = 128, 6
SLOTS = EXPERTS * MOST
BOTH = 2 * SLOTS
C, NC = 512, 5
NN, NS = 3, 2
NU = NT * NS
ZR, XR = NQ * 2 * MOST, 2 * NZ * MOST
H = 1024
N = 256


OUT_STEPS = 28
OUT = dict(
    raw_on=(1, 4,),
    early=(23, 24, 25,),
    out_x=(4, 8, 9,),
    release=(26,),
    out_z=(1, 3, 4,),
    out_y=(10, 13, 17,),
    unit_box=(0, 1, 2, 4, 5, 6, 7, 8,),
    near=(10, 15, 16, 17, 21,),
    unit_z=(8, 9, 10, 12, 14, 16, 17, 19,),
    away=(18, 19, 20, 26, 27,),
    middle=(21, 22, 25, 27,),
    unit_x=(10, 11, 13, 16, 17, 18, 20, 25,),
)
BACK_STEPS = 24
BACK = dict(
    unit_back=(0, 1, 2, 3, 4, 5, 6, 7,),
    back_own=(16, 17, 18,),
    back_x=(18, 19, 22,),
    back_far=(7, 8, 9,),
    grads=(9, 10, 11, 12, 13,),
    vector_1=(16,),
    vector_2=(19,),
    vector_0=(13,),
    unit_back_x=(6, 9, 11, 12, 13, 15, 16, 17,),
    unit_sum=(19, 23,),
    back_near=(11, 12, 13,),
    unit_back_z=(10, 13, 14, 15, 16, 19, 20, 21,),
    back_z=(21, 22, 23,),
)


def dot(a, b, dims=((1,), (0,))):
    return lax.dot_general(a, b, (dims, ((), ())), preferred_element_type=F32)


NTD = ((1,), (1,))
TND = ((0,), (0,))


def iota(shape, axis):
    return lax.broadcasted_iota(I32, shape, axis).astype(F32)


def turn(r):
    return r + 1 - 3 * (r // 2) + 2 * (r // 3)


def at(i, steps, task):
    here = i == steps[0]
    for step in steps[1:]:
        here = here | (i == step)

    @pl.when(here)
    def _():
        k = 0
        for step in steps[1:]:
            k = k + (i + 64 - step) // 64
        task(k)


def onehot(mask):
    return jnp.where(mask, 1.0, 0.0).astype(BF16)


def div(a, b):
    return jnp.floor((a + 0.5) * (1.0 / b))


def source_1(o):
    q = div(o, 2 * NZ * MOST)
    r = o - q * (2 * NZ * MOST)
    a = div(r, NZ * MOST)
    r = r - a * (NZ * MOST)
    z = div(r, MOST)
    k = r - z * MOST
    return z * (NQ * 2 * MOST) + q * (2 * MOST) + a * MOST + k


def source_2(o):
    a = div(o, SLOTS)
    r = o - a * SLOTS
    q = div(r, NZ * MOST)
    m = r - q * (NZ * MOST)
    return q * (2 * NZ * MOST) + a * (NZ * MOST) + m


def kernel(
    ids_ref, live_ref, router_ref, tok_ref, og_ref, up_hbm, down_hbm,
    mixed_ref, tgrad_ref, upg_hbm, downg_hbm, rgrad_ref,
    box, inz, outx, inx, ubox, uinz, uoutx, uinx, raw, yb, wu, wd, hid, dh, act, hc,
    lg, gate_s, slope_s, slope3, sa, ra, sb, rb, ua, ub, gsu, gsd,
    p1, p1t, p2, p2t, plc, pltx, pltc, rrow, vt, vy, vx, vz,
    wsem, zs, zr, xs, xr, ys, yr, as_, ar, bs, br, uzs, uzr, uxs, uxr, rs, rr,
    uas, uar, ubs, ubr, gsem, vts, vtr, vys, vyr, vxs, vxr, vzs, vzr, free,
):
    me = lax.axis_index("expert")
    t = lax.axis_index("tensor")
    z, q = me // NQ, me % NQ
    lo, hi = pl.ds(0, SLOTS), pl.ds(SLOTS, SLOTS)
    rlo, rhi = pl.ds(0, ROWS), pl.ds(ROWS, ROWS)
    ZD, XD, YD = range(1, NZ), range(1, NQ), range(1, NT)

    def zpeer(d):
        return (((z + d) % NZ) * NQ + q, t)

    def xpeer(d):
        return (z * NQ + (q + d) % NQ, t)

    def ypeer(d):
        return (me, (t + d) % NT)

    def remote(src, dst, ssem, rsem, peer):
        return pltpu.make_async_remote_copy(
            src_ref=src, dst_ref=dst, send_sem=ssem, recv_sem=rsem,
            device_id=peer, device_id_type=MESH,
        )

    def piece(s):
        return pl.ds(pl.multiple_of(s * C, C), C)

    def normal(n):
        return n + (n + 1) // 2

    def special(v):
        return 1 + 3 * v

    def weights(s):
        return (
            pltpu.make_async_copy(up_hbm.at[0, piece(s), :], wu.at[s], wsem.at[0, s]),
            pltpu.make_async_copy(down_hbm.at[0, :, piece(s)], wd.at[s], wsem.at[1, s]),
        )

    def zcopy(n, d):
        return remote(box.at[n, (z + d) % NZ], inz.at[n, z], zs.at[n], zr.at[n], zpeer(d))

    def zall(n):
        some = pl.ds(0, NZ - 1)
        return remote(box.at[n, some], inz.at[n, some], zs.at[n], zr.at[n], zpeer(1))

    def xcopy(n, d):
        return remote(outx.at[n, (q + d) % NQ], inx.at[n, q], xs.at[n], xr.at[n], xpeer(d))

    def xall(n):
        some = pl.ds(0, NQ - 1)
        return remote(outx.at[n, some], inx.at[n, some], xs.at[n], xr.at[n], xpeer(1))

    def uzcopy(u, d):
        return remote(ubox.at[u, (z + d) % NZ], uinz.at[u, z], uzs.at[u], uzr.at[u], zpeer(d))

    def uzall(u):
        some = pl.ds(0, NZ - 1)
        return remote(ubox.at[u, some], uinz.at[u, some], uzs.at[u], uzr.at[u], zpeer(1))

    def uxcopy(u, d):
        return remote(uoutx.at[u, (q + d) % NQ], uinx.at[u, q], uxs.at[u], uxr.at[u], xpeer(d))

    def uxall(u):
        some = pl.ds(0, NQ - 1)
        return remote(uoutx.at[u, some], uinx.at[u, some], uxs.at[u], uxr.at[u], xpeer(1))

    SIDE = (1, NT - 1, 1, NT - 1)

    def ycopy(n, i):
        b = yb.at[normal(n)]
        src = (b.at[1], b.at[1], b.at[0, lo], b.at[2, hi])[i]
        dst = (b.at[0], b.at[2], b.at[3, lo], b.at[3, hi])[i]
        return remote(src, dst, ys.at[n, i], yr.at[n, i], ypeer(SIDE[i]))

    def rcopy(v, i):
        b = raw.at[v]
        src = (b.at[1], b.at[1], b.at[0, rlo], b.at[2, rhi])[i]
        dst = (b.at[0], b.at[2], b.at[3, rlo], b.at[3, rhi])[i]
        return remote(src, dst, rs.at[v, i], rr.at[v, i], ypeer(SIDE[i]))

    def acopy(n, i):
        return remote(sa.at[n, i], ra.at[n, i], as_.at[n, i], ar.at[n, i], ypeer(SIDE[i]))

    def bcopy(n, i):
        k, half = i % 2, (lo, hi, hi, lo)[i]
        return remote(sb.at[n, k, half], rb.at[n, k, half], bs.at[n, i], br.at[n, i], ypeer(SIDE[i]))

    def uacopy(v, i):
        src = raw.at[v, 3, (rlo, rhi)[i]]
        return remote(src, ua.at[v, i], uas.at[v, i], uar.at[v, i], ypeer(SIDE[i]))

    def ubcopy(v, i):
        return remote(raw.at[v, (2, 0)[i]], ub.at[v, i], ubs.at[v, i], ubr.at[v, i], ypeer(SIDE[i]))

    def vtcopy(d):
        return remote(vt.at[1], vt.at[(1, 0, 3, 2)[d]], vts.at[d], vtr.at[d], ypeer(d))

    def vycopy(d):
        return remote(vy.at[t], vy.at[t], vys.at[d], vyr.at[d], ypeer(d))

    def vyland(d):
        dst = vy.at[(t + NT - d) % NT]
        return remote(dst, dst, vys.at[d], vyr.at[d], ypeer(d))

    def vxcopy(d):
        return remote(vx.at[q], vx.at[q], vxs.at[d], vxr.at[d], xpeer(d))

    def vxland(d):
        dst = vx.at[(q + NQ - d) % NQ]
        return remote(dst, dst, vxs.at[d], vxr.at[d], xpeer(d))

    def vzcopy(d):
        return remote(vx, vz.at[z], vzs.at[d], vzr.at[d], zpeer(d))

    def vzland(d):
        return remote(vx, vz.at[(z + NZ - d) % NZ], vzs.at[d], vzr.at[d], zpeer(d))

    for s in range(NC):
        for copy in weights(s):
            copy.start()

    barrier = pltpu.get_barrier_semaphore()
    for peers, ds in ((zpeer, ZD), (xpeer, XD), (ypeer, YD)):
        for d in ds:
            pl.semaphore_signal(barrier, inc=1, device_id=peers(d), device_id_type=MESH)

    diag = iota((ROWS, ROWS), 0) == iota((ROWS, ROWS), 1)

    def turned(line):
        return jnp.sum(jnp.where(diag, line, 0.0), axis=1, keepdims=True)

    def both_of(s):
        cot = (gate_s[:, :1] * og_ref[:, piece(s)].astype(F32)).astype(BF16)
        return jnp.concatenate([tok_ref[:, piece(s)], cot], axis=0)

    def place(o):
        line = vt[o]
        slot = iota((BOTH, ROWS), 0)
        plc[o, :, :ROWS] = onehot(slot == line)
        plc[o, :, ROWS:] = onehot(slot == line + MOST)
        column = turned(line)
        lane = iota((ROWS, BOTH), 1)
        pltx[o] = onehot(lane == column)
        pltc[o] = onehot(lane == column + MOST)

    ids = turned(ids_ref[...].astype(F32))
    chosen = ids == iota((ROWS, EXPERTS), 1)
    logits = dot(tok_ref[...], router_ref[...], NTD)
    gate = jax.nn.sigmoid(jnp.sum(jnp.where(chosen, logits, 0.0), axis=1, keepdims=True))
    gate_s[...] = jnp.broadcast_to(gate, (ROWS, 128))
    raw[0, 1] = both_of(special(0))
    pl.semaphore_wait(barrier, NZ + NQ + NT - 3)
    rcopy(0, 0).start()
    rcopy(0, 1).start()

    tri = onehot(iota((ROWS, ROWS), 0) > iota((ROWS, ROWS), 1))
    counts = dot(tri, onehot(chosen))
    rank = jnp.sum(jnp.where(chosen, counts, 0.0), axis=1, keepdims=True)
    live = lax.broadcasted_iota(I32, (ROWS, 1), 0) < live_ref[0]
    target = jnp.where(live, ids * (2.0 * MOST) + rank, -1000.0)
    vt[1] = jnp.sum(jnp.where(diag, target, 0.0), axis=0, keepdims=True)
    raw[1, 1] = both_of(special(1))
    for d in YD:
        vtcopy(d).start()
    rcopy(1, 0).start()
    rcopy(1, 1).start()
    place(1)

    @pl.loop(0, NN)
    def _(n):
        box[n] = dot(plc[1], both_of(normal(n))).astype(BF16).reshape(NZ, ZR, C)
        for d in ZD:
            zcopy(n, d).start()
        inz[n, z] = box[n, z]

    column, line = iota((BOTH, 1), 0), iota((1, BOTH), 1)
    across, down = iota((BOTH, BOTH), 1), iota((BOTH, BOTH), 0)
    p1[...] = onehot(source_1(column) == across)
    p1t[...] = onehot(source_1(line) == down)
    p2[...] = onehot(source_2(column) == across)
    p2t[...] = onehot(source_2(line) == down)
    for d in YD:
        vtcopy(d).wait_recv()
        place((1, 0, 3, 2)[d])

    hid[...] = jnp.zeros_like(hid)
    dh[...] = jnp.zeros_like(dh)
    lg[...] = jnp.zeros_like(lg)
    own = onehot(iota((8, EXPERTS), 1) == me.astype(F32))

    @pl.loop(0, NC)
    def _(s):
        rrow[s] = dot(own, router_ref[:, piece(s)])

    def rows_of(s):
        return yb[s, :, :SLOTS, :].reshape(NT * SLOTS, C)

    def cots_of(s):
        return yb[s, :, SLOTS:, :].reshape(NT * SLOTS, C)

    def order(perm, rows, shape):
        return dot(perm[...], rows.reshape(BOTH, C)).astype(BF16).reshape(shape)

    def out_z(n):
        zall(n).wait_recv()
        outx[n] = order(p1, inz[n], (NQ, XR, C))
        for d in XD:
            xcopy(n, d).start()
        inx[n, q] = outx[n, q]

    def out_x(n):
        xall(n).wait_recv()
        yb[normal(n), 1] = order(p2, inx[n], (BOTH, C))
        ycopy(n, 0).start()
        ycopy(n, 1).start()

    def out_y(n):
        ycopy(n, 0).wait_recv()
        ycopy(n, 2).start()
        ycopy(n, 1).wait_recv()
        ycopy(n, 3).start()

    def raw_on(v):
        rcopy(v, 0).wait_recv()
        rcopy(v, 2).start()
        rcopy(v, 1).wait_recv()
        rcopy(v, 3).start()

    def unit_box(u):
        v, r = u // NT, u % NT

        @pl.when(r == 3)
        def _():
            rcopy(v, 2).wait_recv()
            rcopy(v, 3).wait_recv()

        o = turn(r)
        ubox[u] = dot(plc[o], raw[v, o]).astype(BF16).reshape(NZ, ZR, C)
        for d in ZD:
            uzcopy(u, d).start()
        uinz[u, z] = ubox[u, z]

    def unit_z(u):
        uzall(u).wait_recv()
        uoutx[u] = order(p1, uinz[u], (NQ, XR, C))
        for d in XD:
            uxcopy(u, d).start()
        uinx[u, q] = uoutx[u, q]

    def unit_x(u):
        uxall(u).wait_recv()
        yb[special(u // NT), turn(u % NT)] = order(p2, uinx[u], (BOTH, C))

    def release(_):
        for peers, ds in ((zpeer, ZD), (xpeer, XD)):
            for d in ds:
                pl.semaphore_signal(free, inc=1, device_id=peers(d), device_id_type=MESH)

    def work(s, first, last):
        size = (last - first) * SLOTS
        r = pl.ds(first * SLOTS, size)
        rows = yb[s, first:last, :SLOTS, :].reshape(size, C)
        cots = yb[s, first:last, SLOTS:, :].reshape(size, C)
        lg[r, :] += dot(rows, router_ref[:, piece(s)], NTD)

        @pl.loop(0, H // N)
        def _(n):
            part = pl.ds(pl.multiple_of(n * N, N), N)
            hid[r, part] += dot(rows, wu[s, :, part])
            dh[r, part] += dot(cots, wd[s, part, :], NTD)

    def near(s):
        for copy in weights(s):
            copy.wait()
        work(s, 0, 3)

    def away(s):
        for n in range(NN):

            @pl.when(s == normal(n))
            def _():
                ycopy(n, 2).wait_recv()
                ycopy(n, 3).wait_recv()

        work(s, 3, 4)

    BR = 32

    def middle(k):
        o = 2 * k - 3 * (k // 2)

        @pl.loop(0, SLOTS // BR)
        def _(b):
            silu_rows(pl.ds(pl.multiple_of(o * SLOTS + b * BR, BR), BR))

    def silu_rows(r):
        v, back = hid[r, :], dh[r, :]
        sig = 1.0 / (1.0 + jnp.exp(-v))
        a = (v * sig).astype(BF16)
        act[r, :] = a
        hc[r, :] = (back * (sig * (1.0 + v * (1.0 - sig)))).astype(BF16)
        part = jnp.sum(a.astype(F32) * back, axis=1, keepdims=True)
        mine = iota((BR, EXPERTS), 1) == me.astype(F32)
        logit = jnp.sum(jnp.where(mine, lg[r, :], 0.0), axis=1, keepdims=True)
        slope = part * (1.0 - 1.0 / (1.0 + jnp.exp(-logit)))
        slope_s[r, :] = jnp.broadcast_to(slope, (BR, 128))
        s1 = slope.astype(BF16).astype(F32)
        s2 = (slope - s1).astype(BF16).astype(F32)
        s3 = slope - s1 - s2
        k = iota((BR, 128), 1)
        slope3[r, :] = jnp.where(
            k == 0.0, s1, jnp.where(k == 1.0, s2, jnp.where(k == 2.0, s3, 0.0))
        ).astype(BF16)

    def value_of(s, o):
        r = pl.ds(pl.multiple_of(o * SLOTS, SLOTS), SLOTS)
        return dot(act[r, :], wd[s])

    def grad_of(s, o):
        r = pl.ds(pl.multiple_of(o * SLOTS, SLOTS), SLOTS)
        return dot(hc[r, :], wu[s], NTD) + slope_s[r, :1] * rrow[s, :1, :]

    def early(n):
        s = normal(n)
        sb[n, 0, hi] = grad_of(s, 2).astype(BF16)
        bcopy(n, 2).start()
        sb[n, 1, lo] = value_of(s, 0).astype(BF16)
        bcopy(n, 3).start()

    @pl.loop(0, OUT_STEPS)
    def _(i):
        for task in (
            raw_on, early, out_x, release, out_z, out_y, unit_box, near, unit_z, away, middle, unit_x,
        ):
            at(i, OUT[task.__name__], task)

    def back_far(n):
        s = normal(n)
        sa[n, 0] = value_of(s, 3).astype(BF16)
        acopy(n, 0).start()
        sa[n, 1] = grad_of(s, 3).astype(BF16)
        acopy(n, 1).start()

    def back_near(n):
        s = normal(n)
        value = value_of(s, 2)
        acopy(n, 0).wait_recv()
        sb[n, 0, lo] = (value + ra[n, 0].astype(F32)).astype(BF16)
        bcopy(n, 0).start()
        grad = grad_of(s, 0)
        acopy(n, 1).wait_recv()
        sb[n, 1, hi] = (grad + ra[n, 1].astype(F32)).astype(BF16)
        bcopy(n, 1).start()

    def back_own(n):
        value, grad = value_of(normal(n), 1), grad_of(normal(n), 1)
        for i in range(4):
            bcopy(n, i).wait_recv()
        value = value + rb[n, 0, :SLOTS, :].astype(F32) + rb[n, 1, :SLOTS, :].astype(F32)
        grad = grad + rb[n, 0, SLOTS:, :].astype(F32) + rb[n, 1, SLOTS:, :].astype(F32)
        both = jnp.concatenate([value, grad], axis=0).astype(BF16)
        xall(n).wait_send()
        outx[n] = order(p2t, both, (NQ, XR, C))
        for d in XD:
            xcopy(n, d).start()
        inx[n, q] = outx[n, q]

    def back_x(n):
        xall(n).wait_recv()
        zall(n).wait_send()
        box[n] = order(p1t, inx[n], (NZ, ZR, C))
        for d in ZD:
            zcopy(n, d).start()
        inz[n, z] = box[n, z]

    def back_z(n):
        zall(n).wait_recv()
        got = inz[n].reshape(BOTH, C)
        cols = piece(normal(n))
        mixed_ref[:, cols] = (gate_s[:, :1] * dot(pltx[1], got)).astype(BF16)
        tgrad_ref[:, cols] = dot(pltc[1], got).astype(BF16)

    def unit_back(u):
        s, o = special(u // NT), turn(3 - u % NT)
        value, grad = value_of(s, o), grad_of(s, o)
        both = jnp.concatenate([value, grad], axis=0).astype(BF16)
        uxall(u).wait_send()
        uoutx[u] = order(p2t, both, (NQ, XR, C))

        @pl.when(u == 0)
        def _():
            pl.semaphore_wait(free, NZ + NQ - 2)

        for d in XD:
            uxcopy(u, d).start()
        uinx[u, q] = uoutx[u, q]

    def unit_back_x(u):
        uxall(u).wait_recv()
        uzall(u).wait_send()
        ubox[u] = order(p1t, uinx[u], (NZ, ZR, C))
        for d in ZD:
            uzcopy(u, d).start()
        uinz[u, z] = ubox[u, z]

    def unit_back_z(u):
        uzall(u).wait_recv()
        v, r = u // NT, u % NT

        @pl.when(r == 0)
        def _():
            for i in range(4):
                rcopy(v, i).wait_send()

        o = turn(3 - r)
        got = uinz[u].reshape(BOTH, C)
        raw[v, o, rlo] = dot(pltx[o], got).astype(BF16)
        raw[v, o, rhi] = dot(pltc[o], got).astype(BF16)

        @pl.when(r == 0)
        def _():
            uacopy(v, 0).start()
            uacopy(v, 1).start()

        @pl.when(r == 1)
        def _():
            uacopy(v, 1).wait_recv()
            raw[v, 0, rhi] = (raw[v, 0, rhi].astype(F32) + ua[v, 1].astype(F32)).astype(BF16)
            ubcopy(v, 1).start()

        @pl.when(r == 2)
        def _():
            uacopy(v, 0).wait_recv()
            raw[v, 2, rlo] = (raw[v, 2, rlo].astype(F32) + ua[v, 0].astype(F32)).astype(BF16)
            ubcopy(v, 0).start()

    def unit_sum(v):
        ubcopy(v, 0).wait_recv()
        ubcopy(v, 1).wait_recv()
        got = raw[v, 1].astype(F32) + ub[v, 0].astype(F32) + ub[v, 1].astype(F32)
        cols = piece(special(v))
        value = got[:ROWS].astype(BF16).astype(F32)
        mixed_ref[:, cols] = (gate_s[:, :1] * value).astype(BF16)
        tgrad_ref[:, cols] = got[ROWS:].astype(BF16)

    def grads_out(s, n):
        part = pl.ds(pl.multiple_of(n * N, N), N)
        k = n % 2
        return (
            pltpu.make_async_copy(gsu.at[k], upg_hbm.at[0, piece(s), part], gsem.at[0, k]),
            pltpu.make_async_copy(gsd.at[k], downg_hbm.at[0, part, piece(s)], gsem.at[1, k]),
        )

    def grads(s):
        @pl.loop(0, H // N)
        def _(n):
            @pl.when((s > 0) | (n >= 2))
            def _():
                for copy in grads_out(s, n):
                    copy.wait()

            part = pl.ds(pl.multiple_of(n * N, N), N)
            gsd[n % 2] = dot(act[:, part], cots_of(s), TND).astype(BF16)
            gsu[n % 2] = dot(rows_of(s), hc[:, part], TND).astype(BF16)
            for copy in grads_out(s, n):
                copy.start()

    def vector_0(_):
        @pl.loop(0, NC)
        def _(s):
            three = dot(slope3[...], rows_of(s), TND)
            vy[t, :, piece(s)] = jnp.sum(three, axis=0, keepdims=True)

        for d in YD:
            vycopy(d).start()

    def vector_1(_):
        for d in YD:
            vyland(d).wait_recv()
        vx[q] = (vy[0] + vy[1]) + (vy[2] + vy[3])
        for d in XD:
            vxcopy(d).start()

    def vector_2(_):
        for d in XD:
            vxland(d).wait_recv()
        for d in ZD:
            vzcopy(d).start()
        vz[z] = vx[...]

    @pl.loop(0, BACK_STEPS)
    def _(i):
        for task in (
            unit_back, back_own, back_x, back_far, grads, vector_1, vector_2, vector_0, unit_back_x, unit_sum, back_near, unit_back_z, back_z,
        ):
            at(i, BACK[task.__name__], task)

    for d in ZD:
        vzland(d).wait_recv()
    rgrad_ref[...] = vz[...].reshape(EXPERTS, C * NC)
    for d in YD:
        vtcopy(d).wait_send()
        vycopy(d).wait_send()
    for d in XD:
        vxcopy(d).wait_send()
    for d in ZD:
        vzcopy(d).wait_send()

    @pl.loop(0, NN)
    def _(n):
        for i in range(4):
            ycopy(n, i).wait_send()
            bcopy(n, i).wait_send()
        for i in range(2):
            acopy(n, i).wait_send()
        xall(n).wait_send()
        zall(n).wait_send()

    @pl.loop(0, NU)
    def _(u):
        uxall(u).wait_send()
        uzall(u).wait_send()

    @pl.loop(0, NS)
    def _(v):
        for i in range(2):
            uacopy(v, i).wait_send()
            ubcopy(v, i).wait_send()

    for n in range(2):
        for copy in grads_out(NC - 1, n):
            copy.wait()


def hand_over(arrays):
    cuts = []
    for k, a in enumerate(arrays):
        axis = len(a.shape) - 2
        parts = 4 if a.size > 1 << 20 else 1
        size = a.shape[axis] // parts
        cuts += [(k, (slice(None),) * axis + (pl.ds(p * size, size),)) for p in range(parts)]

    def body(*refs):
        n = len(arrays)
        ins, outs, bufs, sems = refs[:n], refs[n : 2 * n], refs[2 * n : 3 * n], refs[3 * n]
        reads = [
            pltpu.make_async_copy(ins[k].at[c], bufs[k].at[c], sems.at[0, i])
            for i, (k, c) in enumerate(cuts)
        ]
        writes = [
            pltpu.make_async_copy(bufs[k].at[c], outs[k].at[c], sems.at[1, i])
            for i, (k, c) in enumerate(cuts)
        ]
        for copy in reads:
            copy.start()
        for read, write in zip(reads, writes):
            read.wait()
            write.start()
        for copy in writes:
            copy.wait()

    hbm = pl.BlockSpec(memory_space=pl.ANY)
    return pl.pallas_call(
        body,
        out_shape=tuple(jax.ShapeDtypeStruct(a.shape, a.dtype) for a in arrays),
        in_specs=[hbm] * len(arrays),
        out_specs=(hbm,) * len(arrays),
        scratch_shapes=[pltpu.VMEM(a.shape, a.dtype) for a in arrays]
        + [pltpu.SemaphoreType.DMA((2, len(cuts)))],
        compiler_params=pltpu.CompilerParams(vmem_limit_bytes=60 << 20),
    )(*arrays)


def per_device(tokens, expert_ids, live_counts, router, up_weight, down_weight, out_grad):
    width = tokens.shape[1]
    assert tokens.shape == (ROWS, C * NC) and router.shape[1] == EXPERTS
    assert up_weight.shape == (1, C * NC, H)
    vmem = pl.BlockSpec(memory_space=pltpu.VMEM)
    smem = pl.BlockSpec(memory_space=pltpu.SMEM)
    hbm = pl.BlockSpec(memory_space=pl.ANY)
    every = NT * SLOTS
    V, DMA = pltpu.VMEM, pltpu.SemaphoreType.DMA
    scratch = [
        V((NN, NZ, ZR, C), BF16),
        V((NN, NZ, ZR, C), BF16),
        V((NN, NQ, XR, C), BF16),
        V((NN, NQ, XR, C), BF16),
        V((NU, NZ, ZR, C), BF16),
        V((NU, NZ, ZR, C), BF16),
        V((NU, NQ, XR, C), BF16),
        V((NU, NQ, XR, C), BF16),
        V((NS, NT, 2 * ROWS, C), BF16),
        V((NC, NT, BOTH, C), BF16),
        V((NC, C, H), BF16),
        V((NC, H, C), BF16),
        V((every, H), F32),
        V((every, H), F32),
        V((every, H), BF16),
        V((every, H), BF16),
        V((every, EXPERTS), F32),
        V((ROWS, 128), F32),
        V((every, 128), F32),
        V((every, 128), BF16),
        V((NN, 2, SLOTS, C), BF16),
        V((NN, 2, SLOTS, C), BF16),
        V((NN, 2, BOTH, C), BF16),
        V((NN, 2, BOTH, C), BF16),
        V((NS, 2, ROWS, C), BF16),
        V((NS, 2, 2 * ROWS, C), BF16),
        V((2, C, N), BF16),
        V((2, N, C), BF16),
        V((BOTH, BOTH), BF16),
        V((BOTH, BOTH), BF16),
        V((BOTH, BOTH), BF16),
        V((BOTH, BOTH), BF16),
        V((NT, BOTH, 2 * ROWS), BF16),
        V((NT, ROWS, BOTH), BF16),
        V((NT, ROWS, BOTH), BF16),
        V((NC, 8, C), F32),
        V((NT, 1, ROWS), F32),
        V((NT, 1, width), F32),
        V((NQ, 1, width), F32),
        V((NZ, NQ, 1, width), F32),
        DMA((2, NC)),
        DMA((NN,)), DMA((NN,)), DMA((NN,)), DMA((NN,)), DMA((NN, 4)), DMA((NN, 4)),
        DMA((NN, 2)), DMA((NN, 2)), DMA((NN, 4)), DMA((NN, 4)),
        DMA((NU,)), DMA((NU,)), DMA((NU,)), DMA((NU,)), DMA((NS, 4)), DMA((NS, 4)),
        DMA((NS, 2)), DMA((NS, 2)), DMA((NS, 2)), DMA((NS, 2)),
        DMA((2, 2)),
        DMA((NT,)), DMA((NT,)), DMA((NT,)), DMA((NT,)),
        DMA((NQ,)), DMA((NQ,)), DMA((NZ,)), DMA((NZ,)),
        pltpu.SemaphoreType.REGULAR,
    ]
    S = jax.ShapeDtypeStruct
    results = pl.pallas_call(
        kernel,
        out_shape=(
            S((ROWS, width), BF16),
            S((ROWS, width), BF16),
            S((1, width, H), BF16),
            S((1, H, width), BF16),
            S((EXPERTS, width), F32),
        ),
        in_specs=[vmem, smem, vmem, vmem, vmem, hbm, hbm],
        out_specs=(vmem, vmem, hbm, hbm, vmem),
        scratch_shapes=scratch,
        compiler_params=pltpu.CompilerParams(
            collective_id=0, has_side_effects=True, vmem_limit_bytes=67043328
        ),
    )(
        expert_ids.reshape(1, ROWS), live_counts, router.T, tokens, out_grad, up_weight, down_weight
    )
    mixed, tgrad, upg, downg, rgrad = hand_over(results)
    return (mixed, tgrad, upg, downg, rgrad.T)


def solution(mesh):
    rows = P(("expert", "tensor"), None)
    in_specs = (
        rows,
        rows,
        P(("expert", "tensor")),
        P(),
        P("expert", None, "tensor"),
        P("expert", "tensor", None),
        rows,
    )
    out_specs = (rows, rows, P("expert", None, "tensor"), P("expert", "tensor", None), P())
    return jax.shard_map(
        per_device, mesh=mesh, in_specs=in_specs, out_specs=out_specs, check_vma=False
    )
```

```python
import jax
import jax.numpy as jnp
from jax import lax
from jax.experimental import pallas as pl
from jax.experimental.pallas import tpu as pltpu
from jax.sharding import PartitionSpec as P

F32, BF16, I32 = jnp.float32, jnp.bfloat16, jnp.int32
MESH = pl.DeviceIdType.MESH

NZ, NQ, NT = 4, 8, 4
EXPERTS = NZ * NQ
ROWS, MOST = 128, 6
SLOTS = EXPERTS * MOST
BOTH = 2 * SLOTS
C, NC = 512, 5
NN, NS = 3, 2
NU = NT * NS
ZR, XR = NQ * 2 * MOST, 2 * NZ * MOST
H = 1024
N = 256


OUT_STEPS = 24
OUT = dict(
    out_z=(0, 1, 2,),
    unit_box=(0, 2, 3, 4, 5, 7, 8, 10,),
    unit_z=(5, 8, 9, 10, 12, 14, 15, 16,),
    unit_x=(9, 10, 11, 14, 15, 16, 18, 22,),
    release=(22,),
    out_y=(9, 13, 14,),
    raw_on=(0, 1,),
    unit_work=(15, 17, 19,),
    away=(16, 17, 20, 22, 23,),
    out_x=(1, 5, 6,),
    near=(9, 12, 13, 14,),
    early=(20, 21, 23,),
    middle=(15, 18, 19, 23,),
)
BACK_STEPS = 23
BACK = dict(
    unit_back_x=(4, 6, 7, 9, 10, 11, 13, 15,),
    unit_back=(0, 1, 2, 3, 4, 5, 6, 9,),
    back_near=(7, 8, 10,),
    back_x=(16, 17, 19,),
    grads=(6, 12, 13, 20, 22,),
    vector_0=(6,),
    back_own=(10, 14, 15,),
    vector_2=(14,),
    unit_sum=(20, 22,),
    back_z=(20, 21, 22,),
    back_far=(1, 2, 4,),
    unit_back_z=(7, 11, 12, 13, 15, 17, 18, 19,),
    vector_1=(10,),
)


def dot(a, b, dims=((1,), (0,))):
    return lax.dot_general(a, b, (dims, ((), ())), preferred_element_type=F32)


NTD = ((1,), (1,))
TND = ((0,), (0,))


def iota(shape, axis):
    return lax.broadcasted_iota(I32, shape, axis).astype(F32)


def turn(r):
    return r + 1 - 3 * (r // 2) + 2 * (r // 3)


def at(i, steps, task):
    here = i == steps[0]
    for step in steps[1:]:
        here = here | (i == step)

    @pl.when(here)
    def _():
        k = 0
        for step in steps[1:]:
            k = k + (i + 64 - step) // 64
        task(k)


def onehot(mask):
    return jnp.where(mask, 1.0, 0.0).astype(BF16)


def div(a, b):
    return jnp.floor((a + 0.5) * (1.0 / b))


def source_1(o):
    q = div(o, 2 * NZ * MOST)
    r = o - q * (2 * NZ * MOST)
    a = div(r, NZ * MOST)
    r = r - a * (NZ * MOST)
    z = div(r, MOST)
    k = r - z * MOST
    return z * (NQ * 2 * MOST) + q * (2 * MOST) + a * MOST + k


def source_2(o):
    a = div(o, SLOTS)
    r = o - a * SLOTS
    q = div(r, NZ * MOST)
    m = r - q * (NZ * MOST)
    return q * (2 * NZ * MOST) + a * (NZ * MOST) + m


def kernel(
    ids_ref, live_ref, router_ref, tok_ref, og_ref, up_hbm, down_hbm,
    mixed_ref, tgrad_ref, upg_hbm, downg_hbm, rgrad_ref,
    box, inz, outx, inx, ubox, uinz, uoutx, uinx, raw, yb, wu, wd, hid, dh, act, hc,
    lg, gate_s, slope_s, slope3, sa, ra, sb, rb, ua, ub, gsu, gsd,
    p1, p1t, p2, p2t, plc, pltx, pltc, rrow, vt, vy, vx, vz,
    wsem, zs, zr, xs, xr, ys, yr, as_, ar, bs, br, uzs, uzr, uxs, uxr, rs, rr,
    uas, uar, ubs, ubr, gsem, vts, vtr, vys, vyr, vxs, vxr, vzs, vzr, free,
):
    me = lax.axis_index("expert")
    t = lax.axis_index("tensor")
    z, q = me // NQ, me % NQ
    lo, hi = pl.ds(0, SLOTS), pl.ds(SLOTS, SLOTS)
    rlo, rhi = pl.ds(0, ROWS), pl.ds(ROWS, ROWS)
    ZD, XD, YD = range(1, NZ), range(1, NQ), range(1, NT)

    def zpeer(d):
        return (((z + d) % NZ) * NQ + q, t)

    def xpeer(d):
        return (z * NQ + (q + d) % NQ, t)

    def ypeer(d):
        return (me, (t + d) % NT)

    def remote(src, dst, ssem, rsem, peer):
        return pltpu.make_async_remote_copy(
            src_ref=src, dst_ref=dst, send_sem=ssem, recv_sem=rsem,
            device_id=peer, device_id_type=MESH,
        )

    def piece(s):
        return pl.ds(pl.multiple_of(s * C, C), C)

    def normal(n):
        return n + (n + 1) // 2

    def special(v):
        return 1 + 3 * v

    def weights(s):
        return (
            pltpu.make_async_copy(up_hbm.at[0, piece(s), :], wu.at[s], wsem.at[0, s]),
            pltpu.make_async_copy(down_hbm.at[0, :, piece(s)], wd.at[s], wsem.at[1, s]),
        )

    def zcopy(n, d):
        return remote(box.at[n, (z + d) % NZ], inz.at[n, z], zs.at[n], zr.at[n], zpeer(d))

    def zall(n):
        some = pl.ds(0, NZ - 1)
        return remote(box.at[n, some], inz.at[n, some], zs.at[n], zr.at[n], zpeer(1))

    def xcopy(n, d):
        return remote(outx.at[n, (q + d) % NQ], inx.at[n, q], xs.at[n], xr.at[n], xpeer(d))

    def xall(n):
        some = pl.ds(0, NQ - 1)
        return remote(outx.at[n, some], inx.at[n, some], xs.at[n], xr.at[n], xpeer(1))

    def uzcopy(u, d):
        return remote(ubox.at[u, (z + d) % NZ], uinz.at[u, z], uzs.at[u], uzr.at[u], zpeer(d))

    def uzall(u):
        some = pl.ds(0, NZ - 1)
        return remote(ubox.at[u, some], uinz.at[u, some], uzs.at[u], uzr.at[u], zpeer(1))

    def uxcopy(u, d):
        return remote(uoutx.at[u, (q + d) % NQ], uinx.at[u, q], uxs.at[u], uxr.at[u], xpeer(d))

    def uxall(u):
        some = pl.ds(0, NQ - 1)
        return remote(uoutx.at[u, some], uinx.at[u, some], uxs.at[u], uxr.at[u], xpeer(1))

    SIDE = (1, NT - 1, 1, NT - 1)

    def ycopy(n, i):
        b = yb.at[normal(n)]
        src = (b.at[1], b.at[1], b.at[0, lo], b.at[2, hi])[i]
        dst = (b.at[0], b.at[2], b.at[3, lo], b.at[3, hi])[i]
        return remote(src, dst, ys.at[n, i], yr.at[n, i], ypeer(SIDE[i]))

    def rcopy(v, i):
        b = raw.at[v]
        src = (b.at[1], b.at[1], b.at[0, rlo], b.at[2, rhi])[i]
        dst = (b.at[0], b.at[2], b.at[3, rlo], b.at[3, rhi])[i]
        return remote(src, dst, rs.at[v, i], rr.at[v, i], ypeer(SIDE[i]))

    def acopy(n, i):
        return remote(sa.at[n, i], ra.at[n, i], as_.at[n, i], ar.at[n, i], ypeer(SIDE[i]))

    def bcopy(n, i):
        k, half = i % 2, (lo, hi, hi, lo)[i]
        return remote(sb.at[n, k, half], rb.at[n, k, half], bs.at[n, i], br.at[n, i], ypeer(SIDE[i]))

    def uacopy(v, i):
        src = raw.at[v, 3, (rlo, rhi)[i]]
        return remote(src, ua.at[v, i], uas.at[v, i], uar.at[v, i], ypeer(SIDE[i]))

    def ubcopy(v, i):
        return remote(raw.at[v, (2, 0)[i]], ub.at[v, i], ubs.at[v, i], ubr.at[v, i], ypeer(SIDE[i]))

    def vtcopy(d):
        return remote(vt.at[1], vt.at[(1, 0, 3, 2)[d]], vts.at[d], vtr.at[d], ypeer(d))

    def vycopy(d):
        return remote(vy.at[t], vy.at[t], vys.at[d], vyr.at[d], ypeer(d))

    def vyland(d):
        dst = vy.at[(t + NT - d) % NT]
        return remote(dst, dst, vys.at[d], vyr.at[d], ypeer(d))

    def vxcopy(d):
        return remote(vx.at[q], vx.at[q], vxs.at[d], vxr.at[d], xpeer(d))

    def vxland(d):
        dst = vx.at[(q + NQ - d) % NQ]
        return remote(dst, dst, vxs.at[d], vxr.at[d], xpeer(d))

    def vzcopy(d):
        return remote(vx, vz.at[z], vzs.at[d], vzr.at[d], zpeer(d))

    def vzland(d):
        return remote(vx, vz.at[(z + NZ - d) % NZ], vzs.at[d], vzr.at[d], zpeer(d))

    for s in range(NC):
        for copy in weights(s):
            copy.start()

    barrier = pltpu.get_barrier_semaphore()
    for peers, ds in ((zpeer, ZD), (xpeer, XD), (ypeer, YD)):
        for d in ds:
            pl.semaphore_signal(barrier, inc=1, device_id=peers(d), device_id_type=MESH)

    diag = iota((ROWS, ROWS), 0) == iota((ROWS, ROWS), 1)

    def turned(line):
        return jnp.sum(jnp.where(diag, line, 0.0), axis=1, keepdims=True)

    def both_of(s):
        cot = (gate_s[:, :1] * og_ref[:, piece(s)].astype(F32)).astype(BF16)
        return jnp.concatenate([tok_ref[:, piece(s)], cot], axis=0)

    def place(o):
        line = vt[o]
        slot = iota((BOTH, ROWS), 0)
        plc[o, :, :ROWS] = onehot(slot == line)
        plc[o, :, ROWS:] = onehot(slot == line + MOST)
        column = turned(line)
        lane = iota((ROWS, BOTH), 1)
        pltx[o] = onehot(lane == column)
        pltc[o] = onehot(lane == column + MOST)

    ids = turned(ids_ref[...].astype(F32))
    chosen = ids == iota((ROWS, EXPERTS), 1)
    logits = dot(tok_ref[...], router_ref[...], NTD)
    gate = jax.nn.sigmoid(jnp.sum(jnp.where(chosen, logits, 0.0), axis=1, keepdims=True))
    gate_s[...] = jnp.broadcast_to(gate, (ROWS, 128))
    raw[0, 1] = both_of(special(0))
    pl.semaphore_wait(barrier, NZ + NQ + NT - 3)
    rcopy(0, 0).start()
    rcopy(0, 1).start()

    tri = onehot(iota((ROWS, ROWS), 0) > iota((ROWS, ROWS), 1))
    counts = dot(tri, onehot(chosen))
    rank = jnp.sum(jnp.where(chosen, counts, 0.0), axis=1, keepdims=True)
    live = lax.broadcasted_iota(I32, (ROWS, 1), 0) < live_ref[0]
    target = jnp.where(live, ids * (2.0 * MOST) + rank, -1000.0)
    vt[1] = jnp.sum(jnp.where(diag, target, 0.0), axis=0, keepdims=True)
    raw[1, 1] = both_of(special(1))
    for d in YD:
        vtcopy(d).start()
    rcopy(1, 0).start()
    rcopy(1, 1).start()
    place(1)

    @pl.loop(0, NN)
    def _(n):
        box[n] = dot(plc[1], both_of(normal(n))).astype(BF16).reshape(NZ, ZR, C)
        for d in ZD:
            zcopy(n, d).start()
        inz[n, z] = box[n, z]

    column, line = iota((BOTH, 1), 0), iota((1, BOTH), 1)
    across, down = iota((BOTH, BOTH), 1), iota((BOTH, BOTH), 0)
    p1[...] = onehot(source_1(column) == across)
    p1t[...] = onehot(source_1(line) == down)
    p2[...] = onehot(source_2(column) == across)
    p2t[...] = onehot(source_2(line) == down)
    for d in YD:
        vtcopy(d).wait_recv()
        place((1, 0, 3, 2)[d])

    hid[...] = jnp.zeros_like(hid)
    dh[...] = jnp.zeros_like(dh)
    lg[...] = jnp.zeros_like(lg)
    own = onehot(iota((8, EXPERTS), 1) == me.astype(F32))

    @pl.loop(0, NC)
    def _(s):
        rrow[s] = dot(own, router_ref[:, piece(s)])

    def rows_of(s):
        return yb[s, :, :SLOTS, :].reshape(NT * SLOTS, C)

    def cots_of(s):
        return yb[s, :, SLOTS:, :].reshape(NT * SLOTS, C)

    def order(perm, rows, shape):
        return dot(perm[...], rows.reshape(BOTH, C)).astype(BF16).reshape(shape)

    def out_z(n):
        zall(n).wait_recv()
        outx[n] = order(p1, inz[n], (NQ, XR, C))
        for d in XD:
            xcopy(n, d).start()
        inx[n, q] = outx[n, q]

    def out_x(n):
        xall(n).wait_recv()
        yb[normal(n), 1] = order(p2, inx[n], (BOTH, C))
        ycopy(n, 0).start()
        ycopy(n, 1).start()

    def out_y(n):
        ycopy(n, 0).wait_recv()
        ycopy(n, 2).start()
        ycopy(n, 1).wait_recv()
        ycopy(n, 3).start()

    def raw_on(v):
        rcopy(v, 0).wait_recv()
        rcopy(v, 2).start()
        rcopy(v, 1).wait_recv()
        rcopy(v, 3).start()

    def unit_box(u):
        v, r = u // NT, u % NT

        @pl.when(r == 3)
        def _():
            rcopy(v, 2).wait_recv()
            rcopy(v, 3).wait_recv()

        o = turn(r)
        ubox[u] = dot(plc[o], raw[v, o]).astype(BF16).reshape(NZ, ZR, C)
        for d in ZD:
            uzcopy(u, d).start()
        uinz[u, z] = ubox[u, z]

    def unit_z(u):
        uzall(u).wait_recv()
        uoutx[u] = order(p1, uinz[u], (NQ, XR, C))
        for d in XD:
            uxcopy(u, d).start()
        uinx[u, q] = uoutx[u, q]

    def unit_x(u):
        uxall(u).wait_recv()
        yb[special(u // NT), turn(u % NT)] = order(p2, uinx[u], (BOTH, C))

    def release(_):
        for peers, ds in ((zpeer, ZD), (xpeer, XD)):
            for d in ds:
                pl.semaphore_signal(free, inc=1, device_id=peers(d), device_id_type=MESH)

    def work(s, first, count):
        size = count * SLOTS
        r = pl.ds(pl.multiple_of(first * SLOTS, SLOTS), size)
        rows = yb[s, pl.ds(first, count), :SLOTS, :].reshape(size, C)
        cots = yb[s, pl.ds(first, count), SLOTS:, :].reshape(size, C)
        lg[r, :] += dot(rows, router_ref[:, piece(s)], NTD)

        @pl.loop(0, H // N)
        def _(n):
            part = pl.ds(pl.multiple_of(n * N, N), N)
            hid[r, part] += dot(rows, wu[s, :, part])
            dh[r, part] += dot(cots, wd[s, part, :], NTD)

    def near(s):
        for copy in weights(s):
            copy.wait()
        work(s, 0, 3)

    def unit_work(r):
        s = special(NS - 1)

        @pl.when(r == 0)
        def _():
            for copy in weights(s):
                copy.wait()

        work(s, turn(r), 1)

    def away(s):
        for n in range(NN):

            @pl.when(s == normal(n))
            def _():
                ycopy(n, 2).wait_recv()
                ycopy(n, 3).wait_recv()

        work(s, 3, 1)

    BR = 32

    def middle(k):
        o = turn(k)

        @pl.loop(0, SLOTS // BR)
        def _(b):
            silu_rows(pl.ds(pl.multiple_of(o * SLOTS + b * BR, BR), BR))

    def silu_rows(r):
        v, back = hid[r, :], dh[r, :]
        sig = 1.0 / (1.0 + jnp.exp(-v))
        a = (v * sig).astype(BF16)
        act[r, :] = a
        hc[r, :] = (back * (sig * (1.0 + v * (1.0 - sig)))).astype(BF16)
        part = jnp.sum(a.astype(F32) * back, axis=1, keepdims=True)
        mine = iota((BR, EXPERTS), 1) == me.astype(F32)
        logit = jnp.sum(jnp.where(mine, lg[r, :], 0.0), axis=1, keepdims=True)
        slope = part * (1.0 - 1.0 / (1.0 + jnp.exp(-logit)))
        slope_s[r, :] = jnp.broadcast_to(slope, (BR, 128))
        s1 = slope.astype(BF16).astype(F32)
        s2 = (slope - s1).astype(BF16).astype(F32)
        s3 = slope - s1 - s2
        k = iota((BR, 128), 1)
        slope3[r, :] = jnp.where(
            k == 0.0, s1, jnp.where(k == 1.0, s2, jnp.where(k == 2.0, s3, 0.0))
        ).astype(BF16)

    def value_of(s, o):
        r = pl.ds(pl.multiple_of(o * SLOTS, SLOTS), SLOTS)
        return dot(act[r, :], wd[s])

    def grad_of(s, o):
        r = pl.ds(pl.multiple_of(o * SLOTS, SLOTS), SLOTS)
        return dot(hc[r, :], wu[s], NTD) + slope_s[r, :1] * rrow[s, :1, :]

    def early(n):
        s = normal(n)
        sb[n, 0, hi] = grad_of(s, 2).astype(BF16)
        bcopy(n, 2).start()
        sb[n, 1, lo] = value_of(s, 0).astype(BF16)
        bcopy(n, 3).start()

    @pl.loop(0, OUT_STEPS)
    def _(i):
        for task in (
            out_z, unit_box, unit_z, unit_x, release, out_y, raw_on, unit_work, away, out_x, near, early, middle,
        ):
            at(i, OUT[task.__name__], task)

    def back_far(n):
        s = normal(n)
        sa[n, 0] = value_of(s, 3).astype(BF16)
        acopy(n, 0).start()
        sa[n, 1] = grad_of(s, 3).astype(BF16)
        acopy(n, 1).start()

    def back_near(n):
        s = normal(n)
        value = value_of(s, 2)
        acopy(n, 0).wait_recv()
        sb[n, 0, lo] = (value + ra[n, 0].astype(F32)).astype(BF16)
        bcopy(n, 0).start()
        grad = grad_of(s, 0)
        acopy(n, 1).wait_recv()
        sb[n, 1, hi] = (grad + ra[n, 1].astype(F32)).astype(BF16)
        bcopy(n, 1).start()

    def back_own(n):
        value, grad = value_of(normal(n), 1), grad_of(normal(n), 1)
        for i in range(4):
            bcopy(n, i).wait_recv()
        value = value + rb[n, 0, :SLOTS, :].astype(F32) + rb[n, 1, :SLOTS, :].astype(F32)
        grad = grad + rb[n, 0, SLOTS:, :].astype(F32) + rb[n, 1, SLOTS:, :].astype(F32)
        both = jnp.concatenate([value, grad], axis=0).astype(BF16)
        xall(n).wait_send()
        outx[n] = order(p2t, both, (NQ, XR, C))
        for d in XD:
            xcopy(n, d).start()
        inx[n, q] = outx[n, q]

    def back_x(n):
        xall(n).wait_recv()
        zall(n).wait_send()
        box[n] = order(p1t, inx[n], (NZ, ZR, C))
        for d in ZD:
            zcopy(n, d).start()
        inz[n, z] = box[n, z]

    def back_z(n):
        zall(n).wait_recv()
        got = inz[n].reshape(BOTH, C)
        cols = piece(normal(n))
        mixed_ref[:, cols] = (gate_s[:, :1] * dot(pltx[1], got)).astype(BF16)
        tgrad_ref[:, cols] = dot(pltc[1], got).astype(BF16)

    def unit_back(u):
        s, o = special(u // NT), turn(3 - u % NT)
        value, grad = value_of(s, o), grad_of(s, o)
        both = jnp.concatenate([value, grad], axis=0).astype(BF16)
        uxall(u).wait_send()
        uoutx[u] = order(p2t, both, (NQ, XR, C))

        @pl.when(u == 0)
        def _():
            pl.semaphore_wait(free, NZ + NQ - 2)

        for d in XD:
            uxcopy(u, d).start()
        uinx[u, q] = uoutx[u, q]

    def unit_back_x(u):
        uxall(u).wait_recv()
        uzall(u).wait_send()
        ubox[u] = order(p1t, uinx[u], (NZ, ZR, C))
        for d in ZD:
            uzcopy(u, d).start()
        uinz[u, z] = ubox[u, z]

    def unit_back_z(u):
        uzall(u).wait_recv()
        v, r = u // NT, u % NT

        @pl.when(r == 0)
        def _():
            for i in range(4):
                rcopy(v, i).wait_send()

        o = turn(3 - r)
        got = uinz[u].reshape(BOTH, C)
        raw[v, o, rlo] = dot(pltx[o], got).astype(BF16)
        raw[v, o, rhi] = dot(pltc[o], got).astype(BF16)

        @pl.when(r == 0)
        def _():
            uacopy(v, 0).start()
            uacopy(v, 1).start()

        @pl.when(r == 1)
        def _():
            uacopy(v, 1).wait_recv()
            raw[v, 0, rhi] = (raw[v, 0, rhi].astype(F32) + ua[v, 1].astype(F32)).astype(BF16)
            ubcopy(v, 1).start()

        @pl.when(r == 2)
        def _():
            uacopy(v, 0).wait_recv()
            raw[v, 2, rlo] = (raw[v, 2, rlo].astype(F32) + ua[v, 0].astype(F32)).astype(BF16)
            ubcopy(v, 0).start()

    def unit_sum(v):
        ubcopy(v, 0).wait_recv()
        ubcopy(v, 1).wait_recv()
        got = raw[v, 1].astype(F32) + ub[v, 0].astype(F32) + ub[v, 1].astype(F32)
        cols = piece(special(v))
        value = got[:ROWS].astype(BF16).astype(F32)
        mixed_ref[:, cols] = (gate_s[:, :1] * value).astype(BF16)
        tgrad_ref[:, cols] = got[ROWS:].astype(BF16)

    def grads_out(s, n):
        part = pl.ds(pl.multiple_of(n * N, N), N)
        k = n % 2
        return (
            pltpu.make_async_copy(gsu.at[k], upg_hbm.at[0, piece(s), part], gsem.at[0, k]),
            pltpu.make_async_copy(gsd.at[k], downg_hbm.at[0, part, piece(s)], gsem.at[1, k]),
        )

    def grads(s):
        @pl.loop(0, H // N)
        def _(n):
            @pl.when((s > 0) | (n >= 2))
            def _():
                for copy in grads_out(s, n):
                    copy.wait()

            part = pl.ds(pl.multiple_of(n * N, N), N)
            gsd[n % 2] = dot(act[:, part], cots_of(s), TND).astype(BF16)
            gsu[n % 2] = dot(rows_of(s), hc[:, part], TND).astype(BF16)
            for copy in grads_out(s, n):
                copy.start()

    def vector_0(_):
        @pl.loop(0, NC)
        def _(s):
            three = dot(slope3[...], rows_of(s), TND)
            vy[t, :, piece(s)] = jnp.sum(three, axis=0, keepdims=True)

        for d in YD:
            vycopy(d).start()

    def vector_1(_):
        for d in YD:
            vyland(d).wait_recv()
        vx[q] = (vy[0] + vy[1]) + (vy[2] + vy[3])
        for d in XD:
            vxcopy(d).start()

    def vector_2(_):
        for d in XD:
            vxland(d).wait_recv()
        for d in ZD:
            vzcopy(d).start()
        vz[z] = vx[...]

    @pl.loop(0, BACK_STEPS)
    def _(i):
        for task in (
            unit_back_x, unit_back, back_near, back_x, grads, vector_0, back_own, vector_2, unit_sum, back_z, back_far, unit_back_z, vector_1,
        ):
            at(i, BACK[task.__name__], task)

    for d in ZD:
        vzland(d).wait_recv()
    rgrad_ref[...] = vz[...].reshape(EXPERTS, C * NC)
    for d in YD:
        vtcopy(d).wait_send()
        vycopy(d).wait_send()
    for d in XD:
        vxcopy(d).wait_send()
    for d in ZD:
        vzcopy(d).wait_send()

    @pl.loop(0, NN)
    def _(n):
        for i in range(4):
            ycopy(n, i).wait_send()
            bcopy(n, i).wait_send()
        for i in range(2):
            acopy(n, i).wait_send()
        xall(n).wait_send()
        zall(n).wait_send()

    @pl.loop(0, NU)
    def _(u):
        uxall(u).wait_send()
        uzall(u).wait_send()

    @pl.loop(0, NS)
    def _(v):
        for i in range(2):
            uacopy(v, i).wait_send()
            ubcopy(v, i).wait_send()

    for n in range(2):
        for copy in grads_out(NC - 1, n):
            copy.wait()


def hand_over(arrays):
    cuts = []
    for k, a in enumerate(arrays):
        axis = len(a.shape) - 2
        parts = 4 if a.size > 1 << 20 else 1
        size = a.shape[axis] // parts
        cuts += [(k, (slice(None),) * axis + (pl.ds(p * size, size),)) for p in range(parts)]

    def body(*refs):
        n = len(arrays)
        ins, outs, bufs, sems = refs[:n], refs[n : 2 * n], refs[2 * n : 3 * n], refs[3 * n]
        reads = [
            pltpu.make_async_copy(ins[k].at[c], bufs[k].at[c], sems.at[0, i])
            for i, (k, c) in enumerate(cuts)
        ]
        writes = [
            pltpu.make_async_copy(bufs[k].at[c], outs[k].at[c], sems.at[1, i])
            for i, (k, c) in enumerate(cuts)
        ]
        for copy in reads:
            copy.start()
        for read, write in zip(reads, writes):
            read.wait()
            write.start()
        for copy in writes:
            copy.wait()

    hbm = pl.BlockSpec(memory_space=pl.ANY)
    return pl.pallas_call(
        body,
        out_shape=tuple(jax.ShapeDtypeStruct(a.shape, a.dtype) for a in arrays),
        in_specs=[hbm] * len(arrays),
        out_specs=(hbm,) * len(arrays),
        scratch_shapes=[pltpu.VMEM(a.shape, a.dtype) for a in arrays]
        + [pltpu.SemaphoreType.DMA((2, len(cuts)))],
        compiler_params=pltpu.CompilerParams(vmem_limit_bytes=60 << 20),
    )(*arrays)


def per_device(tokens, expert_ids, live_counts, router, up_weight, down_weight, out_grad):
    width = tokens.shape[1]
    assert tokens.shape == (ROWS, C * NC) and router.shape[1] == EXPERTS
    assert up_weight.shape == (1, C * NC, H)
    vmem = pl.BlockSpec(memory_space=pltpu.VMEM)
    smem = pl.BlockSpec(memory_space=pltpu.SMEM)
    hbm = pl.BlockSpec(memory_space=pl.ANY)
    every = NT * SLOTS
    V, DMA = pltpu.VMEM, pltpu.SemaphoreType.DMA
    scratch = [
        V((NN, NZ, ZR, C), BF16),
        V((NN, NZ, ZR, C), BF16),
        V((NN, NQ, XR, C), BF16),
        V((NN, NQ, XR, C), BF16),
        V((NU, NZ, ZR, C), BF16),
        V((NU, NZ, ZR, C), BF16),
        V((NU, NQ, XR, C), BF16),
        V((NU, NQ, XR, C), BF16),
        V((NS, NT, 2 * ROWS, C), BF16),
        V((NC, NT, BOTH, C), BF16),
        V((NC, C, H), BF16),
        V((NC, H, C), BF16),
        V((every, H), F32),
        V((every, H), F32),
        V((every, H), BF16),
        V((every, H), BF16),
        V((every, EXPERTS), F32),
        V((ROWS, 128), F32),
        V((every, 128), F32),
        V((every, 128), BF16),
        V((NN, 2, SLOTS, C), BF16),
        V((NN, 2, SLOTS, C), BF16),
        V((NN, 2, BOTH, C), BF16),
        V((NN, 2, BOTH, C), BF16),
        V((NS, 2, ROWS, C), BF16),
        V((NS, 2, 2 * ROWS, C), BF16),
        V((2, C, N), BF16),
        V((2, N, C), BF16),
        V((BOTH, BOTH), BF16),
        V((BOTH, BOTH), BF16),
        V((BOTH, BOTH), BF16),
        V((BOTH, BOTH), BF16),
        V((NT, BOTH, 2 * ROWS), BF16),
        V((NT, ROWS, BOTH), BF16),
        V((NT, ROWS, BOTH), BF16),
        V((NC, 8, C), F32),
        V((NT, 1, ROWS), F32),
        V((NT, 1, width), F32),
        V((NQ, 1, width), F32),
        V((NZ, NQ, 1, width), F32),
        DMA((2, NC)),
        DMA((NN,)), DMA((NN,)), DMA((NN,)), DMA((NN,)), DMA((NN, 4)), DMA((NN, 4)),
        DMA((NN, 2)), DMA((NN, 2)), DMA((NN, 4)), DMA((NN, 4)),
        DMA((NU,)), DMA((NU,)), DMA((NU,)), DMA((NU,)), DMA((NS, 4)), DMA((NS, 4)),
        DMA((NS, 2)), DMA((NS, 2)), DMA((NS, 2)), DMA((NS, 2)),
        DMA((2, 2)),
        DMA((NT,)), DMA((NT,)), DMA((NT,)), DMA((NT,)),
        DMA((NQ,)), DMA((NQ,)), DMA((NZ,)), DMA((NZ,)),
        pltpu.SemaphoreType.REGULAR,
    ]
    S = jax.ShapeDtypeStruct
    results = pl.pallas_call(
        kernel,
        out_shape=(
            S((ROWS, width), BF16),
            S((ROWS, width), BF16),
            S((1, width, H), BF16),
            S((1, H, width), BF16),
            S((EXPERTS, width), F32),
        ),
        in_specs=[vmem, smem, vmem, vmem, vmem, hbm, hbm],
        out_specs=(vmem, vmem, hbm, hbm, vmem),
        scratch_shapes=scratch,
        compiler_params=pltpu.CompilerParams(
            collective_id=0, has_side_effects=True, vmem_limit_bytes=67043328
        ),
    )(
        expert_ids.reshape(1, ROWS), live_counts, router.T, tokens, out_grad, up_weight, down_weight
    )
    mixed, tgrad, upg, downg, rgrad = hand_over(results)
    return (mixed, tgrad, upg, downg, rgrad.T)


def solution(mesh):
    rows = P(("expert", "tensor"), None)
    in_specs = (
        rows,
        rows,
        P(("expert", "tensor")),
        P(),
        P("expert", None, "tensor"),
        P("expert", "tensor", None),
        rows,
    )
    out_specs = (rows, rows, P("expert", None, "tensor"), P("expert", "tensor", None), P())
    return jax.shard_map(
        per_device, mesh=mesh, in_specs=in_specs, out_specs=out_specs, check_vma=False
    )
```

```python
import jax
import jax.numpy as jnp
from jax import lax
from jax.experimental import pallas as pl
from jax.experimental.pallas import tpu as pltpu
from jax.sharding import PartitionSpec as P

F32, BF16, I32 = jnp.float32, jnp.bfloat16, jnp.int32
MESH = pl.DeviceIdType.MESH

NZ, NQ, NT = 4, 8, 4
EXPERTS = NZ * NQ
ROWS, MOST = 128, 6
SLOTS = EXPERTS * MOST
BOTH = 2 * SLOTS
C, NC = 512, 5
NN, NS = 3, 2
NU = NT * NS
ZR, XR = NQ * 2 * MOST, 2 * NZ * MOST
H = 1024
N = 256


OUT_STEPS = 24
OUT = dict(
    out_z=(0, 1, 2,),
    unit_box=(0, 2, 3, 4, 5, 7, 8, 10,),
    unit_z=(5, 8, 9, 10, 12, 14, 15, 16,),
    unit_x=(9, 10, 11, 14, 15, 16, 18, 22,),
    release=(22,),
    out_y=(9, 13, 14,),
    raw_on=(0, 1,),
    unit_work=(15, 17, 19,),
    away=(16, 17, 20, 22, 23,),
    out_x=(1, 5, 6,),
    near=(9, 12, 13, 14,),
    early=(20, 21, 23,),
    middle=(15, 18, 19, 23,),
)
BACK_STEPS = 23
BACK = dict(
    unit_back_x=(4, 6, 7, 9, 10, 11, 13, 15,),
    unit_back=(0, 1, 2, 3, 4, 5, 6, 9,),
    back_near=(7, 8, 10,),
    back_x=(16, 17, 19,),
    grads=(6, 12, 13, 20, 22,),
    vector_0=(6,),
    back_own=(10, 14, 15,),
    vector_2=(14,),
    unit_sum=(20, 22,),
    back_z=(20, 21, 22,),
    back_far=(1, 2, 4,),
    unit_back_z=(7, 11, 12, 13, 15, 17, 18, 19,),
    vector_1=(10,),
)


def dot(a, b, dims=((1,), (0,))):
    return lax.dot_general(a, b, (dims, ((), ())), preferred_element_type=F32)


NTD = ((1,), (1,))
TND = ((0,), (0,))


def iota(shape, axis):
    return lax.broadcasted_iota(I32, shape, axis).astype(F32)


def turn(r):
    return r + 1 - 3 * (r // 2) + 2 * (r // 3)


def at(i, steps, task):
    here = i == steps[0]
    for step in steps[1:]:
        here = here | (i == step)

    @pl.when(here)
    def _():
        k = 0
        for step in steps[1:]:
            k = k + (i + 64 - step) // 64
        task(k)


def onehot(mask):
    return jnp.where(mask, 1.0, 0.0).astype(BF16)


def div(a, b):
    return jnp.floor((a + 0.5) * (1.0 / b))


def source_1(o):
    q = div(o, 2 * NZ * MOST)
    r = o - q * (2 * NZ * MOST)
    a = div(r, NZ * MOST)
    r = r - a * (NZ * MOST)
    z = div(r, MOST)
    k = r - z * MOST
    return z * (NQ * 2 * MOST) + q * (2 * MOST) + a * MOST + k


def source_2(o):
    a = div(o, SLOTS)
    r = o - a * SLOTS
    q = div(r, NZ * MOST)
    m = r - q * (NZ * MOST)
    return q * (2 * NZ * MOST) + a * (NZ * MOST) + m


def kernel(
    ids_ref, live_ref, router_ref, tok_hbm, og_hbm, up_hbm, down_hbm,
    mixed_ref, tgrad_ref, upg_hbm, downg_hbm, rgrad_ref,
    tok_ref, og_ref, box, inz, outx, inx, ubox, uinz, uoutx, uinx, raw, yb, wu, wd, hid, dh, act, hc,
    lg, gate_s, slope_s, slope3, sa, ra, sb, rb, ua, ub, gsu, gsd,
    p1, p1t, p2, p2t, plc, pltx, pltc, rrow, vt, vy, vx, vz,
    tsem, wsem, zs, zr, xs, xr, ys, yr, as_, ar, bs, br, uzs, uzr, uxs, uxr, rs, rr,
    uas, uar, ubs, ubr, gsem, vts, vtr, vys, vyr, vxs, vxr, vzs, vzr, free,
):
    me = lax.axis_index("expert")
    t = lax.axis_index("tensor")
    z, q = me // NQ, me % NQ
    lo, hi = pl.ds(0, SLOTS), pl.ds(SLOTS, SLOTS)
    rlo, rhi = pl.ds(0, ROWS), pl.ds(ROWS, ROWS)
    ZD, XD, YD = range(1, NZ), range(1, NQ), range(1, NT)

    def zpeer(d):
        return (((z + d) % NZ) * NQ + q, t)

    def xpeer(d):
        return (z * NQ + (q + d) % NQ, t)

    def ypeer(d):
        return (me, (t + d) % NT)

    def remote(src, dst, ssem, rsem, peer):
        return pltpu.make_async_remote_copy(
            src_ref=src, dst_ref=dst, send_sem=ssem, recv_sem=rsem,
            device_id=peer, device_id_type=MESH,
        )

    def piece(s):
        return pl.ds(pl.multiple_of(s * C, C), C)

    def normal(n):
        return n + (n + 1) // 2

    def special(v):
        return 1 + 3 * v

    def weights(s):
        return (
            pltpu.make_async_copy(up_hbm.at[0, piece(s), :], wu.at[s], wsem.at[0, s]),
            pltpu.make_async_copy(down_hbm.at[0, :, piece(s)], wd.at[s], wsem.at[1, s]),
        )

    def zcopy(n, d):
        return remote(box.at[n, (z + d) % NZ], inz.at[n, z], zs.at[n], zr.at[n], zpeer(d))

    def zall(n):
        some = pl.ds(0, NZ - 1)
        return remote(box.at[n, some], inz.at[n, some], zs.at[n], zr.at[n], zpeer(1))

    def xcopy(n, d):
        return remote(outx.at[n, (q + d) % NQ], inx.at[n, q], xs.at[n], xr.at[n], xpeer(d))

    def xall(n):
        some = pl.ds(0, NQ - 1)
        return remote(outx.at[n, some], inx.at[n, some], xs.at[n], xr.at[n], xpeer(1))

    def uzcopy(u, d):
        return remote(ubox.at[u, (z + d) % NZ], uinz.at[u, z], uzs.at[u], uzr.at[u], zpeer(d))

    def uzall(u):
        some = pl.ds(0, NZ - 1)
        return remote(ubox.at[u, some], uinz.at[u, some], uzs.at[u], uzr.at[u], zpeer(1))

    def uxcopy(u, d):
        return remote(uoutx.at[u, (q + d) % NQ], uinx.at[u, q], uxs.at[u], uxr.at[u], xpeer(d))

    def uxall(u):
        some = pl.ds(0, NQ - 1)
        return remote(uoutx.at[u, some], uinx.at[u, some], uxs.at[u], uxr.at[u], xpeer(1))

    SIDE = (1, NT - 1, 1, NT - 1)

    def ycopy(n, i):
        b = yb.at[normal(n)]
        src = (b.at[1], b.at[1], b.at[0, lo], b.at[2, hi])[i]
        dst = (b.at[0], b.at[2], b.at[3, lo], b.at[3, hi])[i]
        return remote(src, dst, ys.at[n, i], yr.at[n, i], ypeer(SIDE[i]))

    def rcopy(v, i):
        b = raw.at[v]
        src = (b.at[1], b.at[1], b.at[0, rlo], b.at[2, rhi])[i]
        dst = (b.at[0], b.at[2], b.at[3, rlo], b.at[3, rhi])[i]
        return remote(src, dst, rs.at[v, i], rr.at[v, i], ypeer(SIDE[i]))

    def acopy(n, i):
        return remote(sa.at[n, i], ra.at[n, i], as_.at[n, i], ar.at[n, i], ypeer(SIDE[i]))

    def bcopy(n, i):
        k, half = i % 2, (lo, hi, hi, lo)[i]
        return remote(sb.at[n, k, half], rb.at[n, k, half], bs.at[n, i], br.at[n, i], ypeer(SIDE[i]))

    def uacopy(v, i):
        src = raw.at[v, 3, (rlo, rhi)[i]]
        return remote(src, ua.at[v, i], uas.at[v, i], uar.at[v, i], ypeer(SIDE[i]))

    def ubcopy(v, i):
        return remote(raw.at[v, (2, 0)[i]], ub.at[v, i], ubs.at[v, i], ubr.at[v, i], ypeer(SIDE[i]))

    def vtcopy(d):
        return remote(vt.at[1], vt.at[(1, 0, 3, 2)[d]], vts.at[d], vtr.at[d], ypeer(d))

    def vycopy(d):
        return remote(vy.at[t], vy.at[t], vys.at[d], vyr.at[d], ypeer(d))

    def vyland(d):
        dst = vy.at[(t + NT - d) % NT]
        return remote(dst, dst, vys.at[d], vyr.at[d], ypeer(d))

    def vxcopy(d):
        return remote(vx.at[q], vx.at[q], vxs.at[d], vxr.at[d], xpeer(d))

    def vxland(d):
        dst = vx.at[(q + NQ - d) % NQ]
        return remote(dst, dst, vxs.at[d], vxr.at[d], xpeer(d))

    def vzcopy(d):
        return remote(vx, vz.at[z], vzs.at[d], vzr.at[d], zpeer(d))

    def vzland(d):
        return remote(vx, vz.at[(z + NZ - d) % NZ], vzs.at[d], vzr.at[d], zpeer(d))

    rows_in = (
        pltpu.make_async_copy(tok_hbm, tok_ref, tsem.at[0]),
        pltpu.make_async_copy(og_hbm, og_ref, tsem.at[1]),
    )
    for copy in rows_in:
        copy.start()

    barrier = pltpu.get_barrier_semaphore()
    for peers, ds in ((zpeer, ZD), (xpeer, XD), (ypeer, YD)):
        for d in ds:
            pl.semaphore_signal(barrier, inc=1, device_id=peers(d), device_id_type=MESH)

    for s in range(NC):
        for copy in weights(s):
            copy.start()
    for copy in rows_in:
        copy.wait()

    diag = iota((ROWS, ROWS), 0) == iota((ROWS, ROWS), 1)

    def turned(line):
        return jnp.sum(jnp.where(diag, line, 0.0), axis=1, keepdims=True)

    def both_of(s):
        cot = (gate_s[:, :1] * og_ref[:, piece(s)].astype(F32)).astype(BF16)
        return jnp.concatenate([tok_ref[:, piece(s)], cot], axis=0)

    def place(o):
        line = vt[o]
        slot = iota((BOTH, ROWS), 0)
        plc[o, :, :ROWS] = onehot(slot == line)
        plc[o, :, ROWS:] = onehot(slot == line + MOST)
        column = turned(line)
        lane = iota((ROWS, BOTH), 1)
        pltx[o] = onehot(lane == column)
        pltc[o] = onehot(lane == column + MOST)

    ids = turned(ids_ref[...].astype(F32))
    chosen = ids == iota((ROWS, EXPERTS), 1)
    logits = dot(tok_ref[...], router_ref[...], NTD)
    gate = jax.nn.sigmoid(jnp.sum(jnp.where(chosen, logits, 0.0), axis=1, keepdims=True))
    gate_s[...] = jnp.broadcast_to(gate, (ROWS, 128))
    raw[0, 1] = both_of(special(0))
    pl.semaphore_wait(barrier, NZ + NQ + NT - 3)
    rcopy(0, 0).start()
    rcopy(0, 1).start()

    tri = onehot(iota((ROWS, ROWS), 0) > iota((ROWS, ROWS), 1))
    counts = dot(tri, onehot(chosen))
    rank = jnp.sum(jnp.where(chosen, counts, 0.0), axis=1, keepdims=True)
    live = lax.broadcasted_iota(I32, (ROWS, 1), 0) < live_ref[0]
    target = jnp.where(live, ids * (2.0 * MOST) + rank, -1000.0)
    vt[1] = jnp.sum(jnp.where(diag, target, 0.0), axis=0, keepdims=True)
    raw[1, 1] = both_of(special(1))
    for d in YD:
        vtcopy(d).start()
    rcopy(1, 0).start()
    rcopy(1, 1).start()
    place(1)

    @pl.loop(0, NN)
    def _(n):
        box[n] = dot(plc[1], both_of(normal(n))).astype(BF16).reshape(NZ, ZR, C)
        for d in ZD:
            zcopy(n, d).start()
        inz[n, z] = box[n, z]

    column, line = iota((BOTH, 1), 0), iota((1, BOTH), 1)
    across, down = iota((BOTH, BOTH), 1), iota((BOTH, BOTH), 0)
    p1[...] = onehot(source_1(column) == across)
    p1t[...] = onehot(source_1(line) == down)
    p2[...] = onehot(source_2(column) == across)
    p2t[...] = onehot(source_2(line) == down)
    for d in YD:
        vtcopy(d).wait_recv()
        place((1, 0, 3, 2)[d])

    hid[...] = jnp.zeros_like(hid)
    dh[...] = jnp.zeros_like(dh)
    lg[...] = jnp.zeros_like(lg)
    own = onehot(iota((8, EXPERTS), 1) == me.astype(F32))

    @pl.loop(0, NC)
    def _(s):
        rrow[s] = dot(own, router_ref[:, piece(s)])

    def rows_of(s):
        return yb[s, :, :SLOTS, :].reshape(NT * SLOTS, C)

    def cots_of(s):
        return yb[s, :, SLOTS:, :].reshape(NT * SLOTS, C)

    def order(perm, rows, shape):
        return dot(perm[...], rows.reshape(BOTH, C)).astype(BF16).reshape(shape)

    def out_z(n):
        zall(n).wait_recv()
        outx[n] = order(p1, inz[n], (NQ, XR, C))
        for d in XD:
            xcopy(n, d).start()
        inx[n, q] = outx[n, q]

    def out_x(n):
        xall(n).wait_recv()
        yb[normal(n), 1] = order(p2, inx[n], (BOTH, C))
        ycopy(n, 0).start()
        ycopy(n, 1).start()

    def out_y(n):
        ycopy(n, 0).wait_recv()
        ycopy(n, 2).start()
        ycopy(n, 1).wait_recv()
        ycopy(n, 3).start()

    def raw_on(v):
        rcopy(v, 0).wait_recv()
        rcopy(v, 2).start()
        rcopy(v, 1).wait_recv()
        rcopy(v, 3).start()

    def unit_box(u):
        v, r = u // NT, u % NT

        @pl.when(r == 3)
        def _():
            rcopy(v, 2).wait_recv()
            rcopy(v, 3).wait_recv()

        o = turn(r)
        ubox[u] = dot(plc[o], raw[v, o]).astype(BF16).reshape(NZ, ZR, C)
        for d in ZD:
            uzcopy(u, d).start()
        uinz[u, z] = ubox[u, z]

    def unit_z(u):
        uzall(u).wait_recv()
        uoutx[u] = order(p1, uinz[u], (NQ, XR, C))
        for d in XD:
            uxcopy(u, d).start()
        uinx[u, q] = uoutx[u, q]

    def unit_x(u):
        uxall(u).wait_recv()
        yb[special(u // NT), turn(u % NT)] = order(p2, uinx[u], (BOTH, C))

    def release(_):
        for peers, ds in ((zpeer, ZD), (xpeer, XD)):
            for d in ds:
                pl.semaphore_signal(free, inc=1, device_id=peers(d), device_id_type=MESH)

    def work(s, first, count):
        size = count * SLOTS
        r = pl.ds(pl.multiple_of(first * SLOTS, SLOTS), size)
        rows = yb[s, pl.ds(first, count), :SLOTS, :].reshape(size, C)
        cots = yb[s, pl.ds(first, count), SLOTS:, :].reshape(size, C)
        lg[r, :] += dot(rows, router_ref[:, piece(s)], NTD)

        @pl.loop(0, H // N)
        def _(n):
            part = pl.ds(pl.multiple_of(n * N, N), N)
            hid[r, part] += dot(rows, wu[s, :, part])
            dh[r, part] += dot(cots, wd[s, part, :], NTD)

    def near(s):
        for copy in weights(s):
            copy.wait()
        work(s, 0, 3)

    def unit_work(r):
        s = special(NS - 1)

        @pl.when(r == 0)
        def _():
            for copy in weights(s):
                copy.wait()

        work(s, turn(r), 1)

    def away(s):
        for n in range(NN):

            @pl.when(s == normal(n))
            def _():
                ycopy(n, 2).wait_recv()
                ycopy(n, 3).wait_recv()

        work(s, 3, 1)

    BR = 32

    def middle(k):
        o = turn(k)

        @pl.loop(0, SLOTS // BR)
        def _(b):
            silu_rows(pl.ds(pl.multiple_of(o * SLOTS + b * BR, BR), BR))

    def silu_rows(r):
        v, back = hid[r, :], dh[r, :]
        sig = 1.0 / (1.0 + jnp.exp(-v))
        a = (v * sig).astype(BF16)
        act[r, :] = a
        hc[r, :] = (back * (sig * (1.0 + v * (1.0 - sig)))).astype(BF16)
        part = jnp.sum(a.astype(F32) * back, axis=1, keepdims=True)
        mine = iota((BR, EXPERTS), 1) == me.astype(F32)
        logit = jnp.sum(jnp.where(mine, lg[r, :], 0.0), axis=1, keepdims=True)
        slope = part * (1.0 - 1.0 / (1.0 + jnp.exp(-logit)))
        slope_s[r, :] = jnp.broadcast_to(slope, (BR, 128))
        s1 = slope.astype(BF16).astype(F32)
        s2 = (slope - s1).astype(BF16).astype(F32)
        s3 = slope - s1 - s2
        k = iota((BR, 128), 1)
        slope3[r, :] = jnp.where(
            k == 0.0, s1, jnp.where(k == 1.0, s2, jnp.where(k == 2.0, s3, 0.0))
        ).astype(BF16)

    def value_of(s, o):
        r = pl.ds(pl.multiple_of(o * SLOTS, SLOTS), SLOTS)
        return dot(act[r, :], wd[s])

    def grad_of(s, o):
        r = pl.ds(pl.multiple_of(o * SLOTS, SLOTS), SLOTS)
        return dot(hc[r, :], wu[s], NTD) + slope_s[r, :1] * rrow[s, :1, :]

    def early(n):
        s = normal(n)
        sb[n, 0, hi] = grad_of(s, 2).astype(BF16)
        bcopy(n, 2).start()
        sb[n, 1, lo] = value_of(s, 0).astype(BF16)
        bcopy(n, 3).start()

    @pl.loop(0, OUT_STEPS)
    def _(i):
        for task in (
            out_z, unit_box, unit_z, unit_x, release, out_y, raw_on, unit_work, away, out_x, near, early, middle,
        ):
            at(i, OUT[task.__name__], task)

    def back_far(n):
        s = normal(n)
        sa[n, 0] = value_of(s, 3).astype(BF16)
        acopy(n, 0).start()
        sa[n, 1] = grad_of(s, 3).astype(BF16)
        acopy(n, 1).start()

    def back_near(n):
        s = normal(n)
        value = value_of(s, 2)
        acopy(n, 0).wait_recv()
        sb[n, 0, lo] = (value + ra[n, 0].astype(F32)).astype(BF16)
        bcopy(n, 0).start()
        grad = grad_of(s, 0)
        acopy(n, 1).wait_recv()
        sb[n, 1, hi] = (grad + ra[n, 1].astype(F32)).astype(BF16)
        bcopy(n, 1).start()

    def back_own(n):
        value, grad = value_of(normal(n), 1), grad_of(normal(n), 1)
        for i in range(4):
            bcopy(n, i).wait_recv()
        value = value + rb[n, 0, :SLOTS, :].astype(F32) + rb[n, 1, :SLOTS, :].astype(F32)
        grad = grad + rb[n, 0, SLOTS:, :].astype(F32) + rb[n, 1, SLOTS:, :].astype(F32)
        both = jnp.concatenate([value, grad], axis=0).astype(BF16)
        xall(n).wait_send()
        outx[n] = order(p2t, both, (NQ, XR, C))
        for d in XD:
            xcopy(n, d).start()
        inx[n, q] = outx[n, q]

    def back_x(n):
        xall(n).wait_recv()
        zall(n).wait_send()
        box[n] = order(p1t, inx[n], (NZ, ZR, C))
        for d in ZD:
            zcopy(n, d).start()
        inz[n, z] = box[n, z]

    def back_z(n):
        zall(n).wait_recv()
        got = inz[n].reshape(BOTH, C)
        cols = piece(normal(n))
        mixed_ref[:, cols] = (gate_s[:, :1] * dot(pltx[1], got)).astype(BF16)
        tgrad_ref[:, cols] = dot(pltc[1], got).astype(BF16)

    def unit_back(u):
        s, o = special(u // NT), turn(3 - u % NT)
        value, grad = value_of(s, o), grad_of(s, o)
        both = jnp.concatenate([value, grad], axis=0).astype(BF16)
        uxall(u).wait_send()
        uoutx[u] = order(p2t, both, (NQ, XR, C))

        @pl.when(u == 0)
        def _():
            pl.semaphore_wait(free, NZ + NQ - 2)

        for d in XD:
            uxcopy(u, d).start()
        uinx[u, q] = uoutx[u, q]

    def unit_back_x(u):
        uxall(u).wait_recv()
        uzall(u).wait_send()
        ubox[u] = order(p1t, uinx[u], (NZ, ZR, C))
        for d in ZD:
            uzcopy(u, d).start()
        uinz[u, z] = ubox[u, z]

    def unit_back_z(u):
        uzall(u).wait_recv()
        v, r = u // NT, u % NT

        @pl.when(r == 0)
        def _():
            for i in range(4):
                rcopy(v, i).wait_send()

        o = turn(3 - r)
        got = uinz[u].reshape(BOTH, C)
        raw[v, o, rlo] = dot(pltx[o], got).astype(BF16)
        raw[v, o, rhi] = dot(pltc[o], got).astype(BF16)

        @pl.when(r == 0)
        def _():
            uacopy(v, 0).start()
            uacopy(v, 1).start()

        @pl.when(r == 1)
        def _():
            uacopy(v, 1).wait_recv()
            raw[v, 0, rhi] = (raw[v, 0, rhi].astype(F32) + ua[v, 1].astype(F32)).astype(BF16)
            ubcopy(v, 1).start()

        @pl.when(r == 2)
        def _():
            uacopy(v, 0).wait_recv()
            raw[v, 2, rlo] = (raw[v, 2, rlo].astype(F32) + ua[v, 0].astype(F32)).astype(BF16)
            ubcopy(v, 0).start()

    def unit_sum(v):
        ubcopy(v, 0).wait_recv()
        ubcopy(v, 1).wait_recv()
        got = raw[v, 1].astype(F32) + ub[v, 0].astype(F32) + ub[v, 1].astype(F32)
        cols = piece(special(v))
        value = got[:ROWS].astype(BF16).astype(F32)
        mixed_ref[:, cols] = (gate_s[:, :1] * value).astype(BF16)
        tgrad_ref[:, cols] = got[ROWS:].astype(BF16)

    def grads_out(s, n):
        part = pl.ds(pl.multiple_of(n * N, N), N)
        k = n % 2
        return (
            pltpu.make_async_copy(gsu.at[k], upg_hbm.at[0, piece(s), part], gsem.at[0, k]),
            pltpu.make_async_copy(gsd.at[k], downg_hbm.at[0, part, piece(s)], gsem.at[1, k]),
        )

    def grads(s):
        @pl.loop(0, H // N)
        def _(n):
            @pl.when((s > 0) | (n >= 2))
            def _():
                for copy in grads_out(s, n):
                    copy.wait()

            part = pl.ds(pl.multiple_of(n * N, N), N)
            gsd[n % 2] = dot(act[:, part], cots_of(s), TND).astype(BF16)
            gsu[n % 2] = dot(rows_of(s), hc[:, part], TND).astype(BF16)
            for copy in grads_out(s, n):
                copy.start()

    def vector_0(_):
        @pl.loop(0, NC)
        def _(s):
            three = dot(slope3[...], rows_of(s), TND)
            vy[t, :, piece(s)] = jnp.sum(three, axis=0, keepdims=True)

        for d in YD:
            vycopy(d).start()

    def vector_1(_):
        for d in YD:
            vyland(d).wait_recv()
        vx[q] = (vy[0] + vy[1]) + (vy[2] + vy[3])
        for d in XD:
            vxcopy(d).start()

    def vector_2(_):
        for d in XD:
            vxland(d).wait_recv()
        for d in ZD:
            vzcopy(d).start()
        vz[z] = vx[...]

    @pl.loop(0, BACK_STEPS)
    def _(i):
        for task in (
            unit_back_x, unit_back, back_near, back_x, grads, vector_0, back_own, vector_2, unit_sum, back_z, back_far, unit_back_z, vector_1,
        ):
            at(i, BACK[task.__name__], task)

    for d in ZD:
        vzland(d).wait_recv()
    rgrad_ref[...] = vz[...].reshape(EXPERTS, C * NC)
    for d in YD:
        vtcopy(d).wait_send()
        vycopy(d).wait_send()
    for d in XD:
        vxcopy(d).wait_send()
    for d in ZD:
        vzcopy(d).wait_send()

    @pl.loop(0, NN)
    def _(n):
        for i in range(4):
            ycopy(n, i).wait_send()
            bcopy(n, i).wait_send()
        for i in range(2):
            acopy(n, i).wait_send()
        xall(n).wait_send()
        zall(n).wait_send()

    @pl.loop(0, NU)
    def _(u):
        uxall(u).wait_send()
        uzall(u).wait_send()

    @pl.loop(0, NS)
    def _(v):
        for i in range(2):
            uacopy(v, i).wait_send()
            ubcopy(v, i).wait_send()

    for n in range(2):
        for copy in grads_out(NC - 1, n):
            copy.wait()


def hand_over(arrays):
    cuts = []
    for k, a in enumerate(arrays):
        axis = len(a.shape) - 2
        parts = 4 if a.size > 1 << 20 else 1
        size = a.shape[axis] // parts
        cuts += [(k, (slice(None),) * axis + (pl.ds(p * size, size),)) for p in range(parts)]

    def body(*refs):
        n = len(arrays)
        ins, outs, bufs, sems = refs[:n], refs[n : 2 * n], refs[2 * n : 3 * n], refs[3 * n]
        reads = [
            pltpu.make_async_copy(ins[k].at[c], bufs[k].at[c], sems.at[0, i])
            for i, (k, c) in enumerate(cuts)
        ]
        writes = [
            pltpu.make_async_copy(bufs[k].at[c], outs[k].at[c], sems.at[1, i])
            for i, (k, c) in enumerate(cuts)
        ]
        for copy in reads:
            copy.start()
        for read, write in zip(reads, writes):
            read.wait()
            write.start()
        for copy in writes:
            copy.wait()

    hbm = pl.BlockSpec(memory_space=pl.ANY)
    return pl.pallas_call(
        body,
        out_shape=tuple(jax.ShapeDtypeStruct(a.shape, a.dtype) for a in arrays),
        in_specs=[hbm] * len(arrays),
        out_specs=(hbm,) * len(arrays),
        scratch_shapes=[pltpu.VMEM(a.shape, a.dtype) for a in arrays]
        + [pltpu.SemaphoreType.DMA((2, len(cuts)))],
        compiler_params=pltpu.CompilerParams(vmem_limit_bytes=60 << 20),
    )(*arrays)


def per_device(tokens, expert_ids, live_counts, router, up_weight, down_weight, out_grad):
    width = tokens.shape[1]
    assert tokens.shape == (ROWS, C * NC) and router.shape[1] == EXPERTS
    assert up_weight.shape == (1, C * NC, H)
    vmem = pl.BlockSpec(memory_space=pltpu.VMEM)
    smem = pl.BlockSpec(memory_space=pltpu.SMEM)
    hbm = pl.BlockSpec(memory_space=pl.ANY)
    every = NT * SLOTS
    V, DMA = pltpu.VMEM, pltpu.SemaphoreType.DMA
    scratch = [
        V((ROWS, width), BF16),
        V((ROWS, width), BF16),
        V((NN, NZ, ZR, C), BF16),
        V((NN, NZ, ZR, C), BF16),
        V((NN, NQ, XR, C), BF16),
        V((NN, NQ, XR, C), BF16),
        V((NU, NZ, ZR, C), BF16),
        V((NU, NZ, ZR, C), BF16),
        V((NU, NQ, XR, C), BF16),
        V((NU, NQ, XR, C), BF16),
        V((NS, NT, 2 * ROWS, C), BF16),
        V((NC, NT, BOTH, C), BF16),
        V((NC, C, H), BF16),
        V((NC, H, C), BF16),
        V((every, H), F32),
        V((every, H), F32),
        V((every, H), BF16),
        V((every, H), BF16),
        V((every, EXPERTS), F32),
        V((ROWS, 128), F32),
        V((every, 128), F32),
        V((every, 128), BF16),
        V((NN, 2, SLOTS, C), BF16),
        V((NN, 2, SLOTS, C), BF16),
        V((NN, 2, BOTH, C), BF16),
        V((NN, 2, BOTH, C), BF16),
        V((NS, 2, ROWS, C), BF16),
        V((NS, 2, 2 * ROWS, C), BF16),
        V((2, C, N), BF16),
        V((2, N, C), BF16),
        V((BOTH, BOTH), BF16),
        V((BOTH, BOTH), BF16),
        V((BOTH, BOTH), BF16),
        V((BOTH, BOTH), BF16),
        V((NT, BOTH, 2 * ROWS), BF16),
        V((NT, ROWS, BOTH), BF16),
        V((NT, ROWS, BOTH), BF16),
        V((NC, 8, C), F32),
        V((NT, 1, ROWS), F32),
        V((NT, 1, width), F32),
        V((NQ, 1, width), F32),
        V((NZ, NQ, 1, width), F32),
        DMA((2,)),
        DMA((2, NC)),
        DMA((NN,)), DMA((NN,)), DMA((NN,)), DMA((NN,)), DMA((NN, 4)), DMA((NN, 4)),
        DMA((NN, 2)), DMA((NN, 2)), DMA((NN, 4)), DMA((NN, 4)),
        DMA((NU,)), DMA((NU,)), DMA((NU,)), DMA((NU,)), DMA((NS, 4)), DMA((NS, 4)),
        DMA((NS, 2)), DMA((NS, 2)), DMA((NS, 2)), DMA((NS, 2)),
        DMA((2, 2)),
        DMA((NT,)), DMA((NT,)), DMA((NT,)), DMA((NT,)),
        DMA((NQ,)), DMA((NQ,)), DMA((NZ,)), DMA((NZ,)),
        pltpu.SemaphoreType.REGULAR,
    ]
    S = jax.ShapeDtypeStruct
    results = pl.pallas_call(
        kernel,
        out_shape=(
            S((ROWS, width), BF16),
            S((ROWS, width), BF16),
            S((1, width, H), BF16),
            S((1, H, width), BF16),
            S((EXPERTS, width), F32),
        ),
        in_specs=[vmem, smem, vmem, hbm, hbm, hbm, hbm],
        out_specs=(vmem, vmem, hbm, hbm, vmem),
        scratch_shapes=scratch,
        compiler_params=pltpu.CompilerParams(
            collective_id=0, has_side_effects=True, vmem_limit_bytes=67043328
        ),
    )(
        expert_ids.reshape(1, ROWS), live_counts, router.T, tokens, out_grad, up_weight, down_weight
    )
    mixed, tgrad, upg, downg, rgrad = hand_over(results)
    return (mixed, tgrad, upg, downg, rgrad.T)


def solution(mesh):
    rows = P(("expert", "tensor"), None)
    in_specs = (
        rows,
        rows,
        P(("expert", "tensor")),
        P(),
        P("expert", None, "tensor"),
        P("expert", "tensor", None),
        rows,
    )
    out_specs = (rows, rows, P("expert", None, "tensor"), P("expert", "tensor", None), P())
    return jax.shard_map(
        per_device, mesh=mesh, in_specs=in_specs, out_specs=out_specs, check_vma=False
    )
```
